32 devices in a mesh: grp: 2 (over y), tile: 4 (over z), span: 4 (over x, core).
Axes of the slice: x: 2, y: 2, z: 4, core: 2. Of those that a mesh axis runs over, the one named last changes fastest.
Arguments:
- features: bfloat16 [16, 8, 160, 384], P(('grp', 'span'), 'tile'), parts along dimension 0, may hold values from -24 to 24
- clip_lengths: int32 [8], P('grp'), parts along dimension 0, may hold values from 1 to 4, as said below
- norm_gain: float32 [384], replicated, may hold values from 0.1 to 1.9
- w_qkv: bfloat16 [384, 1152], replicated, may hold values from -6 to 6
- w_out: bfloat16 [384, 384], replicated, may hold values from -1 to 1
- conv_gain: float32 [384], replicated, may hold values from 0.1 to 1.9
- w_conv: bfloat16 [3, 3, 3, 384, 384], replicated, may hold values from -0.0625 to 0.0625
Outputs:
- attended: bfloat16 [16, 8, 160, 384], P(('grp', 'span'), 'tile'), parts along dimension 0
- hidden: bfloat16 [16, 8, 160, 384], P(('grp', 'span'), 'tile'), parts along dimension 0
The draws below stay inside these ranges and needn't reach their ends.
There are 2 independent parts, one for each index of `grp`. The reference program is written for one: setup_inputs(seed, part) draws one part's arguments, and reference() takes and returns one part's arrays. A program takes and returns all parts, laid end to end along the dimension named above; an argument that names none is the same for every part. Nothing has to cross between parts.
Inputs may be any that keep to these rules, and one draw needn't show every extreme that they name: `clip_lengths`: the lengths sum to 8; exactly one clip has 4 frames.
All inputs are finite; a program needn't handle non-finite values.
Results may differ from the reference program's by a relative error of at most 0.0095.
The reference program's roundings to bfloat16 on the way (of `normed`, `qkv`, `raised`, `mixture` and `activated`) count: a program that leaves them out, or rounds other values in their place, can miss the bound.
Values may be sent and summed in bfloat16 or wider, within the bound.
No kernel may reach another device: no remote copies, remote signals or barrier semaphores. Data moves between devices by JAX's collectives and lax.ppermute only.
A program may use at most 128 MiB of HBM per device.

```python
import jax
import jax.numpy as jnp
from jax import lax

C = 384
WIDTH = 160
FRAMES = 8
HEIGHT = 8


def draw_features(key, part):
    array_shape = (FRAMES, HEIGHT, WIDTH, C)
    values = jax.random.normal(key, array_shape, jnp.float32)
    return jnp.clip(values, -6.0, 6.0).astype(jnp.bfloat16)


def draw_clip_lengths(key, part):
    big_len = FRAMES // 2
    rest_len = FRAMES - big_len
    place_key, first_key, second_key = jax.random.split(jax.random.fold_in(key, 7), 3)
    where_big = jax.random.randint(place_key, (), 0, 4, jnp.int32)
    first_len = jax.random.randint(first_key, (), 1, rest_len - 1, jnp.int32)
    second_len = jax.random.randint(second_key, (), 1, rest_len - first_len, jnp.int32)
    third_len = rest_len - first_len - second_len
    others = jnp.stack([first_len, second_len, third_len]).astype(jnp.int32)
    slots = jnp.arange(4, dtype=jnp.int32)
    pick = slots - (slots > where_big).astype(jnp.int32)
    pick = jnp.minimum(pick, 2)
    picked = jnp.sum(jnp.where(pick[:, None] == jnp.arange(3, dtype=jnp.int32)[None, :], others[None, :], 0), axis=1)
    return jnp.where(slots == where_big, big_len, picked).astype(jnp.int32)


def draw_w_qkv(key, part):
    array_shape = (C, 3 * C)
    col_ids = jnp.arange(3 * C)[None, :]
    factor = jnp.where(col_ids < 2 * C, 1.5, 1.0)
    values = jnp.clip(jax.random.normal(key, array_shape, jnp.float32), -6.0, 6.0)
    return (values * C ** (-0.5) * factor).astype(jnp.bfloat16)


def centred(rng, dims, spread, limit, kind=jnp.bfloat16):
    entries = jax.random.normal(rng, dims, jnp.float32) * spread
    return jnp.minimum(jnp.maximum(entries, -limit), limit).astype(kind)


def setup_inputs(seed: int = 0, part: int = 0) -> dict:
    key_of = jax.random.split(jax.random.key(seed), 8)
    part_splits = jax.random.split(jax.random.fold_in(key_of[7], part), 8)
    features = draw_features(jax.random.fold_in(jax.random.fold_in(key_of[7], part), 71), part)
    clip_lengths = draw_clip_lengths(jax.random.fold_in(jax.random.fold_in(key_of[7], part), 71), part)
    norm_gain = jnp.clip(1.0 + 0.18 * jax.random.normal(key_of[2], (C,), jnp.float32), 0.1, 1.9)
    w_qkv = draw_w_qkv(jax.random.fold_in(key_of[7], 71), part)
    w_out = centred(key_of[4], (C, C), (C // 9) ** -0.5, 1.0)
    conv_gain = jnp.clip(1.0 + 0.18 * jax.random.normal(key_of[5], (C,), jnp.float32), 0.1, 1.9)
    w_conv = centred(key_of[6], (3, 3, 3, C, C), (27 * C) ** -0.5, 0.0625)
    return {"features": features, "clip_lengths": clip_lengths, "norm_gain": norm_gain, "w_qkv": w_qkv, "w_out": w_out, "conv_gain": conv_gain, "w_conv": w_conv}


eps = 1e-06

def rms_scale(values, gain_vec):
    as_float = values.astype(jnp.float32)
    return as_float * lax.rsqrt(lax.optimization_barrier(jnp.mean(as_float * as_float, axis=-1, keepdims=True)) + eps) * gain_vec.astype(jnp.float32)

def reference(features, clip_lengths, norm_gain, w_qkv, w_out, conv_gain, w_conv):
    frames, row_count, col_count, channels = features.shape
    tokens = features.reshape(frames, row_count * col_count, channels)
    normed = rms_scale(tokens, norm_gain).astype(jnp.bfloat16)

    def attend(frame_block):
        qkv = jnp.dot(frame_block, w_qkv, preferred_element_type=jnp.float32).astype(jnp.bfloat16)
        queries = qkv[:, :channels]
        key_part = qkv[:, channels:2 * channels]
        value_part = qkv[:, 2 * channels:]
        scores = jnp.dot(queries, key_part.T, preferred_element_type=jnp.float32) * channels ** (-0.5)
        row_top = lax.optimization_barrier(jnp.max(scores, axis=1, keepdims=True))
        raised_f = jnp.exp(scores - row_top)
        row_total = lax.optimization_barrier(jnp.sum(raised_f, axis=1, keepdims=True))
        raised = raised_f.astype(jnp.bfloat16)
        mixture = jnp.dot(raised, value_part, preferred_element_type=jnp.float32) / row_total
        return mixture.astype(jnp.bfloat16)
    mixture = lax.map(attend, normed)
    projected = jnp.dot(mixture.reshape(-1, channels), w_out, preferred_element_type=jnp.float32)
    attended = (tokens.reshape(-1, channels).astype(jnp.float32) + projected).astype(jnp.bfloat16)
    attended = attended.reshape(frames, row_count, col_count, channels)
    lifted = rms_scale(attended, conv_gain)
    activated = (lifted * jax.nn.sigmoid(lifted)).astype(jnp.bfloat16)
    clip_ends = jnp.cumsum(clip_lengths).astype(jnp.int32)
    position = jnp.arange(frames, dtype=jnp.int32)
    clip_start = lax.optimization_barrier(jnp.sum(jnp.where(clip_ends[None, :] <= position[:, None], clip_lengths[None, :], 0), axis=1)).astype(jnp.int32)
    padded = jnp.pad(activated, ((2, 0), (1, 1), (1, 1), (0, 0)))
    summed = jnp.zeros((frames * row_count * col_count, channels), jnp.float32)
    for t_tap in range(3):
        usable = position - (2 - t_tap) >= clip_start
        for r_tap in range(3):
            for c_tap in range(3):
                shifted = padded[t_tap:t_tap + frames, r_tap:r_tap + row_count, c_tap:c_tap + col_count]
                shifted = jnp.where(usable[:, None, None, None], shifted, jnp.zeros((), shifted.dtype))
                summed = summed + jnp.dot(shifted.reshape(-1, channels), w_conv[t_tap, r_tap, c_tap], preferred_element_type=jnp.float32)
    hidden = summed.astype(jnp.bfloat16).reshape(frames, row_count, col_count, channels)
    return (attended, hidden)
```

```python
import functools

import jax
import jax.numpy as jnp
from jax import lax
from jax.experimental import pallas as pl
from jax.experimental.pallas import tpu as pltpu
from jax.sharding import PartitionSpec as P

eps = 1e-06
f32, bf16 = jnp.float32, jnp.bfloat16
LOG2E = 1.4426950408889634

SWAP = [(0, 1), (1, 0), (2, 3), (3, 2)]
MIDDLE = [(1, 2), (2, 1)]
OUTWARD = [(1, 0), (2, 3)]


def from_behind(block, axis, distance):
    devices = range(lax.axis_size(axis))
    route = [(i - distance, i) for i in devices if i - distance in devices]
    return lax.ppermute(block, axis, route)


def rms_scale(values, gain_vec):
    as_float = values.astype(f32)
    return (
        as_float * lax.rsqrt(jnp.mean(as_float * as_float, axis=-1, keepdims=True) + eps) * gain_vec
    )


def dot32(a, b):
    return jnp.dot(a, b, preferred_element_type=f32)


def attend_kernel(
    cols, tile_ref, x, a, b, c, d, e, gain, w_qkv, w_out, conv_gain, att_out, act_out, kv, xq
):
    tile = tile_ref[0]
    inner = jnp.logical_or(tile == 1, tile == 2)
    cells, ch = x.shape
    gain_vec = gain[...]

    def fill(block, place):
        normed = rms_scale(block[...], gain_vec).astype(bf16)
        kv[place * cells : (place + 1) * cells, :] = dot32(normed, w_qkv[:, ch:]).astype(bf16)

    fill(x, 0)
    fill(a, 1)
    xq[cols : 3 * cols, :] = x[...]

    @pl.when(inner)
    def _():
        fill(b, 2)
        fill(c, 3)

    @pl.when(jnp.logical_not(inner))
    def _():
        fill(d, 2)
        fill(e, 3)

    @pl.when(tile == 2)
    def _():
        xq[:cols, :] = b[cols:, :]

    @pl.when(tile != 2)
    def _():
        xq[:cols, :] = a[cols:, :]

    @pl.when(tile == 1)
    def _():
        xq[3 * cols :, :] = b[:cols, :]

    @pl.when(tile != 1)
    def _():
        xq[3 * cols :, :] = a[:cols, :]

    for row in range(4):
        part = slice(row * cols, (row + 1) * cols)
        feats = xq[part, :]
        normed = rms_scale(feats, gain_vec).astype(bf16)
        queries = dot32(normed, w_qkv[:, :ch]).astype(bf16)
        scores = lax.dot_general(
            queries, kv[:, :ch], (((1,), (1,)), ((), ())), preferred_element_type=f32
        ) * (ch ** (-0.5) * LOG2E)
        raised = jnp.exp2(scores - jnp.max(scores, axis=1, keepdims=True))
        total = jnp.sum(raised, axis=1, keepdims=True)
        mixture = (dot32(raised.astype(bf16), kv[:, ch:]) / total).astype(bf16)
        attended = (feats.astype(f32) + dot32(mixture, w_out[...])).astype(bf16)
        if row in (1, 2):
            att_out[(row - 1) * cols : row * cols, :] = attended
        lifted = rms_scale(attended, conv_gain[...])
        active = lifted / (1.0 + jnp.exp(-lifted))
        if row == 0:
            active = jnp.where(tile > 0, active, 0.0)
        if row == 3:
            active = jnp.where(tile < 3, active, 0.0)
        act_out[part, :] = active.astype(bf16)


def attend(cols, tile, blocks, gain, w_qkv, w_out, conv_gain):
    cells, ch = blocks[0].shape
    vmem = pl.BlockSpec(memory_space=pltpu.VMEM)
    return pl.pallas_call(
        functools.partial(attend_kernel, cols),
        out_shape=(
            jax.ShapeDtypeStruct((cells, ch), bf16),
            jax.ShapeDtypeStruct((4 * cols, ch), bf16),
        ),
        in_specs=[pl.BlockSpec(memory_space=pltpu.SMEM)] + [vmem] * 10,
        out_specs=(vmem, vmem),
        scratch_shapes=[
            pltpu.VMEM((4 * cells, 2 * ch), bf16),
            pltpu.VMEM((4 * cols, ch), bf16),
        ],
        compiler_params=pltpu.CompilerParams(vmem_limit_bytes=32 << 20),
        name="attend",
    )(tile, *blocks, gain, w_qkv, w_out, conv_gain)


def shift_add(acc, cols, ch):
    out = []
    lane_col = lax.broadcasted_iota(jnp.int32, (cols, ch), 0)
    for r in range(acc.shape[0] // cols):
        part = acc[r * cols : (r + 1) * cols, :]
        left = jnp.where(lane_col == 0, 0.0, pltpu.roll(part[:, :ch], 1, 0))
        right = jnp.where(lane_col == cols - 1, 0.0, pltpu.roll(part[:, 2 * ch :], cols - 1, 0))
        out.append(part[:, ch : 2 * ch] + left + right)
    return out


def conv_kernel(cols, work, n_in, first, usable, *refs):
    ins, refs = refs[:n_in], refs[n_in:]
    if first:
        w_hbm, out, w, acc, sems = refs
    else:
        w_hbm, partial, out, w, acc, sems = refs
    ch = w_hbm.shape[-1]
    taps = []
    for tap, _, _ in work:
        if tap not in taps:
            taps.append(tap)
    copies = {}
    for tap in taps:
        copies[tap] = [
            pltpu.make_async_copy(
                w_hbm.at[tap, j, k],
                w.at[tap, j * ch : (j + 1) * ch, k * ch : (k + 1) * ch],
                sems.at[tap, j, k],
            )
            for j in range(3)
            for k in range(3)
        ]
        for copy in copies[tap]:
            copy.start()
    acc[...] = jnp.zeros_like(acc)
    waited = []
    for tap, frame, which in work:
        if tap not in waited:
            waited.append(tap)
            for copy in copies[tap]:
                copy.wait()

        @pl.when(usable[frame, tap] != 0)
        def _(tap=tap, frame=frame, which=which):
            src = ins[which]
            lhs = jnp.concatenate(
                [src[j * cols : (j + 2) * cols, :] for j in range(3)], axis=1
            )
            acc[frame] += dot32(lhs, w[tap])

    for frame in range(2):
        rows = shift_add(acc[frame], cols, ch)
        for r, val in enumerate(rows):
            part = slice((2 * frame + r) * cols, (2 * frame + r + 1) * cols)
            if not first:
                val = val + partial[part, :]
            out[part, :] = val.astype(out.dtype)


def conv(cols, work, ins, usable, w_conv, partial=None):
    ch = w_conv.shape[-1]
    first = partial is None
    vmem = pl.BlockSpec(memory_space=pltpu.VMEM)
    extra = [] if first else [partial]
    return pl.pallas_call(
        functools.partial(conv_kernel, cols, work, len(ins), first),
        out_shape=jax.ShapeDtypeStruct((4 * cols, ch), f32 if first else bf16),
        in_specs=[pl.BlockSpec(memory_space=pltpu.SMEM)]
        + [vmem] * len(ins)
        + [pl.BlockSpec(memory_space=pl.ANY)]
        + [vmem] * len(extra),
        out_specs=vmem,
        scratch_shapes=[
            pltpu.VMEM((3, 3 * ch, 3 * ch), bf16),
            pltpu.VMEM((2, 2 * cols, 3 * ch), f32),
            pltpu.SemaphoreType.DMA((3, 3, 3)),
        ],
        compiler_params=pltpu.CompilerParams(vmem_limit_bytes=40 << 20),
        name="conv_first" if first else "conv_rest",
    )(usable, *ins, w_conv, *extra)


def tap_flags(clip_lengths, frames):
    clip_ends = jnp.cumsum(clip_lengths)
    position = lax.axis_index("span") * frames + jnp.arange(frames, dtype=jnp.int32)
    clip_start = jnp.sum(
        jnp.where(clip_ends[None, :] <= position[:, None], clip_lengths[None, :], 0), axis=1
    )
    taps = jnp.arange(3, dtype=jnp.int32)
    return (position[:, None] - (2 - taps[None, :]) >= clip_start[:, None]).astype(jnp.int32)


def on_device(features, clip_lengths, norm_gain, w_qkv, w_out, conv_gain, w_conv):
    frames, row_count, cols, ch = features.shape
    if lax.axis_size("tile") != 4 or frames != 2 or row_count != 2:
        return general(features, clip_lengths, norm_gain, w_qkv, w_out, conv_gain, w_conv)
    cells = row_count * cols
    usable = tap_flags(clip_lengths, frames)
    tile = lax.axis_index("tile").astype(jnp.int32).reshape(1)
    gain, cgain = norm_gain.reshape(1, ch), conv_gain.reshape(1, ch)
    own = [features[f].reshape(cells, ch) for f in range(2)]
    moved = []
    for x in own:
        a = lax.ppermute(x, "tile", SWAP)
        b = lax.ppermute(x, "tile", MIDDLE)
        c = lax.ppermute(a, "tile", MIDDLE)
        d = lax.ppermute(b, "tile", OUTWARD)
        e = lax.ppermute(c, "tile", OUTWARD)
        moved.append((x, a, b, c, d, e))
    att0, act0 = attend(cols, tile, moved[0], gain, w_qkv, w_out, cgain)
    before0 = from_behind(act0, "span", 1)
    att1, act1 = attend(cols, tile, moved[1], gain, w_qkv, w_out, cgain)
    before1 = from_behind(act1, "span", 1)
    first = conv(
        cols, [(2, 0, 1), (2, 1, 2), (1, 1, 1), (0, 0, 0)], [before0, act0, act1], usable, w_conv
    )
    hidden = conv(cols, [(1, 0, 0), (0, 1, 0)], [before1], usable, w_conv, first)
    attended = jnp.stack([att0, att1]).reshape(frames, row_count, cols, ch)
    return attended, hidden.reshape(frames, row_count, cols, ch)


def extended(x, sides, width):
    for axis, dim in sides:
        size, length = (lax.axis_size(axis), x.shape[dim])
        up = [(i, (i + 1) % size) for i in range(size - 1)]
        down = [(j, i) for i, j in up]
        last = lax.slice_in_dim(x, length - width, length, axis=dim)
        first = lax.slice_in_dim(x, 0, width, axis=dim)
        before = lax.ppermute(last, axis, up)
        after = lax.ppermute(first, axis, down)
        x = jnp.concatenate([before, x, after], axis=dim)
    return x


def general(features, clip_lengths, norm_gain, w_qkv, w_out, conv_gain, w_conv):
    frames, row_count, col_count, channels = features.shape
    cell_count = row_count * col_count
    normed_grid = rms_scale(features, norm_gain).astype(jnp.bfloat16)
    view_frames = normed_grid.shape[0]
    view_cells = normed_grid.shape[1] * normed_grid.shape[2]
    normed = normed_grid.reshape(view_frames, view_cells, channels)
    queries = jnp.dot(
        normed.reshape(-1, channels), w_qkv[:, :channels], preferred_element_type=jnp.float32
    )
    queries = queries.astype(jnp.bfloat16).reshape(view_frames, view_cells, channels)
    kv_weight = w_qkv[:, channels:]
    score_scale = channels ** (-0.5)
    outgoing = jnp.dot(normed.reshape(-1, channels), kv_weight, preferred_element_type=jnp.float32)
    outgoing = outgoing.astype(jnp.bfloat16).reshape(view_frames, view_cells, 2 * channels)
    portion = lax.all_gather(outgoing, "tile", axis=1, tiled=True)
    key_part = portion[:, :, :channels]
    value_part = portion[:, :, channels:]
    row_top = jnp.full((view_frames, view_cells, 1), -1e30, jnp.float32)
    scores = (
        jnp.einsum("fqc,fkc->fqk", queries, key_part, preferred_element_type=jnp.float32)
        * score_scale
    )
    new_top = jnp.maximum(row_top, jnp.max(scores, axis=2, keepdims=True))
    raised_f = jnp.exp(scores - new_top)
    row_total = jnp.sum(raised_f, axis=2, keepdims=True)
    weighted = jnp.einsum(
        "fqk,fkc->fqc",
        raised_f.astype(jnp.bfloat16),
        value_part,
        preferred_element_type=jnp.float32,
    )
    mixture_grid = (weighted / row_total).astype(jnp.bfloat16)
    mixture = mixture_grid.reshape(-1, channels)
    projected = jnp.dot(mixture, w_out, preferred_element_type=jnp.float32)
    attended = (features.reshape(-1, channels).astype(jnp.float32) + projected).astype(jnp.bfloat16)
    attended = attended.reshape(frames, row_count, col_count, channels)
    lifted = rms_scale(attended, conv_gain)
    activated = (lifted * jax.nn.sigmoid(lifted)).astype(jnp.bfloat16)
    earlier = from_behind(activated, "span", 1)
    stacked = jnp.concatenate([earlier, activated], axis=0)
    edged = extended(stacked, (("tile", 1),), 1)
    padded = jnp.pad(edged, ((0, 0), (0, 0), (1, 1), (0, 0)))
    clip_ends = jnp.cumsum(clip_lengths)
    position = lax.axis_index("span") * frames + jnp.arange(frames, dtype=jnp.int32)
    clip_start = jnp.sum(
        jnp.where(clip_ends[None, :] <= position[:, None], clip_lengths[None, :], 0), axis=1
    )
    summed = jnp.zeros((frames * cell_count, channels), jnp.float32)
    for t_tap in range(3):
        usable = position - (2 - t_tap) >= clip_start
        for r_tap in range(3):
            for c_tap in range(3):
                shifted = padded[
                    t_tap : t_tap + frames, r_tap : r_tap + row_count, c_tap : c_tap + col_count
                ]
                shifted = jnp.where(
                    usable[:, None, None, None], shifted, jnp.zeros((), shifted.dtype)
                )
                summed = summed + jnp.dot(
                    shifted.reshape(-1, channels),
                    w_conv[t_tap, r_tap, c_tap],
                    preferred_element_type=jnp.float32,
                )
    hidden = summed.astype(jnp.bfloat16).reshape(frames, row_count, col_count, channels)
    return (attended, hidden)


def solution(mesh):
    in_specs = (P(("grp", "span"), "tile", None, None), P("grp"), P(), P(), P(), P(), P())
    out_specs = (P(("grp", "span"), "tile", None, None), P(("grp", "span"), "tile", None, None))
    return jax.shard_map(
        on_device, mesh=mesh, in_specs=in_specs, out_specs=out_specs, check_vma=False
    )
```

```python
import functools

import jax
import jax.numpy as jnp
from jax import lax
from jax.experimental import pallas as pl
from jax.experimental.pallas import tpu as pltpu
from jax.sharding import PartitionSpec as P

eps = 1e-06
f32, bf16 = jnp.float32, jnp.bfloat16
LOG2E = 1.4426950408889634
VMEM = pl.BlockSpec(memory_space=pltpu.VMEM)
SMEM = pl.BlockSpec(memory_space=pltpu.SMEM)
ANY = pl.BlockSpec(memory_space=pl.ANY)


def from_behind(block, axis, distance):
    devices = range(lax.axis_size(axis))
    route = [(i - distance, i) for i in devices if i - distance in devices]
    return lax.ppermute(block, axis, route)


def rms_scale(values, gain_vec):
    as_float = values.astype(f32)
    return (
        as_float * lax.rsqrt(jnp.mean(as_float * as_float, axis=-1, keepdims=True) + eps) * gain_vec
    )


def dot32(a, b):
    return jnp.dot(a, b, preferred_element_type=f32)


def struct(shape, dtype=bf16):
    return jax.ShapeDtypeStruct(shape, dtype)


def call(kernel, name, out_shape, in_specs, scratch=(), limit=24):
    outs = jax.tree.map(lambda _: VMEM, out_shape)
    return pl.pallas_call(
        kernel,
        out_shape=out_shape,
        in_specs=in_specs,
        out_specs=outs,
        scratch_shapes=list(scratch),
        compiler_params=pltpu.CompilerParams(vmem_limit_bytes=limit << 20),
        name=name,
    )


def frame_route(spans, flip):
    route = []
    for tile in range(4):
        for span in range(spans):
            high, low, column, core = tile // 2, tile % 2, span // 2, span % 2
            there = (2 * core + (low ^ flip)) * spans + 2 * column + high
            route.append((tile * spans + span, there))
    return route


def shifted_route(tiles, spans, down, ahead):
    return [
        (t * spans + s, (t + down) * spans + s + ahead)
        for t in range(tiles)
        for s in range(spans)
        if 0 <= t + down < tiles and s + ahead < spans
    ]


def pack_kernel(w_hbm, w_out, sem):
    ch = w_hbm.shape[-1]
    copies = [
        pltpu.make_async_copy(
            w_hbm.at[i, j, k],
            w_out.at[i, j * ch : (j + 1) * ch, k * ch : (k + 1) * ch],
            sem.at[i, j, k],
        )
        for i in range(3)
        for j in range(3)
        for k in range(3)
    ]
    for copy in copies:
        copy.start()
    for copy in copies:
        copy.wait()


def project_keys(block, gain_vec, w_qkv, out, place):
    cells, ch = block.shape
    normed = rms_scale(block[...], gain_vec).astype(bf16)
    out[place * cells : (place + 1) * cells, :] = dot32(normed, w_qkv[:, ch:]).astype(bf16)


def keys_kernel(own, other, gain, w_qkv, kv_out):
    gain_vec = gain[...].reshape(1, own.shape[1])
    project_keys(own, gain_vec, w_qkv, kv_out, 0)
    project_keys(other, gain_vec, w_qkv, kv_out, 1)


def attend_rows(cols, source, kv_parts, gain_vec, w_qkv, w_out, att_out):
    ch = source.shape[1]
    for row in range(source.shape[0] // cols):
        part = slice(row * cols, (row + 1) * cols)
        feats = source[part, :]
        normed = rms_scale(feats, gain_vec).astype(bf16)
        queries = dot32(normed, w_qkv[:, :ch]).astype(bf16)
        scores = [
            lax.dot_general(
                queries, kv[:, :ch], (((1,), (1,)), ((), ())), preferred_element_type=f32
            )
            * (ch ** (-0.5) * LOG2E)
            for kv in kv_parts
        ]
        top = functools.reduce(
            jnp.maximum, [jnp.max(s, axis=1, keepdims=True) for s in scores]
        )
        raised = [jnp.exp2(s - top) for s in scores]
        total = sum(jnp.sum(r, axis=1, keepdims=True) for r in raised)
        mixed = sum(dot32(r.astype(bf16), kv[:, ch:]) for r, kv in zip(raised, kv_parts))
        mixture = (mixed / total).astype(bf16)
        att_out[part, :] = (feats.astype(f32) + dot32(mixture, w_out[...])).astype(bf16)


def attend_kernel(cols, own_b, other_b, own_a, kv_a, gain, w_qkv, w_out, kv_b, att_a):
    gain_vec = gain[...].reshape(1, own_a.shape[1])
    project_keys(own_b, gain_vec, w_qkv, kv_b, 0)
    project_keys(other_b, gain_vec, w_qkv, kv_b, 1)
    attend_rows(cols, own_a, (kv_a, kv_b), gain_vec, w_qkv, w_out, att_a)


def attend_rest_kernel(cols, own_b, kv_a, kv_b, gain, w_qkv, w_out, att_b):
    gain_vec = gain[...].reshape(1, own_b.shape[1])
    attend_rows(cols, own_b, (kv_a, kv_b), gain_vec, w_qkv, w_out, att_b)


def activate_kernel(cols, tile_ref, got_a, got_b, gain, attended, active, top_edge, low_edge):
    low = tile_ref[0] % 2
    gain_vec = gain[...].reshape(1, got_a.shape[1])

    def one(block, frame):
        values = block[...]
        attended[frame] = values
        lifted = rms_scale(values, gain_vec)
        act = (lifted / (1.0 + jnp.exp(-lifted))).astype(bf16)
        active[frame] = act
        top_edge[frame] = act[:cols, :]
        low_edge[frame] = act[cols:, :]

    one(got_a, low)
    one(got_b, 1 - low)


def usable_flag(clips, frame_at, tap):
    end = jnp.int32(0)
    start = jnp.int32(0)
    for i in range(clips.shape[0]):
        end = end + clips[i]
        start = start + jnp.where(end <= frame_at, clips[i], 0)
    return frame_at - (2 - tap) >= start


def shift_add(part, cols, ch):
    at = lax.broadcasted_iota(jnp.int32, (cols, ch), 0)
    left = jnp.where(at == 0, 0.0, pltpu.roll(part[:, :ch], 1, 0))
    right = jnp.where(at == cols - 1, 0.0, pltpu.roll(part[:, 2 * ch :], cols - 1, 0))
    return part[:, ch : 2 * ch] + left + right


def conv_kernel(cols, work, first, span_ref, clips, mid, top, low, w, *refs):
    if first:
        out, acc = refs
    else:
        partial, out, acc = refs
    ch = mid.shape[-1]
    acc[...] = jnp.zeros_like(acc)
    for tap, frame, which in work:

        @pl.when(usable_flag(clips, span_ref[0] * 2 + frame, tap))
        def _(tap=tap, frame=frame, which=which):
            rows = [top[which], mid[which, :cols, :], mid[which, cols:, :], low[which]]
            lhs = jnp.concatenate(
                [jnp.concatenate(rows[r : r + 3], axis=1) for r in range(2)], axis=0
            )
            acc[frame] += dot32(lhs, w[tap])

    for frame in range(2):
        for r in range(2):
            part = slice(r * cols, (r + 1) * cols)
            val = shift_add(acc[frame, part, :], cols, ch)
            if not first:
                val = val + partial[frame, part, :]
            out[frame, part, :] = val.astype(out.dtype)


def on_device(features, clip_lengths, norm_gain, w_qkv, w_out, conv_gain, w_conv):
    frames, row_count, cols, ch = features.shape
    tiles, spans = lax.axis_size("tile"), lax.axis_size("span")
    if tiles != 4 or spans % 2 or frames != 2 or row_count != 2:
        return general(features, clip_lengths, norm_gain, w_qkv, w_out, conv_gain, w_conv)
    cells = row_count * cols
    both = ("tile", "span")
    tile = lax.axis_index("tile").astype(jnp.int32).reshape(1)
    span = lax.axis_index("span").astype(jnp.int32).reshape(1)
    other_core = [(i, i ^ 1) for i in range(spans)]
    route_a, route_b = frame_route(spans, 0), frame_route(spans, 1)
    low = tile[0] % 2
    x = features.reshape(frames, cells, ch)
    send_a = lax.dynamic_index_in_dim(x, low, 0, keepdims=False)
    send_b = lax.dynamic_index_in_dim(x, 1 - low, 0, keepdims=False)
    own_a = lax.ppermute(send_a, both, route_a)
    own_b = lax.ppermute(send_b, both, route_b)
    w_packed = call(
        pack_kernel,
        "pack_weights",
        struct((3, 3 * ch, 3 * ch)),
        [ANY],
        [pltpu.SemaphoreType.DMA((3, 3, 3))],
        16,
    )(w_conv)
    other_a = lax.ppermute(own_a, "span", other_core)
    other_b = lax.ppermute(own_b, "span", other_core)
    kv_a = call(keys_kernel, "keys", struct((2 * cells, 2 * ch)), [VMEM] * 4)(
        own_a, other_a, norm_gain, w_qkv
    )
    kv_b, att_a = call(
        functools.partial(attend_kernel, cols),
        "attend",
        (struct((2 * cells, 2 * ch)), struct((cells, ch))),
        [VMEM] * 7,
    )(own_b, other_b, own_a, kv_a, norm_gain, w_qkv, w_out)
    got_a = lax.ppermute(att_a, both, route_a)
    att_b = call(
        functools.partial(attend_rest_kernel, cols), "attend_rest", struct((cells, ch)), [VMEM] * 6
    )(own_b, kv_a, kv_b, norm_gain, w_qkv, w_out)
    got_b = lax.ppermute(att_b, both, route_b)
    attended, active, top_edge, low_edge = call(
        functools.partial(activate_kernel, cols),
        "activate",
        (
            struct((frames, cells, ch)),
            struct((frames, cells, ch)),
            struct((frames, cols, ch)),
            struct((frames, cols, ch)),
        ),
        [SMEM] + [VMEM] * 3,
    )(tile, got_a, got_b, conv_gain)
    above = lax.ppermute(low_edge, both, shifted_route(tiles, spans, 1, 0))
    below = lax.ppermute(top_edge, both, shifted_route(tiles, spans, -1, 0))
    before = lax.ppermute(active, both, shifted_route(tiles, spans, 0, 1))
    before_above = lax.ppermute(low_edge, both, shifted_route(tiles, spans, 1, 1))
    before_below = lax.ppermute(top_edge, both, shifted_route(tiles, spans, -1, 1))
    acc = pltpu.VMEM((frames, cells, 3 * ch), f32)
    partial = call(
        functools.partial(conv_kernel, cols, [(2, 0, 0), (2, 1, 1), (1, 1, 0)], True),
        "conv_own",
        struct((frames, cells, ch), f32),
        [SMEM, SMEM] + [VMEM] * 4,
        [acc],
    )(span, clip_lengths, active, above, below, w_packed)
    hidden = call(
        functools.partial(conv_kernel, cols, [(0, 0, 0), (1, 0, 1), (0, 1, 1)], False),
        "conv_before",
        struct((frames, cells, ch)),
        [SMEM, SMEM] + [VMEM] * 5,
        [acc],
    )(span, clip_lengths, before, before_above, before_below, w_packed, partial)
    shape = (frames, row_count, cols, ch)
    return attended.reshape(shape), hidden.reshape(shape)


def extended(x, sides, width):
    for axis, dim in sides:
        size, length = (lax.axis_size(axis), x.shape[dim])
        up = [(i, (i + 1) % size) for i in range(size - 1)]
        down = [(j, i) for i, j in up]
        last = lax.slice_in_dim(x, length - width, length, axis=dim)
        first = lax.slice_in_dim(x, 0, width, axis=dim)
        before = lax.ppermute(last, axis, up)
        after = lax.ppermute(first, axis, down)
        x = jnp.concatenate([before, x, after], axis=dim)
    return x


def general(features, clip_lengths, norm_gain, w_qkv, w_out, conv_gain, w_conv):
    frames, row_count, col_count, channels = features.shape
    cell_count = row_count * col_count
    normed_grid = rms_scale(features, norm_gain).astype(jnp.bfloat16)
    view_frames = normed_grid.shape[0]
    view_cells = normed_grid.shape[1] * normed_grid.shape[2]
    normed = normed_grid.reshape(view_frames, view_cells, channels)
    queries = jnp.dot(
        normed.reshape(-1, channels), w_qkv[:, :channels], preferred_element_type=jnp.float32
    )
    queries = queries.astype(jnp.bfloat16).reshape(view_frames, view_cells, channels)
    kv_weight = w_qkv[:, channels:]
    score_scale = channels ** (-0.5)
    outgoing = jnp.dot(normed.reshape(-1, channels), kv_weight, preferred_element_type=jnp.float32)
    outgoing = outgoing.astype(jnp.bfloat16).reshape(view_frames, view_cells, 2 * channels)
    portion = lax.all_gather(outgoing, "tile", axis=1, tiled=True)
    key_part = portion[:, :, :channels]
    value_part = portion[:, :, channels:]
    row_top = jnp.full((view_frames, view_cells, 1), -1e30, jnp.float32)
    scores = (
        jnp.einsum("fqc,fkc->fqk", queries, key_part, preferred_element_type=jnp.float32)
        * score_scale
    )
    new_top = jnp.maximum(row_top, jnp.max(scores, axis=2, keepdims=True))
    raised_f = jnp.exp(scores - new_top)
    row_total = jnp.sum(raised_f, axis=2, keepdims=True)
    weighted = jnp.einsum(
        "fqk,fkc->fqc",
        raised_f.astype(jnp.bfloat16),
        value_part,
        preferred_element_type=jnp.float32,
    )
    mixture_grid = (weighted / row_total).astype(jnp.bfloat16)
    mixture = mixture_grid.reshape(-1, channels)
    projected = jnp.dot(mixture, w_out, preferred_element_type=jnp.float32)
    attended = (features.reshape(-1, channels).astype(jnp.float32) + projected).astype(jnp.bfloat16)
    attended = attended.reshape(frames, row_count, col_count, channels)
    lifted = rms_scale(attended, conv_gain)
    activated = (lifted * jax.nn.sigmoid(lifted)).astype(jnp.bfloat16)
    earlier = from_behind(activated, "span", 1)
    stacked = jnp.concatenate([earlier, activated], axis=0)
    edged = extended(stacked, (("tile", 1),), 1)
    padded = jnp.pad(edged, ((0, 0), (0, 0), (1, 1), (0, 0)))
    clip_ends = jnp.cumsum(clip_lengths)
    position = lax.axis_index("span") * frames + jnp.arange(frames, dtype=jnp.int32)
    clip_start = jnp.sum(
        jnp.where(clip_ends[None, :] <= position[:, None], clip_lengths[None, :], 0), axis=1
    )
    summed = jnp.zeros((frames * cell_count, channels), jnp.float32)
    for t_tap in range(3):
        usable = position - (2 - t_tap) >= clip_start
        for r_tap in range(3):
            for c_tap in range(3):
                shifted = padded[
                    t_tap : t_tap + frames, r_tap : r_tap + row_count, c_tap : c_tap + col_count
                ]
                shifted = jnp.where(
                    usable[:, None, None, None], shifted, jnp.zeros((), shifted.dtype)
                )
                summed = summed + jnp.dot(
                    shifted.reshape(-1, channels),
                    w_conv[t_tap, r_tap, c_tap],
                    preferred_element_type=jnp.float32,
                )
    hidden = summed.astype(jnp.bfloat16).reshape(frames, row_count, col_count, channels)
    return (attended, hidden)


def solution(mesh):
    in_specs = (P(("grp", "span"), "tile", None, None), P("grp"), P(), P(), P(), P(), P())
    out_specs = (P(("grp", "span"), "tile", None, None), P(("grp", "span"), "tile", None, None))
    return jax.shard_map(
        on_device, mesh=mesh, in_specs=in_specs, out_specs=out_specs, check_vma=False
    )
```

```python
import functools

import jax
import jax.numpy as jnp
from jax import lax
from jax.experimental import pallas as pl
from jax.experimental.pallas import tpu as pltpu
from jax.sharding import PartitionSpec as P

eps = 1e-06
f32, bf16 = jnp.float32, jnp.bfloat16
LOG2E = 1.4426950408889634
VMEM = pl.BlockSpec(memory_space=pltpu.VMEM)
SMEM = pl.BlockSpec(memory_space=pltpu.SMEM)
ANY = pl.BlockSpec(memory_space=pl.ANY)


def from_behind(block, axis, distance):
    devices = range(lax.axis_size(axis))
    route = [(i - distance, i) for i in devices if i - distance in devices]
    return lax.ppermute(block, axis, route)


def rms_scale(values, gain_vec):
    as_float = values.astype(f32)
    return (
        as_float * lax.rsqrt(jnp.mean(as_float * as_float, axis=-1, keepdims=True) + eps) * gain_vec
    )


def dot32(a, b):
    return jnp.dot(a, b, preferred_element_type=f32)


def struct(shape, dtype=bf16):
    return jax.ShapeDtypeStruct(shape, dtype)


def call(kernel, name, out_shape, in_specs, scratch=(), limit=16, flops=0, size=1 << 20):
    outs = jax.tree.map(lambda _: VMEM, out_shape)
    cost = pl.CostEstimate(flops=int(flops), transcendentals=0, bytes_accessed=int(size))
    return pl.pallas_call(
        kernel,
        out_shape=out_shape,
        in_specs=in_specs,
        out_specs=outs,
        scratch_shapes=list(scratch),
        compiler_params=pltpu.CompilerParams(vmem_limit_bytes=limit << 20),
        cost_estimate=cost,
        name=name,
    )


def frame_route(spans, flip):
    route = []
    for tile in range(4):
        for span in range(spans):
            high, low, column, core = tile // 2, tile % 2, span // 2, span % 2
            there = (2 * core + (low ^ flip)) * spans + 2 * column + high
            route.append((tile * spans + span, there))
    return route


def shifted_route(tiles, spans, down, ahead):
    return [
        (t * spans + s, (t + down) * spans + s + ahead)
        for t in range(tiles)
        for s in range(spans)
        if 0 <= t + down < tiles and s + ahead < spans
    ]


def load_kernel(w_conv, w_qkv, w_out, conv_vm, qkv_vm, out_vm, sem):
    ch = w_conv.shape[-1]
    copies = [
        pltpu.make_async_copy(w_qkv, qkv_vm, sem.at[27]),
        pltpu.make_async_copy(w_out, out_vm, sem.at[28]),
    ]
    copies += [
        pltpu.make_async_copy(
            w_conv.at[i, j, k],
            conv_vm.at[i, j * ch : (j + 1) * ch, k * ch : (k + 1) * ch],
            sem.at[9 * i + 3 * j + k],
        )
        for i in range(3)
        for j in range(3)
        for k in range(3)
    ]
    for copy in copies:
        copy.start()
    for copy in copies:
        copy.wait()


def project_keys(block, gain_vec, w_qkv, out, place):
    cells, ch = block.shape
    normed = rms_scale(block[...], gain_vec).astype(bf16)
    out[place * cells : (place + 1) * cells, :] = dot32(normed, w_qkv[:, ch:]).astype(bf16)


def keys_kernel(own, other, gain, w_qkv, kv_out):
    gain_vec = gain[...].reshape(1, own.shape[1])
    project_keys(own, gain_vec, w_qkv, kv_out, 0)
    project_keys(other, gain_vec, w_qkv, kv_out, 1)


def attend_rows(cols, source, kv_parts, gain_vec, w_qkv, w_out, att_out):
    ch = source.shape[1]
    for row in range(source.shape[0] // cols):
        part = slice(row * cols, (row + 1) * cols)
        feats = source[part, :]
        normed = rms_scale(feats, gain_vec).astype(bf16)
        queries = dot32(normed, w_qkv[:, :ch]).astype(bf16)
        scores = [
            lax.dot_general(
                queries, kv[:, :ch], (((1,), (1,)), ((), ())), preferred_element_type=f32
            )
            * (ch ** (-0.5) * LOG2E)
            for kv in kv_parts
        ]
        top = functools.reduce(
            jnp.maximum, [jnp.max(s, axis=1, keepdims=True) for s in scores]
        )
        raised = [jnp.exp2(s - top) for s in scores]
        total = sum(jnp.sum(r, axis=1, keepdims=True) for r in raised)
        mixed = sum(dot32(r.astype(bf16), kv[:, ch:]) for r, kv in zip(raised, kv_parts))
        mixture = (mixed / total).astype(bf16)
        att_out[part, :] = (feats.astype(f32) + dot32(mixture, w_out[...])).astype(bf16)


def attend_kernel(cols, own_b, other_b, own_a, kv_a, gain, w_qkv, w_out, kv_b, att_a):
    gain_vec = gain[...].reshape(1, own_a.shape[1])
    project_keys(own_b, gain_vec, w_qkv, kv_b, 0)
    project_keys(other_b, gain_vec, w_qkv, kv_b, 1)
    attend_rows(cols, own_a, (kv_a, kv_b), gain_vec, w_qkv, w_out, att_a)


def attend_rest_kernel(cols, own_b, kv_a, kv_b, gain, w_qkv, w_out, att_b):
    gain_vec = gain[...].reshape(1, own_b.shape[1])
    attend_rows(cols, own_b, (kv_a, kv_b), gain_vec, w_qkv, w_out, att_b)


def activate_kernel(cols, tile_ref, got_a, got_b, gain, attended, active, top_edge, low_edge):
    low = tile_ref[0] % 2
    gain_vec = gain[...].reshape(1, got_a.shape[1])

    def one(block, frame):
        values = block[...]
        attended[frame] = values
        lifted = rms_scale(values, gain_vec)
        act = (lifted / (1.0 + jnp.exp(-lifted))).astype(bf16)
        active[frame] = act
        top_edge[frame] = act[:cols, :]
        low_edge[frame] = act[cols:, :]

    one(got_a, low)
    one(got_b, 1 - low)


def usable_flag(clips, frame_at, tap):
    end = jnp.int32(0)
    start = jnp.int32(0)
    for i in range(clips.shape[0]):
        end = end + clips[i]
        start = start + jnp.where(end <= frame_at, clips[i], 0)
    return frame_at - (2 - tap) >= start


def shift_add(part, cols, ch):
    at = lax.broadcasted_iota(jnp.int32, (cols, ch), 0)
    left = jnp.where(at == 0, 0.0, pltpu.roll(part[:, :ch], 1, 0))
    right = jnp.where(at == cols - 1, 0.0, pltpu.roll(part[:, 2 * ch :], cols - 1, 0))
    return part[:, ch : 2 * ch] + left + right


def conv_kernel(cols, work, use, n_in, ahead, span_ref, clips, *refs):
    ins, (w, *partial, out, acc) = refs[:n_in], refs[n_in:]
    ch = w.shape[-1] // 3
    acc[...] = jnp.zeros_like(acc)
    first_row, second_row = slice(0, cols), slice(cols, 2 * cols)
    for tap, frame, which in work:

        @pl.when(usable_flag(clips, (span_ref[0] + ahead) * 2 + frame, tap))
        def _(tap=tap, frame=frame, which=which):
            if use == "edge":
                above, below = ins
                acc[frame, first_row] += dot32(above[which], w[tap, :ch])
                acc[frame, second_row] += dot32(below[which], w[tap, 2 * ch :])
            else:
                mid = ins[0]
                rows = [mid[which, first_row, :], mid[which, second_row, :]]
                if use == "own":
                    lhs = jnp.concatenate(rows, axis=1)
                    acc[frame, first_row] += dot32(lhs, w[tap, ch:])
                    acc[frame, second_row] += dot32(lhs, w[tap, : 2 * ch])
                else:
                    rows = [ins[1][which]] + rows + [ins[2][which]]
                    lhs = jnp.concatenate(
                        [jnp.concatenate(rows[r : r + 3], axis=1) for r in range(2)], axis=0
                    )
                    acc[frame] += dot32(lhs, w[tap])

    for frame in range(2):
        for part in (first_row, second_row):
            val = shift_add(acc[frame, part, :], cols, ch)
            if partial:
                val = val + partial[0][frame, part, :]
            out[frame, part, :] = val.astype(out.dtype)


def on_device(features, clip_lengths, norm_gain, w_qkv, w_out, conv_gain, w_conv):
    frames, row_count, cols, ch = features.shape
    tiles, spans = lax.axis_size("tile"), lax.axis_size("span")
    if tiles != 4 or spans % 2 or frames != 2 or row_count != 2:
        return general(features, clip_lengths, norm_gain, w_qkv, w_out, conv_gain, w_conv)
    cells = row_count * cols
    both = ("tile", "span")
    tile = lax.axis_index("tile").astype(jnp.int32).reshape(1)
    span = lax.axis_index("span").astype(jnp.int32).reshape(1)
    other_core = [(i, i ^ 1) for i in range(spans)]
    route_a, route_b = frame_route(spans, 0), frame_route(spans, 1)
    low = tile[0] % 2
    x = features.reshape(frames, cells, ch)
    send_a = lax.dynamic_index_in_dim(x, low, 0, keepdims=False)
    send_b = lax.dynamic_index_in_dim(x, 1 - low, 0, keepdims=False)
    own_a = lax.ppermute(send_a, both, route_a)
    own_b = lax.ppermute(send_b, both, route_b)
    w_packed, w_qkv, w_out = call(
        load_kernel,
        "load_weights",
        tuple(
            pltpu.VMEM(shape, bf16) for shape in ((3, 3 * ch, 3 * ch), w_qkv.shape, w_out.shape)
        ),
        [ANY] * 3,
        [pltpu.SemaphoreType.DMA((29,))],
        48,
        size=9 << 20,
    )(w_conv, w_qkv, w_out)
    own_a, w_packed = lax.optimization_barrier((own_a, w_packed))
    other_a = lax.ppermute(own_a, "span", other_core)
    other_b = lax.ppermute(own_b, "span", other_core)
    kv_flops = 2 * 2 * cells * ch * 2 * ch
    row_flops = 2 * cells * ch * (2 * ch + 8 * cells)
    kv_a = call(keys_kernel, "keys", struct((2 * cells, 2 * ch)), [VMEM] * 4, flops=kv_flops)(
        own_a, other_a, norm_gain, w_qkv
    )
    kv_b, att_a = call(
        functools.partial(attend_kernel, cols),
        "attend",
        (struct((2 * cells, 2 * ch)), struct((cells, ch))),
        [VMEM] * 7,
        flops=kv_flops + row_flops,
    )(own_b, other_b, own_a, kv_a, norm_gain, w_qkv, w_out)
    got_a = lax.ppermute(att_a, both, route_a)
    att_b = call(
        functools.partial(attend_rest_kernel, cols),
        "attend_rest",
        struct((cells, ch)),
        [VMEM] * 6,
        flops=3 * row_flops,
    )(own_b, kv_a, kv_b, norm_gain, w_qkv, w_out)
    got_b = lax.ppermute(att_b, both, route_b)
    attended, active, top_edge, low_edge = call(
        functools.partial(activate_kernel, cols),
        "activate",
        (
            struct((frames, cells, ch)),
            struct((frames, cells, ch)),
            struct((frames, cols, ch)),
            struct((frames, cols, ch)),
        ),
        [SMEM] + [VMEM] * 3,
    )(tile, got_a, got_b, conv_gain)
    above = lax.ppermute(low_edge, both, shifted_route(tiles, spans, 1, 0))
    below = lax.ppermute(top_edge, both, shifted_route(tiles, spans, -1, 0))
    acc = pltpu.VMEM((frames, cells, 3 * ch), f32)
    block = struct((frames, cells, ch))
    sums = struct((frames, cells, ch), f32)
    unit = 2 * cells * 9 * ch * ch
    to_next = [(0, 0, 0), (1, 0, 1), (0, 1, 1)]
    to_own = [(2, 0, 0), (2, 1, 1), (1, 1, 0)]

    def conv(work, use, ahead, result, name, ins, *partial):
        share = {"own": 2, "edge": 1, "all": 3}[use]
        return call(
            functools.partial(conv_kernel, cols, work, use, len(ins), ahead),
            name,
            result,
            [SMEM, SMEM] + [VMEM] * (len(ins) + 1 + len(partial)),
            [acc],
            flops=share * unit,
        )(span, clip_lengths, *ins, w_packed, *partial)

    started = conv(to_next, "own", 1, sums, "conv_next_own", [active])
    for_next = conv(to_next, "edge", 1, block, "conv_next_edge", [above, below], started)
    earlier = lax.ppermute(for_next, both, shifted_route(tiles, spans, 0, 1))
    own = conv(to_own, "all", 0, sums, "conv_own", [active, above, below])
    hidden = (own + earlier.astype(f32)).astype(bf16)
    shape = (frames, row_count, cols, ch)
    return attended.reshape(shape), hidden.reshape(shape)


def extended(x, sides, width):
    for axis, dim in sides:
        size, length = (lax.axis_size(axis), x.shape[dim])
        up = [(i, (i + 1) % size) for i in range(size - 1)]
        down = [(j, i) for i, j in up]
        last = lax.slice_in_dim(x, length - width, length, axis=dim)
        first = lax.slice_in_dim(x, 0, width, axis=dim)
        before = lax.ppermute(last, axis, up)
        after = lax.ppermute(first, axis, down)
        x = jnp.concatenate([before, x, after], axis=dim)
    return x


def general(features, clip_lengths, norm_gain, w_qkv, w_out, conv_gain, w_conv):
    frames, row_count, col_count, channels = features.shape
    cell_count = row_count * col_count
    normed_grid = rms_scale(features, norm_gain).astype(jnp.bfloat16)
    view_frames = normed_grid.shape[0]
    view_cells = normed_grid.shape[1] * normed_grid.shape[2]
    normed = normed_grid.reshape(view_frames, view_cells, channels)
    queries = jnp.dot(
        normed.reshape(-1, channels), w_qkv[:, :channels], preferred_element_type=jnp.float32
    )
    queries = queries.astype(jnp.bfloat16).reshape(view_frames, view_cells, channels)
    kv_weight = w_qkv[:, channels:]
    score_scale = channels ** (-0.5)
    outgoing = jnp.dot(normed.reshape(-1, channels), kv_weight, preferred_element_type=jnp.float32)
    outgoing = outgoing.astype(jnp.bfloat16).reshape(view_frames, view_cells, 2 * channels)
    portion = lax.all_gather(outgoing, "tile", axis=1, tiled=True)
    key_part = portion[:, :, :channels]
    value_part = portion[:, :, channels:]
    row_top = jnp.full((view_frames, view_cells, 1), -1e30, jnp.float32)
    scores = (
        jnp.einsum("fqc,fkc->fqk", queries, key_part, preferred_element_type=jnp.float32)
        * score_scale
    )
    new_top = jnp.maximum(row_top, jnp.max(scores, axis=2, keepdims=True))
    raised_f = jnp.exp(scores - new_top)
    row_total = jnp.sum(raised_f, axis=2, keepdims=True)
    weighted = jnp.einsum(
        "fqk,fkc->fqc",
        raised_f.astype(jnp.bfloat16),
        value_part,
        preferred_element_type=jnp.float32,
    )
    mixture_grid = (weighted / row_total).astype(jnp.bfloat16)
    mixture = mixture_grid.reshape(-1, channels)
    projected = jnp.dot(mixture, w_out, preferred_element_type=jnp.float32)
    attended = (features.reshape(-1, channels).astype(jnp.float32) + projected).astype(jnp.bfloat16)
    attended = attended.reshape(frames, row_count, col_count, channels)
    lifted = rms_scale(attended, conv_gain)
    activated = (lifted * jax.nn.sigmoid(lifted)).astype(jnp.bfloat16)
    earlier = from_behind(activated, "span", 1)
    stacked = jnp.concatenate([earlier, activated], axis=0)
    edged = extended(stacked, (("tile", 1),), 1)
    padded = jnp.pad(edged, ((0, 0), (0, 0), (1, 1), (0, 0)))
    clip_ends = jnp.cumsum(clip_lengths)
    position = lax.axis_index("span") * frames + jnp.arange(frames, dtype=jnp.int32)
    clip_start = jnp.sum(
        jnp.where(clip_ends[None, :] <= position[:, None], clip_lengths[None, :], 0), axis=1
    )
    summed = jnp.zeros((frames * cell_count, channels), jnp.float32)
    for t_tap in range(3):
        usable = position - (2 - t_tap) >= clip_start
        for r_tap in range(3):
            for c_tap in range(3):
                shifted = padded[
                    t_tap : t_tap + frames, r_tap : r_tap + row_count, c_tap : c_tap + col_count
                ]
                shifted = jnp.where(
                    usable[:, None, None, None], shifted, jnp.zeros((), shifted.dtype)
                )
                summed = summed + jnp.dot(
                    shifted.reshape(-1, channels),
                    w_conv[t_tap, r_tap, c_tap],
                    preferred_element_type=jnp.float32,
                )
    hidden = summed.astype(jnp.bfloat16).reshape(frames, row_count, col_count, channels)
    return (attended, hidden)


def solution(mesh):
    in_specs = (P(("grp", "span"), "tile", None, None), P("grp"), P(), P(), P(), P(), P())
    out_specs = (P(("grp", "span"), "tile", None, None), P(("grp", "span"), "tile", None, None))
    return jax.shard_map(
        on_device, mesh=mesh, in_specs=in_specs, out_specs=out_specs, check_vma=False
    )
```

```python
import functools

import jax
import jax.numpy as jnp
from jax import lax
from jax.experimental import pallas as pl
from jax.experimental.pallas import tpu as pltpu
from jax.sharding import PartitionSpec as P

eps = 1e-06
f32, bf16 = jnp.float32, jnp.bfloat16
LOG2E = 1.4426950408889634
VMEM = pl.BlockSpec(memory_space=pltpu.VMEM)
SMEM = pl.BlockSpec(memory_space=pltpu.SMEM)
ANY = pl.BlockSpec(memory_space=pl.ANY)


def from_behind(block, axis, distance):
    devices = range(lax.axis_size(axis))
    route = [(i - distance, i) for i in devices if i - distance in devices]
    return lax.ppermute(block, axis, route)


def rms_scale(values, gain_vec):
    as_float = values.astype(f32)
    return (
        as_float * lax.rsqrt(jnp.mean(as_float * as_float, axis=-1, keepdims=True) + eps) * gain_vec
    )


def dot32(a, b):
    return jnp.dot(a, b, preferred_element_type=f32)


def struct(shape, dtype=bf16):
    return jax.ShapeDtypeStruct(shape, dtype)


def call(kernel, name, out_shape, in_specs, scratch=(), limit=16, flops=0, size=1 << 20):
    outs = jax.tree.map(lambda _: VMEM, out_shape)
    cost = pl.CostEstimate(flops=int(flops), transcendentals=0, bytes_accessed=int(size))
    return pl.pallas_call(
        kernel,
        out_shape=out_shape,
        in_specs=in_specs,
        out_specs=outs,
        scratch_shapes=list(scratch),
        compiler_params=pltpu.CompilerParams(vmem_limit_bytes=limit << 20),
        cost_estimate=cost,
        name=name,
    )


def frame_route(spans, flip):
    route = []
    for tile in range(4):
        for span in range(spans):
            high, low, column, core = tile // 2, tile % 2, span // 2, span % 2
            there = (2 * core + (low ^ flip)) * spans + 2 * column + high
            route.append((tile * spans + span, there))
    return route


def shifted_route(tiles, spans, down, ahead):
    return [
        (t * spans + s, (t + down) * spans + s + ahead)
        for t in range(tiles)
        for s in range(spans)
        if 0 <= t + down < tiles and s + ahead < spans
    ]


def load_small_kernel(w_qkv, w_out, qkv_vm, out_vm, sem):
    copies = [
        pltpu.make_async_copy(w_qkv, qkv_vm, sem.at[0]),
        pltpu.make_async_copy(w_out, out_vm, sem.at[1]),
    ]
    for copy in copies:
        copy.start()
    for copy in copies:
        copy.wait()


def project_keys(block, gain_vec, w_qkv, out, place):
    cells, ch = block.shape
    normed = rms_scale(block[...], gain_vec).astype(bf16)
    out[place * cells : (place + 1) * cells, :] = dot32(normed, w_qkv[:, ch:]).astype(bf16)


def keys_kernel(own, other, gain, w_qkv, kv_out):
    gain_vec = gain[...].reshape(1, own.shape[1])
    project_keys(own, gain_vec, w_qkv, kv_out, 0)
    project_keys(other, gain_vec, w_qkv, kv_out, 1)


def attend_rows(cols, source, kv_parts, gain_vec, w_qkv, w_out, att_out):
    ch = source.shape[1]
    for row in range(source.shape[0] // cols):
        part = slice(row * cols, (row + 1) * cols)
        feats = source[part, :]
        normed = rms_scale(feats, gain_vec).astype(bf16)
        queries = dot32(normed, w_qkv[:, :ch]).astype(bf16)
        scores = [
            lax.dot_general(
                queries, kv[:, :ch], (((1,), (1,)), ((), ())), preferred_element_type=f32
            )
            * (ch ** (-0.5) * LOG2E)
            for kv in kv_parts
        ]
        top = functools.reduce(
            jnp.maximum, [jnp.max(s, axis=1, keepdims=True) for s in scores]
        )
        raised = [jnp.exp2(s - top) for s in scores]
        total = sum(jnp.sum(r, axis=1, keepdims=True) for r in raised)
        mixed = sum(dot32(r.astype(bf16), kv[:, ch:]) for r, kv in zip(raised, kv_parts))
        mixture = (mixed / total).astype(bf16)
        att_out[part, :] = (feats.astype(f32) + dot32(mixture, w_out[...])).astype(bf16)


def attend_kernel(cols, own_b, other_b, own_a, kv_a, gain, w_qkv, w_out, kv_b, att_a):
    gain_vec = gain[...].reshape(1, own_a.shape[1])
    project_keys(own_b, gain_vec, w_qkv, kv_b, 0)
    project_keys(other_b, gain_vec, w_qkv, kv_b, 1)
    attend_rows(cols, own_a, (kv_a, kv_b), gain_vec, w_qkv, w_out, att_a)


def attend_rest_kernel(cols, own_b, kv_a, kv_b, gain, w_qkv, w_out, att_b):
    gain_vec = gain[...].reshape(1, own_b.shape[1])
    attend_rows(cols, own_b, (kv_a, kv_b), gain_vec, w_qkv, w_out, att_b)


def activate_kernel(cols, tile_ref, got_a, got_b, gain, attended, active, pair_edge, mid_edge):
    low = tile_ref[0] % 2
    gain_vec = gain[...].reshape(1, got_a.shape[1])
    first_row, second_row = slice(0, cols), slice(cols, 2 * cols)

    def one(block, frame):
        values = block[...]
        attended[frame] = values
        lifted = rms_scale(values, gain_vec)
        act = (lifted / (1.0 + jnp.exp(-lifted))).astype(bf16)
        active[frame] = act

        @pl.when(low == 0)
        def _():
            pair_edge[frame] = act[second_row, :]
            mid_edge[frame] = act[first_row, :]

        @pl.when(low == 1)
        def _():
            pair_edge[frame] = act[first_row, :]
            mid_edge[frame] = act[second_row, :]

    one(got_a, low)
    one(got_b, 1 - low)


def usable_flag(clips, frame_at, tap):
    end = jnp.int32(0)
    start = jnp.int32(0)
    for i in range(clips.shape[0]):
        end = end + clips[i]
        start = start + jnp.where(end <= frame_at, clips[i], 0)
    return frame_at - (2 - tap) >= start


def shift_add(part, cols, ch):
    at = lax.broadcasted_iota(jnp.int32, (cols, ch), 0)
    left = jnp.where(at == 0, 0.0, pltpu.roll(part[:, :ch], 1, 0))
    right = jnp.where(at == cols - 1, 0.0, pltpu.roll(part[:, 2 * ch :], cols - 1, 0))
    return part[:, ch : 2 * ch] + left + right


def weigh(flag, block):
    return (block.astype(f32) * flag).astype(bf16)


def flags_of(clips, frame_at):
    return [
        [usable_flag(clips, frame_at + f, tap).astype(f32) for tap in range(3)] for f in range(2)
    ]


def next_own_kernel(cols, span_ref, clips, mid, w_hbm, out, w, sem):
    ch = mid.shape[-1]
    copies = [
        [
            pltpu.make_async_copy(
                w_hbm.at[i, j, k],
                w.at[i, j * ch : (j + 1) * ch, k * ch : (k + 1) * ch],
                sem.at[9 * i + 3 * j + k],
            )
            for j in range(3)
            for k in range(3)
        ]
        for i in range(3)
    ]
    for tap in copies:
        for copy in tap:
            copy.start()
    flag = flags_of(clips, (span_ref[0] + 1) * 2)
    first_row, second_row = slice(0, cols), slice(cols, 2 * cols)
    pair = [
        jnp.concatenate([mid[f, first_row, :], mid[f, second_row, :]], axis=1) for f in range(2)
    ]
    last = jnp.concatenate([weigh(flag[0][0], pair[0]), weigh(flag[1][0], pair[1])], axis=0)
    middle = weigh(flag[0][1], pair[1])
    parts = ((first_row, slice(ch, 3 * ch)), (second_row, slice(0, 2 * ch)))
    for copy in copies[0]:
        copy.wait()
    for part, taps in parts:
        far = dot32(last, w[0, taps])
        out[0, part, :] = shift_add(far[:cols], cols, ch)
        out[1, part, :] = shift_add(far[cols:], cols, ch)
    for copy in copies[1]:
        copy.wait()
    for part, taps in parts:
        out[0, part, :] += shift_add(dot32(middle, w[1, taps]), cols, ch)
    for copy in copies[2]:
        copy.wait()


def next_edge_kernel(cols, tile_ref, span_ref, clips, pair_got, mid_got, w, partial, out):
    ch = w.shape[-1] // 3
    flag = flags_of(clips, (span_ref[0] + 1) * 2)
    odd = tile_ref[0] % 2 == 1
    for f_pair, part, taps in (
        (odd, slice(0, cols), slice(0, ch)),
        (jnp.logical_not(odd), slice(cols, 2 * cols), slice(2 * ch, 3 * ch)),
    ):
        pick = f_pair.astype(f32)
        edge = [
            pair_got[f].astype(f32) * pick + mid_got[f].astype(f32) * (1.0 - pick)
            for f in range(2)
        ]
        last = jnp.concatenate([edge[0] * flag[0][0], edge[1] * flag[1][0]], axis=0).astype(bf16)
        middle = (edge[1] * flag[0][1]).astype(bf16)
        far = dot32(last, w[0, taps])
        near = far[:cols] + dot32(middle, w[1, taps])
        for f, val in ((0, near), (1, far[cols:])):
            out[f, part, :] = (shift_add(val, cols, ch) + partial[f, part, :]).astype(bf16)


def own_kernel(cols, tile_ref, span_ref, clips, mid, pair_got, mid_got, w, out):
    ch = mid.shape[-1]
    flag = flags_of(clips, span_ref[0] * 2)
    pick = (tile_ref[0] % 2).astype(f32)
    first_row, second_row = slice(0, cols), slice(cols, 2 * cols)
    wide = []
    for f in range(2):
        pair, other = pair_got[f].astype(f32), mid_got[f].astype(f32)
        above = (pair * pick + other * (1.0 - pick)).astype(bf16)
        below = (other * pick + pair * (1.0 - pick)).astype(bf16)
        rows = [above, mid[f, first_row, :], mid[f, second_row, :], below]
        wide.append([jnp.concatenate(rows[r : r + 3], axis=1) for r in range(2)])
    here = dot32(jnp.concatenate(wide[0] + wide[1], axis=0), w[2])
    back = dot32(jnp.concatenate([weigh(flag[1][1], x) for x in wide[0]], axis=0), w[1])
    for r in range(2):
        part = slice(r * cols, (r + 1) * cols)
        out[0, part, :] = shift_add(here[part], cols, ch)
        after = here[(2 + r) * cols : (3 + r) * cols]
        out[1, part, :] = shift_add(after + back[part], cols, ch)


def on_device(features, clip_lengths, norm_gain, w_qkv, w_out, conv_gain, w_conv):
    frames, row_count, cols, ch = features.shape
    tiles, spans = lax.axis_size("tile"), lax.axis_size("span")
    if tiles != 4 or spans % 2 or frames != 2 or row_count != 2:
        return general(features, clip_lengths, norm_gain, w_qkv, w_out, conv_gain, w_conv)
    cells = row_count * cols
    both = ("tile", "span")
    tile = lax.axis_index("tile").astype(jnp.int32).reshape(1)
    span = lax.axis_index("span").astype(jnp.int32).reshape(1)
    other_core = [(i, i ^ 1) for i in range(spans)]
    route_a, route_b = frame_route(spans, 0), frame_route(spans, 1)
    low = tile[0] % 2
    x = features.reshape(frames, cells, ch)
    send_a = lax.dynamic_index_in_dim(x, low, 0, keepdims=False)
    send_b = lax.dynamic_index_in_dim(x, 1 - low, 0, keepdims=False)
    own_a = lax.ppermute(send_a, both, route_a)
    own_b = lax.ppermute(send_b, both, route_b)
    w_qkv, w_out = call(
        load_small_kernel,
        "load_small",
        tuple(pltpu.VMEM(w.shape, bf16) for w in (w_qkv, w_out)),
        [ANY] * 2,
        [pltpu.SemaphoreType.DMA((2,))],
        60,
    )(w_qkv, w_out)
    own_a, w_qkv = lax.optimization_barrier((own_a, w_qkv))
    other_a = lax.ppermute(own_a, "span", other_core)
    other_b = lax.ppermute(own_b, "span", other_core)
    kv_flops = 2 * 2 * cells * ch * 2 * ch
    row_flops = 2 * cells * ch * (2 * ch + 8 * cells)
    kv_a = call(keys_kernel, "keys", struct((2 * cells, 2 * ch)), [VMEM] * 4, flops=kv_flops)(
        own_a, other_a, norm_gain, w_qkv
    )
    kv_b, att_a = call(
        functools.partial(attend_kernel, cols),
        "attend",
        (struct((2 * cells, 2 * ch)), struct((cells, ch))),
        [VMEM] * 7,
        flops=kv_flops + row_flops,
    )(own_b, other_b, own_a, kv_a, norm_gain, w_qkv, w_out)
    got_a = lax.ppermute(att_a, both, route_a)
    att_b = call(
        functools.partial(attend_rest_kernel, cols),
        "attend_rest",
        struct((cells, ch)),
        [VMEM] * 6,
        flops=3 * row_flops,
    )(own_b, kv_a, kv_b, norm_gain, w_qkv, w_out)
    got_b = lax.ppermute(att_b, both, route_b)
    attended, active, pair_edge, mid_edge = call(
        functools.partial(activate_kernel, cols),
        "activate",
        (
            struct((frames, cells, ch)),
            struct((frames, cells, ch)),
            struct((frames, cols, ch)),
            struct((frames, cols, ch)),
        ),
        [SMEM] + [VMEM] * 3,
    )(tile, got_a, got_b, conv_gain)
    pair_got = lax.ppermute(pair_edge, "tile", [(0, 1), (1, 0), (2, 3), (3, 2)])
    mid_got = lax.ppermute(mid_edge, "tile", [(1, 2), (2, 1)])
    block = struct((frames, cells, ch))
    sums = struct((frames, cells, ch), f32)
    unit = 2 * cells * 9 * ch * ch
    started, w_packed = call(
        functools.partial(next_own_kernel, cols),
        "next_own",
        (sums, struct((3, 3 * ch, 3 * ch))),
        [SMEM] * 2 + [VMEM, ANY],
        [pltpu.SemaphoreType.DMA((27,))],
        42,
        flops=2 * unit,
    )(span, clip_lengths, active, w_conv)
    for_next = call(
        functools.partial(next_edge_kernel, cols),
        "next_edge",
        block,
        [SMEM] * 3 + [VMEM] * 4,
        flops=unit,
    )(tile, span, clip_lengths, pair_got, mid_got, w_packed, started)
    earlier = lax.ppermute(for_next, both, shifted_route(tiles, spans, 0, 1))
    own = call(
        functools.partial(own_kernel, cols), "own", sums, [SMEM] * 3 + [VMEM] * 4, flops=3 * unit
    )(tile, span, clip_lengths, active, pair_got, mid_got, w_packed)
    hidden = (own + earlier.astype(f32)).astype(bf16)
    shape = (frames, row_count, cols, ch)
    return attended.reshape(shape), hidden.reshape(shape)


def extended(x, sides, width):
    for axis, dim in sides:
        size, length = (lax.axis_size(axis), x.shape[dim])
        up = [(i, (i + 1) % size) for i in range(size - 1)]
        down = [(j, i) for i, j in up]
        last = lax.slice_in_dim(x, length - width, length, axis=dim)
        first = lax.slice_in_dim(x, 0, width, axis=dim)
        before = lax.ppermute(last, axis, up)
        after = lax.ppermute(first, axis, down)
        x = jnp.concatenate([before, x, after], axis=dim)
    return x


def general(features, clip_lengths, norm_gain, w_qkv, w_out, conv_gain, w_conv):
    frames, row_count, col_count, channels = features.shape
    cell_count = row_count * col_count
    normed_grid = rms_scale(features, norm_gain).astype(jnp.bfloat16)
    view_frames = normed_grid.shape[0]
    view_cells = normed_grid.shape[1] * normed_grid.shape[2]
    normed = normed_grid.reshape(view_frames, view_cells, channels)
    queries = jnp.dot(
        normed.reshape(-1, channels), w_qkv[:, :channels], preferred_element_type=jnp.float32
    )
    queries = queries.astype(jnp.bfloat16).reshape(view_frames, view_cells, channels)
    kv_weight = w_qkv[:, channels:]
    score_scale = channels ** (-0.5)
    outgoing = jnp.dot(normed.reshape(-1, channels), kv_weight, preferred_element_type=jnp.float32)
    outgoing = outgoing.astype(jnp.bfloat16).reshape(view_frames, view_cells, 2 * channels)
    portion = lax.all_gather(outgoing, "tile", axis=1, tiled=True)
    key_part = portion[:, :, :channels]
    value_part = portion[:, :, channels:]
    row_top = jnp.full((view_frames, view_cells, 1), -1e30, jnp.float32)
    scores = (
        jnp.einsum("fqc,fkc->fqk", queries, key_part, preferred_element_type=jnp.float32)
        * score_scale
    )
    new_top = jnp.maximum(row_top, jnp.max(scores, axis=2, keepdims=True))
    raised_f = jnp.exp(scores - new_top)
    row_total = jnp.sum(raised_f, axis=2, keepdims=True)
    weighted = jnp.einsum(
        "fqk,fkc->fqc",
        raised_f.astype(jnp.bfloat16),
        value_part,
        preferred_element_type=jnp.float32,
    )
    mixture_grid = (weighted / row_total).astype(jnp.bfloat16)
    mixture = mixture_grid.reshape(-1, channels)
    projected = jnp.dot(mixture, w_out, preferred_element_type=jnp.float32)
    attended = (features.reshape(-1, channels).astype(jnp.float32) + projected).astype(jnp.bfloat16)
    attended = attended.reshape(frames, row_count, col_count, channels)
    lifted = rms_scale(attended, conv_gain)
    activated = (lifted * jax.nn.sigmoid(lifted)).astype(jnp.bfloat16)
    earlier = from_behind(activated, "span", 1)
    stacked = jnp.concatenate([earlier, activated], axis=0)
    edged = extended(stacked, (("tile", 1),), 1)
    padded = jnp.pad(edged, ((0, 0), (0, 0), (1, 1), (0, 0)))
    clip_ends = jnp.cumsum(clip_lengths)
    position = lax.axis_index("span") * frames + jnp.arange(frames, dtype=jnp.int32)
    clip_start = jnp.sum(
        jnp.where(clip_ends[None, :] <= position[:, None], clip_lengths[None, :], 0), axis=1
    )
    summed = jnp.zeros((frames * cell_count, channels), jnp.float32)
    for t_tap in range(3):
        usable = position - (2 - t_tap) >= clip_start
        for r_tap in range(3):
            for c_tap in range(3):
                shifted = padded[
                    t_tap : t_tap + frames, r_tap : r_tap + row_count, c_tap : c_tap + col_count
                ]
                shifted = jnp.where(
                    usable[:, None, None, None], shifted, jnp.zeros((), shifted.dtype)
                )
                summed = summed + jnp.dot(
                    shifted.reshape(-1, channels),
                    w_conv[t_tap, r_tap, c_tap],
                    preferred_element_type=jnp.float32,
                )
    hidden = summed.astype(jnp.bfloat16).reshape(frames, row_count, col_count, channels)
    return (attended, hidden)


def solution(mesh):
    in_specs = (P(("grp", "span"), "tile", None, None), P("grp"), P(), P(), P(), P(), P())
    out_specs = (P(("grp", "span"), "tile", None, None), P(("grp", "span"), "tile", None, None))
    return jax.shard_map(
        on_device, mesh=mesh, in_specs=in_specs, out_specs=out_specs, check_vma=False
    )
```

```python
import functools

import jax
import jax.numpy as jnp
from jax import lax
from jax.experimental import pallas as pl
from jax.experimental.pallas import tpu as pltpu
from jax.sharding import PartitionSpec as P

eps = 1e-06
f32, bf16 = jnp.float32, jnp.bfloat16
LOG2E = 1.4426950408889634
VMEM = pl.BlockSpec(memory_space=pltpu.VMEM)
SMEM = pl.BlockSpec(memory_space=pltpu.SMEM)
ANY = pl.BlockSpec(memory_space=pl.ANY)


def from_behind(block, axis, distance):
    devices = range(lax.axis_size(axis))
    route = [(i - distance, i) for i in devices if i - distance in devices]
    return lax.ppermute(block, axis, route)


def rms_scale(values, gain_vec):
    as_float = values.astype(f32)
    return (
        as_float * lax.rsqrt(jnp.mean(as_float * as_float, axis=-1, keepdims=True) + eps) * gain_vec
    )


def dot32(a, b):
    return jnp.dot(a, b, preferred_element_type=f32)


def struct(shape, dtype=bf16):
    return jax.ShapeDtypeStruct(shape, dtype)


def call(kernel, name, out_shape, in_specs, scratch=(), limit=16, flops=0, size=1 << 20):
    outs = jax.tree.map(lambda _: VMEM, out_shape)
    cost = pl.CostEstimate(flops=int(flops), transcendentals=0, bytes_accessed=int(size))
    return pl.pallas_call(
        kernel,
        out_shape=out_shape,
        in_specs=in_specs,
        out_specs=outs,
        scratch_shapes=list(scratch),
        compiler_params=pltpu.CompilerParams(vmem_limit_bytes=limit << 20),
        cost_estimate=cost,
        name=name,
    )


def frame_route(spans, flip):
    route = []
    for tile in range(4):
        for span in range(spans):
            high, low, column, core = tile // 2, tile % 2, span // 2, span % 2
            there = (2 * core + (low ^ flip)) * spans + 2 * column + high
            route.append((tile * spans + span, there))
    return route


def shifted_route(tiles, spans, down, ahead):
    return [
        (t * spans + s, (t + down) * spans + s + ahead)
        for t in range(tiles)
        for s in range(spans)
        if 0 <= t + down < tiles and s + ahead < spans
    ]


def load_small_kernel(w_qkv, w_out, gain, qkv_vm, out_vm, gain_vm, sem):
    copies = [
        pltpu.make_async_copy(w_qkv, qkv_vm, sem.at[0]),
        pltpu.make_async_copy(w_out, out_vm, sem.at[1]),
    ]
    for copy in copies:
        copy.start()
    gain_vm[...] = gain[...]
    for copy in copies:
        copy.wait()


def project_keys(block, gain_vec, w_qkv, out, place):
    cells, ch = block.shape
    normed = rms_scale(block[...], gain_vec).astype(bf16)
    out[place * cells : (place + 1) * cells, :] = dot32(normed, w_qkv[:, ch:]).astype(bf16)


def keys_kernel(own_a, other_a, own_b, gain, w_qkv, kv_out):
    gain_vec = gain[...].reshape(1, own_a.shape[1])
    for place, block in enumerate((own_a, other_a, own_b)):
        project_keys(block, gain_vec, w_qkv, kv_out, place)


def attend_rows(cols, source, kv_parts, gain_vec, w_qkv, w_out, att_out):
    ch = source.shape[1]
    for row in range(source.shape[0] // cols):
        part = slice(row * cols, (row + 1) * cols)
        feats = source[part, :]
        normed = rms_scale(feats, gain_vec).astype(bf16)
        queries = dot32(normed, w_qkv[:, :ch]).astype(bf16)
        scores = [
            lax.dot_general(
                queries, kv[:, :ch], (((1,), (1,)), ((), ())), preferred_element_type=f32
            )
            * (ch ** (-0.5) * LOG2E)
            for kv in kv_parts
        ]
        top = functools.reduce(
            jnp.maximum, [jnp.max(s, axis=1, keepdims=True) for s in scores]
        )
        raised = [jnp.exp2(s - top) for s in scores]
        total = sum(jnp.sum(r, axis=1, keepdims=True) for r in raised)
        mixed = sum(dot32(r.astype(bf16), kv[:, ch:]) for r, kv in zip(raised, kv_parts))
        mixture = (mixed / total).astype(bf16)
        att_out[part, :] = (feats.astype(f32) + dot32(mixture, w_out[...])).astype(bf16)


def attend_kernel(cols, other_b, own_a, kv_a, gain, w_qkv, w_out, kv_b, att_a):
    gain_vec = gain[...].reshape(1, own_a.shape[1])
    project_keys(other_b, gain_vec, w_qkv, kv_b, 0)
    attend_rows(cols, own_a, (kv_a, kv_b), gain_vec, w_qkv, w_out, att_a)


def attend_rest_kernel(cols, own_b, kv_a, kv_b, gain, w_qkv, w_out, att_b):
    gain_vec = gain[...].reshape(1, own_b.shape[1])
    attend_rows(cols, own_b, (kv_a, kv_b), gain_vec, w_qkv, w_out, att_b)


def activate(cols, low, block, gain, act_out, pair_edge, mid_edge):
    lifted = rms_scale(block[...], gain[...].reshape(1, block.shape[1]))
    act = (lifted / (1.0 + jnp.exp(-lifted))).astype(bf16)
    act_out[...] = act

    @pl.when(low == 0)
    def _():
        pair_edge[...] = act[cols:, :]
        mid_edge[...] = act[:cols, :]

    @pl.when(low == 1)
    def _():
        pair_edge[...] = act[:cols, :]
        mid_edge[...] = act[cols:, :]


def activate_a_kernel(cols, tile_ref, got_a, gain, *outs):
    activate(cols, tile_ref[0] % 2, got_a, gain, *outs)


def activate_b_kernel(cols, tile_ref, got_a, got_b, gain, attended, *outs):
    low = tile_ref[0] % 2
    activate(cols, low, got_b, gain, *outs)
    attended[low] = got_a[...]
    attended[1 - low] = got_b[...]


def usable_flag(clips, frame_at, tap):
    end = jnp.int32(0)
    start = jnp.int32(0)
    for i in range(clips.shape[0]):
        end = end + clips[i]
        start = start + jnp.where(end <= frame_at, clips[i], 0)
    return frame_at - (2 - tap) >= start


def shift_add(part, cols, ch):
    at = lax.broadcasted_iota(jnp.int32, (cols, ch), 0)
    left = jnp.where(at == 0, 0.0, pltpu.roll(part[:, :ch], 1, 0))
    right = jnp.where(at == cols - 1, 0.0, pltpu.roll(part[:, 2 * ch :], cols - 1, 0))
    return part[:, ch : 2 * ch] + left + right


def weigh(flag, block):
    return (block.astype(f32) * flag).astype(bf16)


def flag_at(clips, frame_at, tap):
    return usable_flag(clips, frame_at, tap).astype(f32)


def add_next(cols, frame, at_next, clips, block, part, w, taps, partial, out):
    ch = out.shape[-1]

    def put(n, value):
        value = shift_add(value, cols, ch)
        if partial is not None:
            value = value + partial[n, part, :]
        out[n, part, :] = value.astype(out.dtype)

    put(0, dot32(weigh(flag_at(clips, at_next, frame), block), w[frame, taps]))

    @pl.when(frame == 1)
    def _():
        put(1, dot32(weigh(flag_at(clips, at_next + 1, 0), block), w[0, taps]))

    @pl.when(frame == 0)
    def _():
        if partial is None:
            out[1, part, :] = jnp.zeros((cols, ch), out.dtype)
        else:
            out[1, part, :] = partial[1, part, :].astype(out.dtype)


def add_own_rows(cols, frame, at_next, clips, act, w, partial, out):
    ch = act.shape[-1]
    block = jnp.concatenate([act[:cols, :], act[cols:, :]], axis=1)
    for part, taps in (
        (slice(0, cols), slice(ch, 3 * ch)),
        (slice(cols, 2 * cols), slice(0, 2 * ch)),
    ):
        add_next(cols, frame, at_next, clips, block, part, w, taps, partial, out)


def next_a_kernel(cols, tile_ref, span_ref, clips, act, w_hbm, out, w, sem):
    ch = act.shape[-1]
    copies = [
        pltpu.make_async_copy(
            w_hbm.at[i, j, k],
            w.at[i, j * ch : (j + 1) * ch, k * ch : (k + 1) * ch],
            sem.at[9 * i + 3 * j + k],
        )
        for i in range(3)
        for j in range(3)
        for k in range(3)
    ]
    for copy in copies:
        copy.start()
    for copy in copies[:18]:
        copy.wait()
    low, at_next = tile_ref[0] % 2, (span_ref[0] + 1) * 2
    add_own_rows(cols, low, at_next, clips, act, w, None, out)
    for copy in copies[18:]:
        copy.wait()


def next_b_kernel(cols, tile_ref, span_ref, clips, act, w, partial, out):
    low, at_next = tile_ref[0] % 2, (span_ref[0] + 1) * 2
    add_own_rows(cols, 1 - low, at_next, clips, act, w, partial, out)


def edge_kernel(cols, second, tile_ref, span_ref, clips, pair_got, mid_got, w, partial, out):
    ch = w.shape[-1] // 3
    low, at_next = tile_ref[0] % 2, (span_ref[0] + 1) * 2
    frame = low if second else 1 - low
    pick = low.astype(f32)
    pair, mid = pair_got[...].astype(f32), mid_got[...].astype(f32)
    above = pair * pick + mid * (1.0 - pick)
    below = mid * pick + pair * (1.0 - pick)
    for block, part, taps in (
        (above, slice(0, cols), slice(0, ch)),
        (below, slice(cols, 2 * cols), slice(2 * ch, 3 * ch)),
    ):
        add_next(cols, frame, at_next, clips, block, part, w, taps, partial, out)


def own_kernel(
    cols, tile_ref, span_ref, clips, act_a, act_b, pair_a, mid_a, pair_b, mid_b, w, out, rows
):
    ch = act_a.shape[-1]
    low = tile_ref[0] % 2
    for frame, act, pair, mid in ((low, act_a, pair_b, mid_b), (1 - low, act_b, pair_a, mid_a)):
        rows[frame, cols : 3 * cols, :] = act[...]

        @pl.when(low == 0)
        def _(frame=frame, pair=pair, mid=mid):
            rows[frame, :cols, :] = mid[...]
            rows[frame, 3 * cols :, :] = pair[...]

        @pl.when(low == 1)
        def _(frame=frame, pair=pair, mid=mid):
            rows[frame, :cols, :] = pair[...]
            rows[frame, 3 * cols :, :] = mid[...]

    wide = [
        jnp.concatenate([rows[f, j * cols : (j + 2) * cols, :] for j in range(3)], axis=1)
        for f in range(2)
    ]
    here = dot32(jnp.concatenate(wide, axis=0), w[2])
    back = dot32(weigh(flag_at(clips, span_ref[0] * 2 + 1, 1), wide[0]), w[1])
    for r in range(2):
        part = slice(r * cols, (r + 1) * cols)
        out[0, part, :] = shift_add(here[part], cols, ch)
        after = here[(2 + r) * cols : (3 + r) * cols]
        out[1, part, :] = shift_add(after + back[part], cols, ch)


def on_device(features, clip_lengths, norm_gain, w_qkv, w_out, conv_gain, w_conv):
    frames, row_count, cols, ch = features.shape
    tiles, spans = lax.axis_size("tile"), lax.axis_size("span")
    if tiles != 4 or spans % 2 or frames != 2 or row_count != 2:
        return general(features, clip_lengths, norm_gain, w_qkv, w_out, conv_gain, w_conv)
    cells = row_count * cols
    both = ("tile", "span")
    tile = lax.axis_index("tile").astype(jnp.int32).reshape(1)
    span = lax.axis_index("span").astype(jnp.int32).reshape(1)
    other_core = [(i, i ^ 1) for i in range(spans)]
    route_a, route_b = frame_route(spans, 0), frame_route(spans, 1)
    low = tile[0] % 2
    x = features.reshape(frames, cells, ch)
    send_a = lax.dynamic_index_in_dim(x, low, 0, keepdims=False)
    send_b = lax.dynamic_index_in_dim(x, 1 - low, 0, keepdims=False)
    own_a = lax.ppermute(send_a, both, route_a)
    own_b = lax.ppermute(send_b, both, route_b)
    w_qkv, w_out, norm_gain = call(
        load_small_kernel,
        "load_small",
        (pltpu.VMEM(w_qkv.shape, bf16), pltpu.VMEM(w_out.shape, bf16), struct((ch,), f32)),
        [ANY, ANY, VMEM],
        [pltpu.SemaphoreType.DMA((2,))],
        60,
    )(w_qkv, w_out, norm_gain)
    own_a, w_qkv = lax.optimization_barrier((own_a, w_qkv))
    other_a = lax.ppermute(own_a, "span", other_core)
    other_b = lax.ppermute(own_b, "span", other_core)
    kv_flops = 2 * 2 * cells * ch * 2 * ch
    row_flops = 2 * cells * ch * (2 * ch + 8 * cells)
    kv_a = call(keys_kernel, "keys", struct((3 * cells, 2 * ch)), [VMEM] * 5, flops=kv_flops)(
        own_a, other_a, own_b, norm_gain, w_qkv
    )
    kv_b, att_a = call(
        functools.partial(attend_kernel, cols),
        "attend",
        (struct((cells, 2 * ch)), struct((cells, ch))),
        [VMEM] * 6,
        flops=kv_flops + row_flops,
    )(other_b, own_a, kv_a, norm_gain, w_qkv, w_out)
    got_a = lax.ppermute(att_a, both, route_a)
    att_b = call(
        functools.partial(attend_rest_kernel, cols),
        "attend_rest",
        struct((cells, ch)),
        [VMEM] * 6,
        flops=3 * row_flops,
    )(own_b, kv_a, kv_b, norm_gain, w_qkv, w_out)
    got_b = lax.ppermute(att_b, both, route_b)
    pairs, middle = [(0, 1), (1, 0), (2, 3), (3, 2)], [(1, 2), (2, 1)]
    one, edge = struct((cells, ch)), struct((cols, ch))
    sums = struct((frames, cells, ch), f32)
    unit = 2 * cells * 9 * ch * ch
    where = (tile, span, clip_lengths)
    act_a, pair_edge, mid_edge = call(
        functools.partial(activate_a_kernel, cols), "activate_a", (one, edge, edge), [SMEM, VMEM, VMEM]
    )(tile, got_a, conv_gain)
    pair_a = lax.ppermute(pair_edge, "tile", pairs)
    mid_a = lax.ppermute(mid_edge, "tile", middle)
    next_a, w_packed = call(
        functools.partial(next_a_kernel, cols),
        "next_a",
        (sums, struct((3, 3 * ch, 3 * ch))),
        [SMEM] * 3 + [VMEM, ANY],
        [pltpu.SemaphoreType.DMA((27,))],
        42,
        flops=unit,
    )(*where, act_a, w_conv)
    got_b, next_a = lax.optimization_barrier((got_b, next_a))
    attended, act_b, pair_edge, mid_edge = call(
        functools.partial(activate_b_kernel, cols),
        "activate_b",
        (struct((frames, cells, ch)), one, edge, edge),
        [SMEM] + [VMEM] * 3,
    )(tile, got_a, got_b, conv_gain)
    pair_b = lax.ppermute(pair_edge, "tile", pairs)
    mid_b = lax.ppermute(mid_edge, "tile", middle)
    next_b = call(
        functools.partial(next_b_kernel, cols), "next_b", sums, [SMEM] * 3 + [VMEM] * 3, flops=unit
    )(*where, act_b, w_packed, next_a)
    edges_a = call(
        functools.partial(edge_kernel, cols, False),
        "edges_a",
        sums,
        [SMEM] * 3 + [VMEM] * 4,
        flops=unit // 2,
    )(*where, pair_a, mid_a, w_packed, next_b)
    for_next = call(
        functools.partial(edge_kernel, cols, True),
        "edges_b",
        struct((frames, cells, ch)),
        [SMEM] * 3 + [VMEM] * 4,
        flops=unit // 2,
    )(*where, pair_b, mid_b, w_packed, edges_a)
    earlier = lax.ppermute(for_next, both, shifted_route(tiles, spans, 0, 1))
    own = call(
        functools.partial(own_kernel, cols),
        "own",
        sums,
        [SMEM] * 3 + [VMEM] * 7,
        [pltpu.VMEM((frames, 4 * cols, ch), bf16)],
        flops=3 * unit,
    )(*where, act_a, act_b, pair_a, mid_a, pair_b, mid_b, w_packed)
    hidden = (own + earlier.astype(f32)).astype(bf16)
    shape = (frames, row_count, cols, ch)
    return attended.reshape(shape), hidden.reshape(shape)


def extended(x, sides, width):
    for axis, dim in sides:
        size, length = (lax.axis_size(axis), x.shape[dim])
        up = [(i, (i + 1) % size) for i in range(size - 1)]
        down = [(j, i) for i, j in up]
        last = lax.slice_in_dim(x, length - width, length, axis=dim)
        first = lax.slice_in_dim(x, 0, width, axis=dim)
        before = lax.ppermute(last, axis, up)
        after = lax.ppermute(first, axis, down)
        x = jnp.concatenate([before, x, after], axis=dim)
    return x


def general(features, clip_lengths, norm_gain, w_qkv, w_out, conv_gain, w_conv):
    frames, row_count, col_count, channels = features.shape
    cell_count = row_count * col_count
    normed_grid = rms_scale(features, norm_gain).astype(jnp.bfloat16)
    view_frames = normed_grid.shape[0]
    view_cells = normed_grid.shape[1] * normed_grid.shape[2]
    normed = normed_grid.reshape(view_frames, view_cells, channels)
    queries = jnp.dot(
        normed.reshape(-1, channels), w_qkv[:, :channels], preferred_element_type=jnp.float32
    )
    queries = queries.astype(jnp.bfloat16).reshape(view_frames, view_cells, channels)
    kv_weight = w_qkv[:, channels:]
    score_scale = channels ** (-0.5)
    outgoing = jnp.dot(normed.reshape(-1, channels), kv_weight, preferred_element_type=jnp.float32)
    outgoing = outgoing.astype(jnp.bfloat16).reshape(view_frames, view_cells, 2 * channels)
    portion = lax.all_gather(outgoing, "tile", axis=1, tiled=True)
    key_part = portion[:, :, :channels]
    value_part = portion[:, :, channels:]
    row_top = jnp.full((view_frames, view_cells, 1), -1e30, jnp.float32)
    scores = (
        jnp.einsum("fqc,fkc->fqk", queries, key_part, preferred_element_type=jnp.float32)
        * score_scale
    )
    new_top = jnp.maximum(row_top, jnp.max(scores, axis=2, keepdims=True))
    raised_f = jnp.exp(scores - new_top)
    row_total = jnp.sum(raised_f, axis=2, keepdims=True)
    weighted = jnp.einsum(
        "fqk,fkc->fqc",
        raised_f.astype(jnp.bfloat16),
        value_part,
        preferred_element_type=jnp.float32,
    )
    mixture_grid = (weighted / row_total).astype(jnp.bfloat16)
    mixture = mixture_grid.reshape(-1, channels)
    projected = jnp.dot(mixture, w_out, preferred_element_type=jnp.float32)
    attended = (features.reshape(-1, channels).astype(jnp.float32) + projected).astype(jnp.bfloat16)
    attended = attended.reshape(frames, row_count, col_count, channels)
    lifted = rms_scale(attended, conv_gain)
    activated = (lifted * jax.nn.sigmoid(lifted)).astype(jnp.bfloat16)
    earlier = from_behind(activated, "span", 1)
    stacked = jnp.concatenate([earlier, activated], axis=0)
    edged = extended(stacked, (("tile", 1),), 1)
    padded = jnp.pad(edged, ((0, 0), (0, 0), (1, 1), (0, 0)))
    clip_ends = jnp.cumsum(clip_lengths)
    position = lax.axis_index("span") * frames + jnp.arange(frames, dtype=jnp.int32)
    clip_start = jnp.sum(
        jnp.where(clip_ends[None, :] <= position[:, None], clip_lengths[None, :], 0), axis=1
    )
    summed = jnp.zeros((frames * cell_count, channels), jnp.float32)
    for t_tap in range(3):
        usable = position - (2 - t_tap) >= clip_start
        for r_tap in range(3):
            for c_tap in range(3):
                shifted = padded[
                    t_tap : t_tap + frames, r_tap : r_tap + row_count, c_tap : c_tap + col_count
                ]
                shifted = jnp.where(
                    usable[:, None, None, None], shifted, jnp.zeros((), shifted.dtype)
                )
                summed = summed + jnp.dot(
                    shifted.reshape(-1, channels),
                    w_conv[t_tap, r_tap, c_tap],
                    preferred_element_type=jnp.float32,
                )
    hidden = summed.astype(jnp.bfloat16).reshape(frames, row_count, col_count, channels)
    return (attended, hidden)


def solution(mesh):
    in_specs = (P(("grp", "span"), "tile", None, None), P("grp"), P(), P(), P(), P(), P())
    out_specs = (P(("grp", "span"), "tile", None, None), P(("grp", "span"), "tile", None, None))
    return jax.shard_map(
        on_device, mesh=mesh, in_specs=in_specs, out_specs=out_specs, check_vma=False
    )
```

```python
import functools

import jax
import jax.numpy as jnp
from jax import lax
from jax.experimental import pallas as pl
from jax.experimental.pallas import tpu as pltpu
from jax.sharding import PartitionSpec as P

eps = 1e-06
f32, bf16 = jnp.float32, jnp.bfloat16
LOG2E = 1.4426950408889634
VMEM = pl.BlockSpec(memory_space=pltpu.VMEM)
SMEM = pl.BlockSpec(memory_space=pltpu.SMEM)
ANY = pl.BlockSpec(memory_space=pl.ANY)


def from_behind(block, axis, distance):
    devices = range(lax.axis_size(axis))
    route = [(i - distance, i) for i in devices if i - distance in devices]
    return lax.ppermute(block, axis, route)


def rms_scale(values, gain_vec):
    as_float = values.astype(f32)
    return (
        as_float * lax.rsqrt(jnp.mean(as_float * as_float, axis=-1, keepdims=True) + eps) * gain_vec
    )


def dot32(a, b):
    return jnp.dot(a, b, preferred_element_type=f32)


def struct(shape, dtype=bf16):
    return jax.ShapeDtypeStruct(shape, dtype)


def call(kernel, name, out_shape, in_specs, scratch=(), limit=16, flops=0, size=1 << 20):
    outs = jax.tree.map(lambda _: VMEM, out_shape)
    cost = pl.CostEstimate(flops=int(flops), transcendentals=0, bytes_accessed=int(size))
    return pl.pallas_call(
        kernel,
        out_shape=out_shape,
        in_specs=in_specs,
        out_specs=outs,
        scratch_shapes=list(scratch),
        compiler_params=pltpu.CompilerParams(vmem_limit_bytes=limit << 20),
        cost_estimate=cost,
        name=name,
    )


def frame_route(spans, flip):
    route = []
    for tile in range(4):
        for span in range(spans):
            high, low, column, core = tile // 2, tile % 2, span // 2, span % 2
            there = (2 * core + (low ^ flip)) * spans + 2 * column + high
            route.append((tile * spans + span, there))
    return route


def shifted_route(tiles, spans, down, ahead):
    return [
        (t * spans + s, (t + down) * spans + s + ahead)
        for t in range(tiles)
        for s in range(spans)
        if 0 <= t + down < tiles and s + ahead < spans
    ]


def load_small_kernel(w_qkv, w_out, gain, qkv_vm, out_vm, gain_vm, sem):
    copies = [
        pltpu.make_async_copy(w_qkv, qkv_vm, sem.at[0]),
        pltpu.make_async_copy(w_out, out_vm, sem.at[1]),
    ]
    for copy in copies:
        copy.start()
    gain_vm[...] = gain[...]
    for copy in copies:
        copy.wait()


def project_keys(block, gain_vec, w_qkv, out, place):
    cells, ch = block.shape
    normed = rms_scale(block[...], gain_vec).astype(bf16)
    out[place * cells : (place + 1) * cells, :] = dot32(normed, w_qkv[:, ch:]).astype(bf16)


def keys_kernel(own_a, other_a, own_b, gain, w_qkv, kv_out):
    gain_vec = gain[...].reshape(1, own_a.shape[1])
    for place, block in enumerate((own_a, other_a, own_b)):
        project_keys(block, gain_vec, w_qkv, kv_out, place)


def attend_rows(cols, source, kv_parts, gain_vec, w_qkv, w_out, att_out):
    ch = source.shape[1]
    for row in range(source.shape[0] // cols):
        part = slice(row * cols, (row + 1) * cols)
        feats = source[part, :]
        normed = rms_scale(feats, gain_vec).astype(bf16)
        queries = dot32(normed, w_qkv[:, :ch]).astype(bf16)
        scores = [
            lax.dot_general(
                queries, kv[:, :ch], (((1,), (1,)), ((), ())), preferred_element_type=f32
            )
            * (ch ** (-0.5) * LOG2E)
            for kv in kv_parts
        ]
        top = functools.reduce(
            jnp.maximum, [jnp.max(s, axis=1, keepdims=True) for s in scores]
        )
        raised = [jnp.exp2(s - top) for s in scores]
        total = sum(jnp.sum(r, axis=1, keepdims=True) for r in raised)
        mixed = sum(dot32(r.astype(bf16), kv[:, ch:]) for r, kv in zip(raised, kv_parts))
        mixture = (mixed / total).astype(bf16)
        att_out[part, :] = (feats.astype(f32) + dot32(mixture, w_out[...])).astype(bf16)


def attend_kernel(cols, other_b, own_a, kv_a, gain, w_qkv, w_out, kv_b, att_a):
    gain_vec = gain[...].reshape(1, own_a.shape[1])
    project_keys(other_b, gain_vec, w_qkv, kv_b, 0)
    attend_rows(cols, own_a, (kv_a, kv_b), gain_vec, w_qkv, w_out, att_a)


def attend_rest_kernel(cols, own_b, kv_a, kv_b, gain, w_qkv, w_out, att_b):
    gain_vec = gain[...].reshape(1, own_b.shape[1])
    attend_rows(cols, own_b, (kv_a, kv_b), gain_vec, w_qkv, w_out, att_b)


def load_kernel(_, w_hbm, w_vm, sem):
    ch = w_hbm.shape[-1]
    copies = [
        pltpu.make_async_copy(
            w_hbm.at[i, j, k],
            w_vm.at[i, j * ch : (j + 1) * ch, k * ch : (k + 1) * ch],
            sem.at[9 * i + 3 * j + k],
        )
        for i in range(3)
        for j in range(3)
        for k in range(3)
    ]
    for copy in copies:
        copy.start()
    for copy in copies:
        copy.wait()


def activate(cols, low, block, gain, act_out, pair_edge, mid_edge):
    lifted = rms_scale(block[...], gain[...].reshape(1, block.shape[1]))
    act = (lifted / (1.0 + jnp.exp(-lifted))).astype(bf16)
    act_out[...] = act

    @pl.when(low == 0)
    def _():
        pair_edge[...] = act[cols:, :]
        mid_edge[...] = act[:cols, :]

    @pl.when(low == 1)
    def _():
        pair_edge[...] = act[:cols, :]
        mid_edge[...] = act[cols:, :]


def activate_a_kernel(cols, tile_ref, got_a, gain, *outs):
    activate(cols, tile_ref[0] % 2, got_a, gain, *outs)


def activate_b_kernel(
    cols, tile_ref, got_a, got_b, act_a, gain, _, attended, active, pair_edge, mid_edge
):
    low = tile_ref[0] % 2
    activate(cols, low, got_b, gain, active.at[1 - low], pair_edge, mid_edge)
    active[low] = act_a[...]
    attended[low] = got_a[...]
    attended[1 - low] = got_b[...]


def usable_flag(clips, frame_at, tap):
    end = jnp.int32(0)
    start = jnp.int32(0)
    for i in range(clips.shape[0]):
        end = end + clips[i]
        start = start + jnp.where(end <= frame_at, clips[i], 0)
    return frame_at - (2 - tap) >= start


def shift_add(part, cols, ch):
    at = lax.broadcasted_iota(jnp.int32, (cols, ch), 0)
    left = jnp.where(at == 0, 0.0, pltpu.roll(part[:, :ch], 1, 0))
    right = jnp.where(at == cols - 1, 0.0, pltpu.roll(part[:, 2 * ch :], cols - 1, 0))
    return part[:, ch : 2 * ch] + left + right


def weigh(flag, block):
    return (block.astype(f32) * flag).astype(bf16)


def flags_of(clips, frame_at):
    return [
        [usable_flag(clips, frame_at + f, tap).astype(f32) for tap in range(3)] for f in range(2)
    ]


def edge_rows(tile_ref, pair_a, mid_a, pair_b, mid_b):
    odd = (tile_ref[0] % 2).astype(f32)

    def pick(if_odd, if_even):
        return if_odd[...].astype(f32) * odd + if_even[...].astype(f32) * (1.0 - odd)

    above = [pick(pair_a, mid_b), pick(pair_b, mid_a)]
    below = [pick(mid_a, pair_b), pick(mid_b, pair_a)]
    return above, below


def next_own_kernel(cols, span_ref, clips, mid, w, out):
    ch = mid.shape[-1]
    flag = flags_of(clips, (span_ref[0] + 1) * 2)
    first_row, second_row = slice(0, cols), slice(cols, 2 * cols)
    pair = [
        jnp.concatenate([mid[f, first_row, :], mid[f, second_row, :]], axis=1) for f in range(2)
    ]
    last = jnp.concatenate([weigh(flag[0][0], pair[0]), weigh(flag[1][0], pair[1])], axis=0)
    middle = weigh(flag[0][1], pair[1])
    for part, taps in ((first_row, slice(ch, 3 * ch)), (second_row, slice(0, 2 * ch))):
        far = dot32(last, w[0, taps])
        out[0, part, :] = shift_add(far[:cols] + dot32(middle, w[1, taps]), cols, ch)
        out[1, part, :] = shift_add(far[cols:], cols, ch)


def next_edge_kernel(
    cols, tile_ref, span_ref, clips, pair_a, mid_a, pair_b, mid_b, w, partial, out
):
    ch = w.shape[-1] // 3
    flag = flags_of(clips, (span_ref[0] + 1) * 2)
    above, below = edge_rows(tile_ref, pair_a, mid_a, pair_b, mid_b)
    for edge, part, taps in (
        (above, slice(0, cols), slice(0, ch)),
        (below, slice(cols, 2 * cols), slice(2 * ch, 3 * ch)),
    ):
        last = jnp.concatenate([edge[0] * flag[0][0], edge[1] * flag[1][0]], axis=0).astype(bf16)
        middle = (edge[1] * flag[0][1]).astype(bf16)
        far = dot32(last, w[0, taps])
        near = far[:cols] + dot32(middle, w[1, taps])
        for f, val in ((0, near), (1, far[cols:])):
            out[f, part, :] = (shift_add(val, cols, ch) + partial[f, part, :]).astype(bf16)


def own_kernel(cols, tile_ref, span_ref, clips, mid, pair_a, mid_a, pair_b, mid_b, w, out):
    ch = mid.shape[-1]
    above, below = edge_rows(tile_ref, pair_a, mid_a, pair_b, mid_b)
    wide = []
    for f in range(2):
        rows = [above[f].astype(bf16), mid[f, :cols, :], mid[f, cols:, :], below[f].astype(bf16)]
        wide += [jnp.concatenate(rows[r : r + 3], axis=1) for r in range(2)]
    here = dot32(jnp.concatenate(wide, axis=0), w[2])
    flag = usable_flag(clips, span_ref[0] * 2 + 1, 1).astype(f32)
    back = dot32(weigh(flag, jnp.concatenate(wide[:2], axis=0)), w[1])
    for r in range(2):
        part = slice(r * cols, (r + 1) * cols)
        out[0, part, :] = shift_add(here[part], cols, ch)
        after = here[(2 + r) * cols : (3 + r) * cols]
        out[1, part, :] = shift_add(after + back[part], cols, ch)


def on_device(features, clip_lengths, norm_gain, w_qkv, w_out, conv_gain, w_conv):
    frames, row_count, cols, ch = features.shape
    tiles, spans = lax.axis_size("tile"), lax.axis_size("span")
    if tiles != 4 or spans % 2 or frames != 2 or row_count != 2:
        return general(features, clip_lengths, norm_gain, w_qkv, w_out, conv_gain, w_conv)
    cells = row_count * cols
    both = ("tile", "span")
    tile = lax.axis_index("tile").astype(jnp.int32).reshape(1)
    span = lax.axis_index("span").astype(jnp.int32).reshape(1)
    other_core = [(i, i ^ 1) for i in range(spans)]
    route_a, route_b = frame_route(spans, 0), frame_route(spans, 1)
    low = tile[0] % 2
    x = features.reshape(frames, cells, ch)
    send_a = lax.dynamic_index_in_dim(x, low, 0, keepdims=False)
    send_b = lax.dynamic_index_in_dim(x, 1 - low, 0, keepdims=False)
    own_a = lax.ppermute(send_a, both, route_a)
    own_b = lax.ppermute(send_b, both, route_b)
    w_qkv, w_out, norm_gain = call(
        load_small_kernel,
        "load_small",
        (pltpu.VMEM(w_qkv.shape, bf16), pltpu.VMEM(w_out.shape, bf16), pltpu.VMEM((ch,), f32)),
        [ANY, ANY, VMEM],
        [pltpu.SemaphoreType.DMA((2,))],
        60,
    )(w_qkv, w_out, norm_gain)
    own_a, w_qkv = lax.optimization_barrier((own_a, w_qkv))
    other_a = lax.ppermute(own_a, "span", other_core)
    other_b = lax.ppermute(own_b, "span", other_core)
    kv_flops = 2 * 2 * cells * ch * 2 * ch
    row_flops = 2 * cells * ch * (2 * ch + 8 * cells)
    kv_a = call(keys_kernel, "keys", struct((3 * cells, 2 * ch)), [VMEM] * 5, flops=kv_flops)(
        own_a, other_a, own_b, norm_gain, w_qkv
    )
    kv_b, att_a = call(
        functools.partial(attend_kernel, cols),
        "attend",
        (struct((cells, 2 * ch)), struct((cells, ch))),
        [VMEM] * 6,
        flops=kv_flops + row_flops,
    )(other_b, own_a, kv_a, norm_gain, w_qkv, w_out)
    got_a = lax.ppermute(att_a, both, route_a)
    att_b = call(
        functools.partial(attend_rest_kernel, cols),
        "attend_rest",
        struct((cells, ch)),
        [VMEM] * 6,
        flops=3 * row_flops,
    )(own_b, kv_a, kv_b, norm_gain, w_qkv, w_out)
    got_b = lax.ppermute(att_b, both, route_b)
    pairs, middle = [(0, 1), (1, 0), (2, 3), (3, 2)], [(1, 2), (2, 1)]
    one, edge = struct((cells, ch)), struct((cols, ch))
    sums = struct((frames, cells, ch), f32)
    unit = 2 * cells * 9 * ch * ch
    where = (tile, span, clip_lengths)
    act_a, pair_edge, mid_edge = call(
        functools.partial(activate_a_kernel, cols), "activate_a", (one, edge, edge), [SMEM, VMEM, VMEM]
    )(tile, got_a, conv_gain)
    pair_a = lax.ppermute(pair_edge, "tile", pairs)
    mid_a = lax.ppermute(mid_edge, "tile", middle)
    w_packed = call(
        load_kernel,
        "load_conv",
        struct((3, 3 * ch, 3 * ch)),
        [ANY, ANY],
        [pltpu.SemaphoreType.DMA((27,))],
        42,
        size=1 << 12,
    )(act_a, w_conv)
    attended, active, pair_edge, mid_edge = call(
        functools.partial(activate_b_kernel, cols),
        "activate_b",
        (struct((frames, cells, ch)), struct((frames, cells, ch)), edge, edge),
        [SMEM] + [VMEM] * 4 + [ANY],
    )(tile, got_a, got_b, act_a, conv_gain, w_packed)
    pair_b = lax.ppermute(pair_edge, "tile", pairs)
    mid_b = lax.ppermute(mid_edge, "tile", middle)
    edges = (pair_a, mid_a, pair_b, mid_b)
    started = call(
        functools.partial(next_own_kernel, cols),
        "next_own",
        sums,
        [SMEM] * 2 + [VMEM] * 2,
        flops=2 * unit,
    )(span, clip_lengths, active, w_packed)
    for_next = call(
        functools.partial(next_edge_kernel, cols),
        "next_edge",
        struct((frames, cells, ch)),
        [SMEM] * 3 + [VMEM] * 6,
        flops=unit,
    )(*where, *edges, w_packed, started)
    earlier = lax.ppermute(for_next, both, shifted_route(tiles, spans, 0, 1))
    own = call(
        functools.partial(own_kernel, cols), "own", sums, [SMEM] * 3 + [VMEM] * 6, flops=3 * unit
    )(*where, active, *edges, w_packed)
    hidden = (own + earlier.astype(f32)).astype(bf16)
    shape = (frames, row_count, cols, ch)
    return attended.reshape(shape), hidden.reshape(shape)


def extended(x, sides, width):
    for axis, dim in sides:
        size, length = (lax.axis_size(axis), x.shape[dim])
        up = [(i, (i + 1) % size) for i in range(size - 1)]
        down = [(j, i) for i, j in up]
        last = lax.slice_in_dim(x, length - width, length, axis=dim)
        first = lax.slice_in_dim(x, 0, width, axis=dim)
        before = lax.ppermute(last, axis, up)
        after = lax.ppermute(first, axis, down)
        x = jnp.concatenate([before, x, after], axis=dim)
    return x


def general(features, clip_lengths, norm_gain, w_qkv, w_out, conv_gain, w_conv):
    frames, row_count, col_count, channels = features.shape
    cell_count = row_count * col_count
    normed_grid = rms_scale(features, norm_gain).astype(jnp.bfloat16)
    view_frames = normed_grid.shape[0]
    view_cells = normed_grid.shape[1] * normed_grid.shape[2]
    normed = normed_grid.reshape(view_frames, view_cells, channels)
    queries = jnp.dot(
        normed.reshape(-1, channels), w_qkv[:, :channels], preferred_element_type=jnp.float32
    )
    queries = queries.astype(jnp.bfloat16).reshape(view_frames, view_cells, channels)
    kv_weight = w_qkv[:, channels:]
    score_scale = channels ** (-0.5)
    outgoing = jnp.dot(normed.reshape(-1, channels), kv_weight, preferred_element_type=jnp.float32)
    outgoing = outgoing.astype(jnp.bfloat16).reshape(view_frames, view_cells, 2 * channels)
    portion = lax.all_gather(outgoing, "tile", axis=1, tiled=True)
    key_part = portion[:, :, :channels]
    value_part = portion[:, :, channels:]
    row_top = jnp.full((view_frames, view_cells, 1), -1e30, jnp.float32)
    scores = (
        jnp.einsum("fqc,fkc->fqk", queries, key_part, preferred_element_type=jnp.float32)
        * score_scale
    )
    new_top = jnp.maximum(row_top, jnp.max(scores, axis=2, keepdims=True))
    raised_f = jnp.exp(scores - new_top)
    row_total = jnp.sum(raised_f, axis=2, keepdims=True)
    weighted = jnp.einsum(
        "fqk,fkc->fqc",
        raised_f.astype(jnp.bfloat16),
        value_part,
        preferred_element_type=jnp.float32,
    )
    mixture_grid = (weighted / row_total).astype(jnp.bfloat16)
    mixture = mixture_grid.reshape(-1, channels)
    projected = jnp.dot(mixture, w_out, preferred_element_type=jnp.float32)
    attended = (features.reshape(-1, channels).astype(jnp.float32) + projected).astype(jnp.bfloat16)
    attended = attended.reshape(frames, row_count, col_count, channels)
    lifted = rms_scale(attended, conv_gain)
    activated = (lifted * jax.nn.sigmoid(lifted)).astype(jnp.bfloat16)
    earlier = from_behind(activated, "span", 1)
    stacked = jnp.concatenate([earlier, activated], axis=0)
    edged = extended(stacked, (("tile", 1),), 1)
    padded = jnp.pad(edged, ((0, 0), (0, 0), (1, 1), (0, 0)))
    clip_ends = jnp.cumsum(clip_lengths)
    position = lax.axis_index("span") * frames + jnp.arange(frames, dtype=jnp.int32)
    clip_start = jnp.sum(
        jnp.where(clip_ends[None, :] <= position[:, None], clip_lengths[None, :], 0), axis=1
    )
    summed = jnp.zeros((frames * cell_count, channels), jnp.float32)
    for t_tap in range(3):
        usable = position - (2 - t_tap) >= clip_start
        for r_tap in range(3):
            for c_tap in range(3):
                shifted = padded[
                    t_tap : t_tap + frames, r_tap : r_tap + row_count, c_tap : c_tap + col_count
                ]
                shifted = jnp.where(
                    usable[:, None, None, None], shifted, jnp.zeros((), shifted.dtype)
                )
                summed = summed + jnp.dot(
                    shifted.reshape(-1, channels),
                    w_conv[t_tap, r_tap, c_tap],
                    preferred_element_type=jnp.float32,
                )
    hidden = summed.astype(jnp.bfloat16).reshape(frames, row_count, col_count, channels)
    return (attended, hidden)


def solution(mesh):
    in_specs = (P(("grp", "span"), "tile", None, None), P("grp"), P(), P(), P(), P(), P())
    out_specs = (P(("grp", "span"), "tile", None, None), P(("grp", "span"), "tile", None, None))
    return jax.shard_map(
        on_device, mesh=mesh, in_specs=in_specs, out_specs=out_specs, check_vma=False
    )
```

```python
import functools

import jax
import jax.numpy as jnp
from jax import lax
from jax.experimental import pallas as pl
from jax.experimental.pallas import tpu as pltpu
from jax.sharding import PartitionSpec as P

eps = 1e-06
f32, bf16 = jnp.float32, jnp.bfloat16
LOG2E = 1.4426950408889634
VMEM = pl.BlockSpec(memory_space=pltpu.VMEM)
SMEM = pl.BlockSpec(memory_space=pltpu.SMEM)
ANY = pl.BlockSpec(memory_space=pl.ANY)


def from_behind(block, axis, distance):
    devices = range(lax.axis_size(axis))
    route = [(i - distance, i) for i in devices if i - distance in devices]
    return lax.ppermute(block, axis, route)


def rms_scale(values, gain_vec):
    as_float = values.astype(f32)
    return (
        as_float * lax.rsqrt(jnp.mean(as_float * as_float, axis=-1, keepdims=True) + eps) * gain_vec
    )


def dot32(a, b):
    return jnp.dot(a, b, preferred_element_type=f32)


def struct(shape, dtype=bf16):
    return jax.ShapeDtypeStruct(shape, dtype)


def call(kernel, name, out_shape, in_specs, scratch=(), limit=16, flops=0, size=1 << 20):
    outs = jax.tree.map(lambda _: VMEM, out_shape)
    cost = pl.CostEstimate(flops=int(flops), transcendentals=0, bytes_accessed=int(size))
    return pl.pallas_call(
        kernel,
        out_shape=out_shape,
        in_specs=in_specs,
        out_specs=outs,
        scratch_shapes=list(scratch),
        compiler_params=pltpu.CompilerParams(vmem_limit_bytes=limit << 20),
        cost_estimate=cost,
        name=name,
    )


def frame_route(spans, flip):
    route = []
    for tile in range(4):
        for span in range(spans):
            high, low, column, core = tile // 2, tile % 2, span // 2, span % 2
            there = (2 * core + (low ^ flip)) * spans + 2 * column + high
            route.append((tile * spans + span, there))
    return route


def load_small_kernel(w_qkv, w_out, gain, qkv_vm, out_vm, gain_vm, sem):
    copies = [
        pltpu.make_async_copy(w_qkv, qkv_vm, sem.at[0]),
        pltpu.make_async_copy(w_out, out_vm, sem.at[1]),
    ]
    for copy in copies:
        copy.start()
    gain_vm[...] = gain[...]
    for copy in copies:
        copy.wait()


def project_keys(block, gain_vec, w_qkv, out, place):
    cells, ch = block.shape
    normed = rms_scale(block[...], gain_vec).astype(bf16)
    out[place * cells : (place + 1) * cells, :] = dot32(normed, w_qkv[:, ch:]).astype(bf16)


def keys_kernel(own_a, other_a, own_b, gain, w_qkv, kv_out):
    gain_vec = gain[...].reshape(1, own_a.shape[1])
    for place, block in enumerate((own_a, other_a, own_b)):
        project_keys(block, gain_vec, w_qkv, kv_out, place)


def attend_rows(cols, source, kv_parts, gain_vec, w_qkv, w_out, att_out):
    ch = source.shape[1]
    for row in range(source.shape[0] // cols):
        part = slice(row * cols, (row + 1) * cols)
        feats = source[part, :]
        normed = rms_scale(feats, gain_vec).astype(bf16)
        queries = dot32(normed, w_qkv[:, :ch]).astype(bf16)
        scores = [
            lax.dot_general(
                queries, kv[:, :ch], (((1,), (1,)), ((), ())), preferred_element_type=f32
            )
            * (ch ** (-0.5) * LOG2E)
            for kv in kv_parts
        ]
        top = functools.reduce(
            jnp.maximum, [jnp.max(s, axis=1, keepdims=True) for s in scores]
        )
        raised = [jnp.exp2(s - top) for s in scores]
        total = sum(jnp.sum(r, axis=1, keepdims=True) for r in raised)
        mixed = sum(dot32(r.astype(bf16), kv[:, ch:]) for r, kv in zip(raised, kv_parts))
        mixture = (mixed / total).astype(bf16)
        att_out[part, :] = (feats.astype(f32) + dot32(mixture, w_out[...])).astype(bf16)


def attend_kernel(cols, other_b, own_a, kv_a, gain, w_qkv, w_out, kv_b, att_a):
    gain_vec = gain[...].reshape(1, own_a.shape[1])
    project_keys(other_b, gain_vec, w_qkv, kv_b, 0)
    attend_rows(cols, own_a, (kv_a, kv_b), gain_vec, w_qkv, w_out, att_a)


def attend_rest_kernel(cols, own_b, kv_a, kv_b, gain, w_qkv, w_out, att_b):
    gain_vec = gain[...].reshape(1, own_b.shape[1])
    attend_rows(cols, own_b, (kv_a, kv_b), gain_vec, w_qkv, w_out, att_b)


def load_kernel(_, w_hbm, w_vm, sem):
    ch = w_hbm.shape[-1]
    copies = [
        pltpu.make_async_copy(
            w_hbm.at[i, j, k],
            w_vm.at[i, j * ch : (j + 1) * ch, k * ch : (k + 1) * ch],
            sem.at[9 * i + 3 * j + k],
        )
        for i in range(3)
        for j in range(3)
        for k in range(3)
    ]
    for copy in copies:
        copy.start()
    for copy in copies:
        copy.wait()


def activate(cols, low, block, gain, act_out, pair_edge, mid_edge):
    lifted = rms_scale(block[...], gain[...].reshape(1, block.shape[1]))
    act = (lifted / (1.0 + jnp.exp(-lifted))).astype(bf16)
    act_out[...] = act

    @pl.when(low == 0)
    def _():
        pair_edge[...] = act[cols:, :]
        mid_edge[...] = act[:cols, :]

    @pl.when(low == 1)
    def _():
        pair_edge[...] = act[:cols, :]
        mid_edge[...] = act[cols:, :]


def activate_a_kernel(cols, tile_ref, got_a, gain, _, *outs):
    activate(cols, tile_ref[0] % 2, got_a, gain, *outs)


def activate_b_kernel(
    cols, tile_ref, got_a, got_b, act_a, gain, _, attended, active, pair_edge, mid_edge
):
    low = tile_ref[0] % 2
    activate(cols, low, got_b, gain, active.at[1 - low], pair_edge, mid_edge)
    active[low] = act_a[...]
    attended[low] = got_a[...]
    attended[1 - low] = got_b[...]


def usable_flag(clips, frame_at, tap):
    end = jnp.int32(0)
    start = jnp.int32(0)
    for i in range(clips.shape[0]):
        end = end + clips[i]
        start = start + jnp.where(end <= frame_at, clips[i], 0)
    return frame_at - (2 - tap) >= start


def shift_add(part, cols, ch):
    at = lax.broadcasted_iota(jnp.int32, (cols, ch), 0)
    left = jnp.where(at == 0, 0.0, pltpu.roll(part[:, :ch], 1, 0))
    right = jnp.where(at == cols - 1, 0.0, pltpu.roll(part[:, 2 * ch :], cols - 1, 0))
    return part[:, ch : 2 * ch] + left + right


def weigh(flag, block):
    return (block.astype(f32) * flag).astype(bf16)


def flags_of(clips, frame_at):
    return [
        [usable_flag(clips, frame_at + f, tap).astype(f32) for tap in range(3)] for f in range(2)
    ]


def edge_rows(tile_ref, pair_a, mid_a, pair_b, mid_b):
    odd = (tile_ref[0] % 2).astype(f32)

    def pick(if_odd, if_even):
        return if_odd[...].astype(f32) * odd + if_even[...].astype(f32) * (1.0 - odd)

    above = [pick(pair_a, mid_b), pick(pair_b, mid_a)]
    below = [pick(mid_a, pair_b), pick(mid_b, pair_a)]
    return above, below


def next_own_kernel(cols, span_ref, clips, mid, w, out):
    ch = mid.shape[-1]
    flag = flags_of(clips, (span_ref[0] + 1) * 2)
    first_row, second_row = slice(0, cols), slice(cols, 2 * cols)
    pair = [
        jnp.concatenate([mid[f, first_row, :], mid[f, second_row, :]], axis=1) for f in range(2)
    ]
    last = jnp.concatenate([weigh(flag[0][0], pair[0]), weigh(flag[1][0], pair[1])], axis=0)
    middle = weigh(flag[0][1], pair[1])
    for part, taps in ((first_row, slice(ch, 3 * ch)), (second_row, slice(0, 2 * ch))):
        far = dot32(last, w[0, taps])
        out[0, part, :] = shift_add(far[:cols] + dot32(middle, w[1, taps]), cols, ch)
        out[1, part, :] = shift_add(far[cols:], cols, ch)


def next_edge_kernel(
    cols, tile_ref, span_ref, clips, pair_a, mid_a, pair_b, mid_b, w, partial, out
):
    ch = w.shape[-1] // 3
    flag = flags_of(clips, (span_ref[0] + 1) * 2)
    above, below = edge_rows(tile_ref, pair_a, mid_a, pair_b, mid_b)
    for edge, part, taps in (
        (above, slice(0, cols), slice(0, ch)),
        (below, slice(cols, 2 * cols), slice(2 * ch, 3 * ch)),
    ):
        last = jnp.concatenate([edge[0] * flag[0][0], edge[1] * flag[1][0]], axis=0).astype(bf16)
        middle = (edge[1] * flag[0][1]).astype(bf16)
        far = dot32(last, w[0, taps])
        near = far[:cols] + dot32(middle, w[1, taps])
        for f, val in ((0, near), (1, far[cols:])):
            out[f, part, :] = (shift_add(val, cols, ch) + partial[f, part, :]).astype(bf16)


def own_kernel(cols, tile_ref, span_ref, clips, mid, pair_a, mid_a, pair_b, mid_b, w, out):
    ch = mid.shape[-1]
    above, below = edge_rows(tile_ref, pair_a, mid_a, pair_b, mid_b)
    wide = []
    for f in range(2):
        rows = [above[f].astype(bf16), mid[f, :cols, :], mid[f, cols:, :], below[f].astype(bf16)]
        wide += [jnp.concatenate(rows[r : r + 3], axis=1) for r in range(2)]
    here = dot32(jnp.concatenate(wide, axis=0), w[2])
    flag = usable_flag(clips, span_ref[0] * 2 + 1, 1).astype(f32)
    back = dot32(weigh(flag, jnp.concatenate(wide[:2], axis=0)), w[1])
    for r in range(2):
        part = slice(r * cols, (r + 1) * cols)
        out[0, part, :] = shift_add(here[part], cols, ch)
        after = here[(2 + r) * cols : (3 + r) * cols]
        out[1, part, :] = shift_add(after + back[part], cols, ch)


def on_device(features, clip_lengths, norm_gain, w_qkv, w_out, conv_gain, w_conv):
    frames, row_count, cols, ch = features.shape
    tiles, spans = lax.axis_size("tile"), lax.axis_size("span")
    if tiles != 4 or spans % 2 or frames != 2 or row_count != 2:
        return general(features, clip_lengths, norm_gain, w_qkv, w_out, conv_gain, w_conv)
    cells = row_count * cols
    both = ("tile", "span")
    tile = lax.axis_index("tile").astype(jnp.int32).reshape(1)
    span = lax.axis_index("span").astype(jnp.int32).reshape(1)
    other_core = [(i, i ^ 1) for i in range(spans)]
    route_a, route_b = frame_route(spans, 0), frame_route(spans, 1)
    low = tile[0] % 2
    x = features.reshape(frames, cells, ch)
    send_a = lax.dynamic_index_in_dim(x, low, 0, keepdims=False)
    send_b = lax.dynamic_index_in_dim(x, 1 - low, 0, keepdims=False)
    own_a = lax.ppermute(send_a, both, route_a)
    own_b = lax.ppermute(send_b, both, route_b)
    w_qkv, w_out, norm_gain = call(
        load_small_kernel,
        "load_small",
        (pltpu.VMEM(w_qkv.shape, bf16), pltpu.VMEM(w_out.shape, bf16), pltpu.VMEM((ch,), f32)),
        [ANY, ANY, VMEM],
        [pltpu.SemaphoreType.DMA((2,))],
        60,
    )(w_qkv, w_out, norm_gain)
    own_a, w_qkv = lax.optimization_barrier((own_a, w_qkv))
    other_a = lax.ppermute(own_a, "span", other_core)
    other_b = lax.ppermute(own_b, "span", other_core)
    kv_flops = 2 * 2 * cells * ch * 2 * ch
    row_flops = 2 * cells * ch * (2 * ch + 8 * cells)
    kv_a = call(keys_kernel, "keys", struct((3 * cells, 2 * ch)), [VMEM] * 5, flops=kv_flops)(
        own_a, other_a, own_b, norm_gain, w_qkv
    )
    kv_b, att_a = call(
        functools.partial(attend_kernel, cols),
        "attend",
        (struct((cells, 2 * ch)), struct((cells, ch))),
        [VMEM] * 6,
        flops=kv_flops + row_flops,
    )(other_b, own_a, kv_a, norm_gain, w_qkv, w_out)
    got_a = lax.ppermute(att_a, both, route_a)
    att_b = call(
        functools.partial(attend_rest_kernel, cols),
        "attend_rest",
        struct((cells, ch)),
        [VMEM] * 6,
        flops=3 * row_flops,
    )(own_b, kv_a, kv_b, norm_gain, w_qkv, w_out)
    got_b = lax.ppermute(att_b, both, route_b)
    pairs, middle = [(0, 1), (1, 0), (2, 3), (3, 2)], [(1, 2), (2, 1)]
    one, edge = struct((cells, ch)), struct((cols, ch))
    sums = struct((frames, cells, ch), f32)
    unit = 2 * cells * 9 * ch * ch
    where = (tile, span, clip_lengths)
    w_packed = call(
        load_kernel,
        "load_conv",
        struct((3, 3 * ch, 3 * ch)),
        [ANY, ANY],
        [pltpu.SemaphoreType.DMA((27,))],
        42,
        size=1 << 12,
    )(att_b, w_conv)
    act_a, pair_edge, mid_edge = call(
        functools.partial(activate_a_kernel, cols), "activate_a", (one, edge, edge), [SMEM, VMEM, VMEM, ANY]
    )(tile, got_a, conv_gain, w_packed)
    pair_a = lax.ppermute(pair_edge, "tile", pairs)
    mid_a = lax.ppermute(mid_edge, "tile", middle)
    attended, active, pair_edge, mid_edge = call(
        functools.partial(activate_b_kernel, cols),
        "activate_b",
        (struct((frames, cells, ch)), struct((frames, cells, ch)), edge, edge),
        [SMEM] + [VMEM] * 4 + [ANY],
    )(tile, got_a, got_b, act_a, conv_gain, w_packed)
    pair_b = lax.ppermute(pair_edge, "tile", pairs)
    mid_b = lax.ppermute(mid_edge, "tile", middle)
    edges = (pair_a, mid_a, pair_b, mid_b)
    started = call(
        functools.partial(next_own_kernel, cols),
        "next_own",
        sums,
        [SMEM] * 2 + [VMEM] * 2,
        flops=2 * unit,
    )(span, clip_lengths, active, w_packed)
    for_next = call(
        functools.partial(next_edge_kernel, cols),
        "next_edge",
        struct((frames, cells, ch)),
        [SMEM] * 3 + [VMEM] * 6,
        flops=unit,
    )(*where, *edges, w_packed, started)
    from_odd = lax.ppermute(for_next, "span", [(s, s + 1) for s in range(1, spans - 1, 2)])
    from_even = lax.ppermute(for_next, "span", [(s, s + 1) for s in range(0, spans, 2)])
    own = call(
        functools.partial(own_kernel, cols), "own", sums, [SMEM] * 3 + [VMEM] * 6, flops=3 * unit
    )(*where, active, *edges, w_packed)
    hidden = (own + from_odd.astype(f32) + from_even.astype(f32)).astype(bf16)
    shape = (frames, row_count, cols, ch)
    return attended.reshape(shape), hidden.reshape(shape)


def extended(x, sides, width):
    for axis, dim in sides:
        size, length = (lax.axis_size(axis), x.shape[dim])
        up = [(i, (i + 1) % size) for i in range(size - 1)]
        down = [(j, i) for i, j in up]
        last = lax.slice_in_dim(x, length - width, length, axis=dim)
        first = lax.slice_in_dim(x, 0, width, axis=dim)
        before = lax.ppermute(last, axis, up)
        after = lax.ppermute(first, axis, down)
        x = jnp.concatenate([before, x, after], axis=dim)
    return x


def general(features, clip_lengths, norm_gain, w_qkv, w_out, conv_gain, w_conv):
    frames, row_count, col_count, channels = features.shape
    cell_count = row_count * col_count
    normed_grid = rms_scale(features, norm_gain).astype(jnp.bfloat16)
    view_frames = normed_grid.shape[0]
    view_cells = normed_grid.shape[1] * normed_grid.shape[2]
    normed = normed_grid.reshape(view_frames, view_cells, channels)
    queries = jnp.dot(
        normed.reshape(-1, channels), w_qkv[:, :channels], preferred_element_type=jnp.float32
    )
    queries = queries.astype(jnp.bfloat16).reshape(view_frames, view_cells, channels)
    kv_weight = w_qkv[:, channels:]
    score_scale = channels ** (-0.5)
    outgoing = jnp.dot(normed.reshape(-1, channels), kv_weight, preferred_element_type=jnp.float32)
    outgoing = outgoing.astype(jnp.bfloat16).reshape(view_frames, view_cells, 2 * channels)
    portion = lax.all_gather(outgoing, "tile", axis=1, tiled=True)
    key_part = portion[:, :, :channels]
    value_part = portion[:, :, channels:]
    row_top = jnp.full((view_frames, view_cells, 1), -1e30, jnp.float32)
    scores = (
        jnp.einsum("fqc,fkc->fqk", queries, key_part, preferred_element_type=jnp.float32)
        * score_scale
    )
    new_top = jnp.maximum(row_top, jnp.max(scores, axis=2, keepdims=True))
    raised_f = jnp.exp(scores - new_top)
    row_total = jnp.sum(raised_f, axis=2, keepdims=True)
    weighted = jnp.einsum(
        "fqk,fkc->fqc",
        raised_f.astype(jnp.bfloat16),
        value_part,
        preferred_element_type=jnp.float32,
    )
    mixture_grid = (weighted / row_total).astype(jnp.bfloat16)
    mixture = mixture_grid.reshape(-1, channels)
    projected = jnp.dot(mixture, w_out, preferred_element_type=jnp.float32)
    attended = (features.reshape(-1, channels).astype(jnp.float32) + projected).astype(jnp.bfloat16)
    attended = attended.reshape(frames, row_count, col_count, channels)
    lifted = rms_scale(attended, conv_gain)
    activated = (lifted * jax.nn.sigmoid(lifted)).astype(jnp.bfloat16)
    earlier = from_behind(activated, "span", 1)
    stacked = jnp.concatenate([earlier, activated], axis=0)
    edged = extended(stacked, (("tile", 1),), 1)
    padded = jnp.pad(edged, ((0, 0), (0, 0), (1, 1), (0, 0)))
    clip_ends = jnp.cumsum(clip_lengths)
    position = lax.axis_index("span") * frames + jnp.arange(frames, dtype=jnp.int32)
    clip_start = jnp.sum(
        jnp.where(clip_ends[None, :] <= position[:, None], clip_lengths[None, :], 0), axis=1
    )
    summed = jnp.zeros((frames * cell_count, channels), jnp.float32)
    for t_tap in range(3):
        usable = position - (2 - t_tap) >= clip_start
        for r_tap in range(3):
            for c_tap in range(3):
                shifted = padded[
                    t_tap : t_tap + frames, r_tap : r_tap + row_count, c_tap : c_tap + col_count
                ]
                shifted = jnp.where(
                    usable[:, None, None, None], shifted, jnp.zeros((), shifted.dtype)
                )
                summed = summed + jnp.dot(
                    shifted.reshape(-1, channels),
                    w_conv[t_tap, r_tap, c_tap],
                    preferred_element_type=jnp.float32,
                )
    hidden = summed.astype(jnp.bfloat16).reshape(frames, row_count, col_count, channels)
    return (attended, hidden)


def solution(mesh):
    in_specs = (P(("grp", "span"), "tile", None, None), P("grp"), P(), P(), P(), P(), P())
    out_specs = (P(("grp", "span"), "tile", None, None), P(("grp", "span"), "tile", None, None))
    return jax.shard_map(
        on_device, mesh=mesh, in_specs=in_specs, out_specs=out_specs, check_vma=False
    )
```

```python
import functools

import jax
import jax.numpy as jnp
from jax import lax
from jax.experimental import pallas as pl
from jax.experimental.pallas import tpu as pltpu
from jax.sharding import PartitionSpec as P

eps = 1e-06
f32, bf16 = jnp.float32, jnp.bfloat16
LOG2E = 1.4426950408889634
VMEM = pl.BlockSpec(memory_space=pltpu.VMEM)
SMEM = pl.BlockSpec(memory_space=pltpu.SMEM)
ANY = pl.BlockSpec(memory_space=pl.ANY)


def from_behind(block, axis, distance):
    devices = range(lax.axis_size(axis))
    route = [(i - distance, i) for i in devices if i - distance in devices]
    return lax.ppermute(block, axis, route)


def rms_scale(values, gain_vec):
    as_float = values.astype(f32)
    return (
        as_float * lax.rsqrt(jnp.mean(as_float * as_float, axis=-1, keepdims=True) + eps) * gain_vec
    )


def dot32(a, b):
    return jnp.dot(a, b, preferred_element_type=f32)


def struct(shape, dtype=bf16):
    return jax.ShapeDtypeStruct(shape, dtype)


def call(kernel, name, out_shape, in_specs, scratch=(), limit=16, flops=0, size=1 << 20):
    outs = jax.tree.map(lambda _: VMEM, out_shape)
    cost = pl.CostEstimate(flops=int(flops), transcendentals=0, bytes_accessed=int(size))
    return pl.pallas_call(
        kernel,
        out_shape=out_shape,
        in_specs=in_specs,
        out_specs=outs,
        scratch_shapes=list(scratch),
        compiler_params=pltpu.CompilerParams(vmem_limit_bytes=limit << 20),
        cost_estimate=cost,
        name=name,
    )


def frame_route(spans, flip):
    route = []
    for tile in range(4):
        for span in range(spans):
            high, low, column, core = tile // 2, tile % 2, span // 2, span % 2
            there = (2 * core + (low ^ flip)) * spans + 2 * column + high
            route.append((tile * spans + span, there))
    return route


def pick_kernel(tile_ref, x_hbm, first, second, sem):
    low = tile_ref[0] % 2

    def move(a, b):
        copies = [
            pltpu.make_async_copy(x_hbm.at[a], first, sem.at[0]),
            pltpu.make_async_copy(x_hbm.at[b], second, sem.at[1]),
        ]
        for copy in copies:
            copy.start()
        for copy in copies:
            copy.wait()

    @pl.when(low == 0)
    def _():
        move(0, 1)

    @pl.when(low == 1)
    def _():
        move(1, 0)


def load_small_kernel(w_qkv, w_out, gain, qkv_vm, out_vm, gain_vm, sem):
    copies = [
        pltpu.make_async_copy(w_qkv, qkv_vm, sem.at[0]),
        pltpu.make_async_copy(w_out, out_vm, sem.at[1]),
    ]
    for copy in copies:
        copy.start()
    gain_vm[...] = gain[...]
    for copy in copies:
        copy.wait()


def project_keys(block, gain_vec, w_qkv, out, place):
    cells, ch = block.shape
    normed = rms_scale(block[...], gain_vec).astype(bf16)
    out[place * cells : (place + 1) * cells, :] = dot32(normed, w_qkv[:, ch:]).astype(bf16)


def keys_kernel(own_a, other_a, own_b, gain, w_qkv, kv_out):
    gain_vec = gain[...].reshape(1, own_a.shape[1])
    for place, block in enumerate((own_a, other_a, own_b)):
        project_keys(block, gain_vec, w_qkv, kv_out, place)


def attend_rows(source, kv_parts, gain_vec, w_qkv, w_out, att_out):
    ch = source.shape[1]
    feats = source[...]
    normed = rms_scale(feats, gain_vec).astype(bf16)
    queries = dot32(normed, w_qkv[:, :ch]).astype(bf16)
    scores = [
        lax.dot_general(
            queries, kv[:, :ch], (((1,), (1,)), ((), ())), preferred_element_type=f32
        )
        * (ch ** (-0.5) * LOG2E)
        for kv in kv_parts
    ]
    top = functools.reduce(jnp.maximum, [jnp.max(s, axis=1, keepdims=True) for s in scores])
    raised = [jnp.exp2(s - top) for s in scores]
    total = sum(jnp.sum(r, axis=1, keepdims=True) for r in raised)
    mixed = sum(dot32(r.astype(bf16), kv[:, ch:]) for r, kv in zip(raised, kv_parts))
    mixture = (mixed / total).astype(bf16)
    att_out[...] = (feats.astype(f32) + dot32(mixture, w_out[...])).astype(bf16)


def attend_kernel(other_b, own_a, kv_a, gain, w_qkv, w_out, kv_b, att_a):
    gain_vec = gain[...].reshape(1, own_a.shape[1])
    project_keys(other_b, gain_vec, w_qkv, kv_b, 0)
    attend_rows(own_a, (kv_a, kv_b), gain_vec, w_qkv, w_out, att_a)


def attend_rest_kernel(own_b, kv_a, kv_b, gain, w_qkv, w_out, att_b):
    gain_vec = gain[...].reshape(1, own_b.shape[1])
    attend_rows(own_b, (kv_a, kv_b), gain_vec, w_qkv, w_out, att_b)


def load_kernel(_, w_hbm, w_vm, sem):
    ch = w_hbm.shape[-1]
    copies = [
        pltpu.make_async_copy(
            w_hbm.at[i, j, k],
            w_vm.at[i, j * ch : (j + 1) * ch, k * ch : (k + 1) * ch],
            sem.at[9 * i + 3 * j + k],
        )
        for i in range(3)
        for j in range(3)
        for k in range(3)
    ]
    for copy in copies:
        copy.start()
    for copy in copies:
        copy.wait()


def activate(cols, low, block, gain, act_out, pair_edge, mid_edge):
    lifted = rms_scale(block[...], gain[...].reshape(1, block.shape[1]))
    act = (lifted / (1.0 + jnp.exp(-lifted))).astype(bf16)
    act_out[...] = act

    @pl.when(low == 0)
    def _():
        pair_edge[...] = act[cols:, :]
        mid_edge[...] = act[:cols, :]

    @pl.when(low == 1)
    def _():
        pair_edge[...] = act[:cols, :]
        mid_edge[...] = act[cols:, :]


def activate_a_kernel(cols, tile_ref, got_a, gain, _, *outs):
    activate(cols, tile_ref[0] % 2, got_a, gain, *outs)


def activate_b_kernel(cols, tile_ref, got_b, act_a, gain, _, active, pair_edge, mid_edge):
    low = tile_ref[0] % 2
    activate(cols, low, got_b, gain, active.at[1 - low], pair_edge, mid_edge)
    active[low] = act_a[...]


def usable_flag(clips, frame_at, tap):
    end = jnp.int32(0)
    start = jnp.int32(0)
    for i in range(clips.shape[0]):
        end = end + clips[i]
        start = start + jnp.where(end <= frame_at, clips[i], 0)
    return frame_at - (2 - tap) >= start


def shift_add(part, cols, ch):
    at = lax.broadcasted_iota(jnp.int32, (cols, ch), 0)
    left = jnp.where(at == 0, 0.0, pltpu.roll(part[:, :ch], 1, 0))
    right = jnp.where(at == cols - 1, 0.0, pltpu.roll(part[:, 2 * ch :], cols - 1, 0))
    return part[:, ch : 2 * ch] + left + right


def weigh(flag, block):
    return (block.astype(f32) * flag).astype(bf16)


def flags_of(clips, frame_at):
    return [
        [usable_flag(clips, frame_at + f, tap).astype(f32) for tap in range(3)] for f in range(2)
    ]


def edge_rows(tile_ref, pair_a, mid_a, pair_b, mid_b):
    odd = (tile_ref[0] % 2).astype(f32)

    def pick(if_odd, if_even):
        return if_odd[...].astype(f32) * odd + if_even[...].astype(f32) * (1.0 - odd)

    above = [pick(pair_a, mid_b), pick(pair_b, mid_a)]
    below = [pick(mid_a, pair_b), pick(mid_b, pair_a)]
    return above, below


def next_own_kernel(cols, span_ref, clips, mid, w, out):
    ch = mid.shape[-1]
    flag = flags_of(clips, (span_ref[0] + 1) * 2)
    first_row, second_row = slice(0, cols), slice(cols, 2 * cols)
    pair = [
        jnp.concatenate([mid[f, first_row, :], mid[f, second_row, :]], axis=1) for f in range(2)
    ]
    last = jnp.concatenate([weigh(flag[0][0], pair[0]), weigh(flag[1][0], pair[1])], axis=0)
    middle = weigh(flag[0][1], pair[1])
    for part, taps in ((first_row, slice(ch, 3 * ch)), (second_row, slice(0, 2 * ch))):
        far = dot32(last, w[0, taps])
        out[0, part, :] = shift_add(far[:cols] + dot32(middle, w[1, taps]), cols, ch)
        out[1, part, :] = shift_add(far[cols:], cols, ch)


def next_edge_kernel(
    cols, tile_ref, span_ref, clips, pair_a, mid_a, pair_b, mid_b, w, partial, out
):
    ch = w.shape[-1] // 3
    flag = flags_of(clips, (span_ref[0] + 1) * 2)
    above, below = edge_rows(tile_ref, pair_a, mid_a, pair_b, mid_b)
    for edge, part, taps in (
        (above, slice(0, cols), slice(0, ch)),
        (below, slice(cols, 2 * cols), slice(2 * ch, 3 * ch)),
    ):
        last = jnp.concatenate([edge[0] * flag[0][0], edge[1] * flag[1][0]], axis=0).astype(bf16)
        middle = (edge[1] * flag[0][1]).astype(bf16)
        far = dot32(last, w[0, taps])
        near = far[:cols] + dot32(middle, w[1, taps])
        for f, val in ((0, near), (1, far[cols:])):
            out[f, part, :] = (shift_add(val, cols, ch) + partial[f, part, :]).astype(bf16)


def own_kernel(
    cols,
    tile_ref,
    span_ref,
    clips,
    mid,
    pair_a,
    mid_a,
    pair_b,
    mid_b,
    w,
    got_a,
    got_b,
    out,
    attended,
):
    low = tile_ref[0] % 2
    attended[low] = got_a[...]
    attended[1 - low] = got_b[...]
    ch = mid.shape[-1]
    above, below = edge_rows(tile_ref, pair_a, mid_a, pair_b, mid_b)
    wide = []
    for f in range(2):
        rows = [above[f].astype(bf16), mid[f, :cols, :], mid[f, cols:, :], below[f].astype(bf16)]
        wide += [jnp.concatenate(rows[r : r + 3], axis=1) for r in range(2)]
    here = dot32(jnp.concatenate(wide, axis=0), w[2])
    flag = usable_flag(clips, span_ref[0] * 2 + 1, 1).astype(f32)
    back = dot32(weigh(flag, jnp.concatenate(wide[:2], axis=0)), w[1])
    for r in range(2):
        part = slice(r * cols, (r + 1) * cols)
        out[0, part, :] = shift_add(here[part], cols, ch)
        after = here[(2 + r) * cols : (3 + r) * cols]
        out[1, part, :] = shift_add(after + back[part], cols, ch)


def finish_kernel(span_ref, own, link_got, core_got, out):
    span = span_ref[0]

    @pl.when(span == 0)
    def _():
        out[...] = own[...].astype(bf16)

    @pl.when(span % 2 == 1)
    def _():
        out[...] = (own[...] + core_got[...].astype(f32)).astype(bf16)

    @pl.when(jnp.logical_and(span % 2 == 0, span > 0))
    def _():
        out[...] = (own[...] + link_got[...].astype(f32)).astype(bf16)


def on_device(features, clip_lengths, norm_gain, w_qkv, w_out, conv_gain, w_conv):
    frames, row_count, cols, ch = features.shape
    tiles, spans = lax.axis_size("tile"), lax.axis_size("span")
    if tiles != 4 or spans % 2 or frames != 2 or row_count != 2:
        return general(features, clip_lengths, norm_gain, w_qkv, w_out, conv_gain, w_conv)
    cells = row_count * cols
    both = ("tile", "span")
    tile = lax.axis_index("tile").astype(jnp.int32).reshape(1)
    span = lax.axis_index("span").astype(jnp.int32).reshape(1)
    other_core = [(i, i ^ 1) for i in range(spans)]
    route_a, route_b = frame_route(spans, 0), frame_route(spans, 1)
    x = features.reshape(frames, cells, ch)
    send_a, send_b = call(
        pick_kernel,
        "pick",
        (pltpu.VMEM((cells, ch), bf16), pltpu.VMEM((cells, ch), bf16)),
        [SMEM, ANY],
        [pltpu.SemaphoreType.DMA((2,))],
        62,
    )(tile, x)
    own_a = lax.ppermute(send_a, both, route_a)
    own_b = lax.ppermute(send_b, both, route_b)
    w_qkv, w_out, norm_gain = call(
        load_small_kernel,
        "load_small",
        (pltpu.VMEM(w_qkv.shape, bf16), pltpu.VMEM(w_out.shape, bf16), pltpu.VMEM((ch,), f32)),
        [ANY, ANY, VMEM],
        [pltpu.SemaphoreType.DMA((2,))],
        60,
    )(w_qkv, w_out, norm_gain)
    own_a, w_qkv = lax.optimization_barrier((own_a, w_qkv))
    other_a = lax.ppermute(own_a, "span", other_core)
    other_b = lax.ppermute(own_b, "span", other_core)
    kv_flops = 2 * 2 * cells * ch * 2 * ch
    row_flops = 2 * cells * ch * (2 * ch + 8 * cells)
    kv_a = call(keys_kernel, "keys", struct((3 * cells, 2 * ch)), [VMEM] * 5, flops=kv_flops)(
        own_a, other_a, own_b, norm_gain, w_qkv
    )
    kv_b, att_a = call(
        attend_kernel,
        "attend",
        (struct((cells, 2 * ch)), struct((cells, ch))),
        [VMEM] * 6,
        flops=kv_flops + row_flops,
    )(other_b, own_a, kv_a, norm_gain, w_qkv, w_out)
    got_a = lax.ppermute(att_a, both, route_a)
    att_b = call(
        attend_rest_kernel,
        "attend_rest",
        struct((cells, ch)),
        [VMEM] * 6,
        flops=3 * row_flops,
    )(own_b, kv_a, kv_b, norm_gain, w_qkv, w_out)
    got_b = lax.ppermute(att_b, both, route_b)
    pairs, middle = [(0, 1), (1, 0), (2, 3), (3, 2)], [(1, 2), (2, 1)]
    one, edge = struct((cells, ch)), struct((cols, ch))
    sums = struct((frames, cells, ch), f32)
    unit = 2 * cells * 9 * ch * ch
    where = (tile, span, clip_lengths)
    w_packed = call(
        load_kernel,
        "load_conv",
        struct((3, 3 * ch, 3 * ch)),
        [ANY, ANY],
        [pltpu.SemaphoreType.DMA((27,))],
        42,
        size=1 << 12,
    )(att_b, w_conv)
    act_a, pair_edge, mid_edge = call(
        functools.partial(activate_a_kernel, cols), "activate_a", (one, edge, edge), [SMEM, VMEM, VMEM, ANY]
    )(tile, got_a, conv_gain, w_packed)
    pair_a = lax.ppermute(pair_edge, "tile", pairs)
    mid_a = lax.ppermute(mid_edge, "tile", middle)
    active, pair_edge, mid_edge = call(
        functools.partial(activate_b_kernel, cols),
        "activate_b",
        (struct((frames, cells, ch)), edge, edge),
        [SMEM] + [VMEM] * 3 + [ANY],
    )(tile, got_b, act_a, conv_gain, w_packed)
    pair_b = lax.ppermute(pair_edge, "tile", pairs)
    mid_b = lax.ppermute(mid_edge, "tile", middle)
    edges = (pair_a, mid_a, pair_b, mid_b)
    started = call(
        functools.partial(next_own_kernel, cols),
        "next_own",
        sums,
        [SMEM] * 2 + [VMEM] * 2,
        flops=2 * unit,
    )(span, clip_lengths, active, w_packed)
    for_next = call(
        functools.partial(next_edge_kernel, cols),
        "next_edge",
        struct((frames, cells, ch)),
        [SMEM] * 3 + [VMEM] * 6,
        flops=unit,
    )(*where, *edges, w_packed, started)
    link = [(s + d, s + 1 - d) for s in range(1, spans - 1, 2) for d in range(2)]
    link_got = lax.ppermute(for_next, "span", link)
    core_got = lax.ppermute(for_next, "span", other_core)
    own, attended = call(
        functools.partial(own_kernel, cols),
        "own",
        (sums, struct((frames, cells, ch))),
        [SMEM] * 3 + [VMEM] * 8,
        flops=3 * unit,
    )(*where, active, *edges, w_packed, got_a, got_b)
    hidden = call(
        finish_kernel, "finish", struct((frames, cells, ch)), [SMEM] + [VMEM] * 3
    )(span, own, link_got, core_got)
    shape = (frames, row_count, cols, ch)
    return attended.reshape(shape), hidden.reshape(shape)


def extended(x, sides, width):
    for axis, dim in sides:
        size, length = (lax.axis_size(axis), x.shape[dim])
        up = [(i, (i + 1) % size) for i in range(size - 1)]
        down = [(j, i) for i, j in up]
        last = lax.slice_in_dim(x, length - width, length, axis=dim)
        first = lax.slice_in_dim(x, 0, width, axis=dim)
        before = lax.ppermute(last, axis, up)
        after = lax.ppermute(first, axis, down)
        x = jnp.concatenate([before, x, after], axis=dim)
    return x


def general(features, clip_lengths, norm_gain, w_qkv, w_out, conv_gain, w_conv):
    frames, row_count, col_count, channels = features.shape
    cell_count = row_count * col_count
    normed_grid = rms_scale(features, norm_gain).astype(jnp.bfloat16)
    view_frames = normed_grid.shape[0]
    view_cells = normed_grid.shape[1] * normed_grid.shape[2]
    normed = normed_grid.reshape(view_frames, view_cells, channels)
    queries = jnp.dot(
        normed.reshape(-1, channels), w_qkv[:, :channels], preferred_element_type=jnp.float32
    )
    queries = queries.astype(jnp.bfloat16).reshape(view_frames, view_cells, channels)
    kv_weight = w_qkv[:, channels:]
    score_scale = channels ** (-0.5)
    outgoing = jnp.dot(normed.reshape(-1, channels), kv_weight, preferred_element_type=jnp.float32)
    outgoing = outgoing.astype(jnp.bfloat16).reshape(view_frames, view_cells, 2 * channels)
    portion = lax.all_gather(outgoing, "tile", axis=1, tiled=True)
    key_part = portion[:, :, :channels]
    value_part = portion[:, :, channels:]
    row_top = jnp.full((view_frames, view_cells, 1), -1e30, jnp.float32)
    scores = (
        jnp.einsum("fqc,fkc->fqk", queries, key_part, preferred_element_type=jnp.float32)
        * score_scale
    )
    new_top = jnp.maximum(row_top, jnp.max(scores, axis=2, keepdims=True))
    raised_f = jnp.exp(scores - new_top)
    row_total = jnp.sum(raised_f, axis=2, keepdims=True)
    weighted = jnp.einsum(
        "fqk,fkc->fqc",
        raised_f.astype(jnp.bfloat16),
        value_part,
        preferred_element_type=jnp.float32,
    )
    mixture_grid = (weighted / row_total).astype(jnp.bfloat16)
    mixture = mixture_grid.reshape(-1, channels)
    projected = jnp.dot(mixture, w_out, preferred_element_type=jnp.float32)
    attended = (features.reshape(-1, channels).astype(jnp.float32) + projected).astype(jnp.bfloat16)
    attended = attended.reshape(frames, row_count, col_count, channels)
    lifted = rms_scale(attended, conv_gain)
    activated = (lifted * jax.nn.sigmoid(lifted)).astype(jnp.bfloat16)
    earlier = from_behind(activated, "span", 1)
    stacked = jnp.concatenate([earlier, activated], axis=0)
    edged = extended(stacked, (("tile", 1),), 1)
    padded = jnp.pad(edged, ((0, 0), (0, 0), (1, 1), (0, 0)))
    clip_ends = jnp.cumsum(clip_lengths)
    position = lax.axis_index("span") * frames + jnp.arange(frames, dtype=jnp.int32)
    clip_start = jnp.sum(
        jnp.where(clip_ends[None, :] <= position[:, None], clip_lengths[None, :], 0), axis=1
    )
    summed = jnp.zeros((frames * cell_count, channels), jnp.float32)
    for t_tap in range(3):
        usable = position - (2 - t_tap) >= clip_start
        for r_tap in range(3):
            for c_tap in range(3):
                shifted = padded[
                    t_tap : t_tap + frames, r_tap : r_tap + row_count, c_tap : c_tap + col_count
                ]
                shifted = jnp.where(
                    usable[:, None, None, None], shifted, jnp.zeros((), shifted.dtype)
                )
                summed = summed + jnp.dot(
                    shifted.reshape(-1, channels),
                    w_conv[t_tap, r_tap, c_tap],
                    preferred_element_type=jnp.float32,
                )
    hidden = summed.astype(jnp.bfloat16).reshape(frames, row_count, col_count, channels)
    return (attended, hidden)


def solution(mesh):
    in_specs = (P(("grp", "span"), "tile", None, None), P("grp"), P(), P(), P(), P(), P())
    out_specs = (P(("grp", "span"), "tile", None, None), P(("grp", "span"), "tile", None, None))
    return jax.shard_map(
        on_device, mesh=mesh, in_specs=in_specs, out_specs=out_specs, check_vma=False
    )
```

```python
import functools

import jax
import jax.numpy as jnp
from jax import lax
from jax.experimental import pallas as pl
from jax.experimental.pallas import tpu as pltpu
from jax.sharding import PartitionSpec as P

eps = 1e-06
f32, bf16 = jnp.float32, jnp.bfloat16
LOG2E = 1.4426950408889634
VMEM = pl.BlockSpec(memory_space=pltpu.VMEM)
SMEM = pl.BlockSpec(memory_space=pltpu.SMEM)
ANY = pl.BlockSpec(memory_space=pl.ANY)


def from_behind(block, axis, distance):
    devices = range(lax.axis_size(axis))
    route = [(i - distance, i) for i in devices if i - distance in devices]
    return lax.ppermute(block, axis, route)


def rms_scale(values, gain_vec):
    as_float = values.astype(f32)
    return (
        as_float * lax.rsqrt(jnp.mean(as_float * as_float, axis=-1, keepdims=True) + eps) * gain_vec
    )


def dot32(a, b):
    return jnp.dot(a, b, preferred_element_type=f32)


def struct(shape, dtype=bf16):
    return jax.ShapeDtypeStruct(shape, dtype)


def call(kernel, name, out_shape, in_specs, scratch=(), limit=16, flops=0, size=1 << 20):
    outs = jax.tree.map(lambda _: VMEM, out_shape)
    cost = pl.CostEstimate(flops=int(flops), transcendentals=0, bytes_accessed=int(size))
    return pl.pallas_call(
        kernel,
        out_shape=out_shape,
        in_specs=in_specs,
        out_specs=outs,
        scratch_shapes=list(scratch),
        compiler_params=pltpu.CompilerParams(vmem_limit_bytes=limit << 20),
        cost_estimate=cost,
        name=name,
    )


def frame_route(spans, flip):
    route = []
    for tile in range(4):
        for span in range(spans):
            high, low, column, core = tile // 2, tile % 2, span // 2, span % 2
            there = (2 * core + (low ^ flip)) * spans + 2 * column + high
            route.append((tile * spans + span, there))
    return route


def pick_kernel(tile_ref, x_hbm, first, second, sem):
    low = tile_ref[0] % 2

    def move(a, b):
        copies = [
            pltpu.make_async_copy(x_hbm.at[a], first, sem.at[0]),
            pltpu.make_async_copy(x_hbm.at[b], second, sem.at[1]),
        ]
        for copy in copies:
            copy.start()
        for copy in copies:
            copy.wait()

    @pl.when(low == 0)
    def _():
        move(0, 1)

    @pl.when(low == 1)
    def _():
        move(1, 0)


def load_small_kernel(w_qkv, w_out, gain, qkv_vm, out_vm, gain_vm, sem):
    copies = [
        pltpu.make_async_copy(w_qkv, qkv_vm, sem.at[0]),
        pltpu.make_async_copy(w_out, out_vm, sem.at[1]),
    ]
    for copy in copies:
        copy.start()
    gain_vm[...] = gain[...]
    for copy in copies:
        copy.wait()


def project_keys(block, gain_vec, w_qkv, out, place):
    cells, ch = block.shape
    normed = rms_scale(block[...], gain_vec).astype(bf16)
    out[place * cells : (place + 1) * cells, :] = dot32(normed, w_qkv[:, ch:]).astype(bf16)


def keys_kernel(own_a, other_a, own_b, gain, w_qkv, kv_out):
    gain_vec = gain[...].reshape(1, own_a.shape[1])
    for place, block in enumerate((own_a, other_a, own_b)):
        project_keys(block, gain_vec, w_qkv, kv_out, place)


def attend_rows(source, kv_parts, gain_vec, w_qkv, w_out, att_out):
    ch = source.shape[1]
    feats = source[...]
    normed = rms_scale(feats, gain_vec).astype(bf16)
    queries = dot32(normed, w_qkv[:, :ch]).astype(bf16)
    scores = [
        lax.dot_general(
            queries, kv[:, :ch], (((1,), (1,)), ((), ())), preferred_element_type=f32
        )
        * (ch ** (-0.5) * LOG2E)
        for kv in kv_parts
    ]
    top = functools.reduce(jnp.maximum, [jnp.max(s, axis=1, keepdims=True) for s in scores])
    raised = [jnp.exp2(s - top) for s in scores]
    total = sum(jnp.sum(r, axis=1, keepdims=True) for r in raised)
    mixed = sum(dot32(r.astype(bf16), kv[:, ch:]) for r, kv in zip(raised, kv_parts))
    mixture = (mixed / total).astype(bf16)
    att_out[...] = (feats.astype(f32) + dot32(mixture, w_out[...])).astype(bf16)


def attend_kernel(other_b, own_a, kv_a, gain, w_qkv, w_out, kv_b, att_a):
    gain_vec = gain[...].reshape(1, own_a.shape[1])
    project_keys(other_b, gain_vec, w_qkv, kv_b, 0)
    attend_rows(own_a, (kv_a, kv_b), gain_vec, w_qkv, w_out, att_a)


def attend_rest_kernel(own_b, kv_a, kv_b, gain, w_qkv, w_out, att_b):
    gain_vec = gain[...].reshape(1, own_b.shape[1])
    attend_rows(own_b, (kv_a, kv_b), gain_vec, w_qkv, w_out, att_b)


def load_kernel(_, w_hbm, w_vm, sem):
    ch = w_hbm.shape[-1]
    copies = [
        pltpu.make_async_copy(
            w_hbm.at[i, j, k],
            w_vm.at[i, j * ch : (j + 1) * ch, k * ch : (k + 1) * ch],
            sem.at[9 * i + 3 * j + k],
        )
        for i in range(3)
        for j in range(3)
        for k in range(3)
    ]
    for copy in copies:
        copy.start()
    for copy in copies:
        copy.wait()


def activate(cols, low, block, gain, act_out, mid_edge, pair_edge):
    lifted = rms_scale(block[...], gain[...].reshape(1, block.shape[1]))
    act = (lifted / (1.0 + jnp.exp(-lifted))).astype(bf16)
    act_out[...] = act

    @pl.when(low == 0)
    def _():
        pair_edge[...] = act[cols:, :]
        mid_edge[...] = act[:cols, :]

    @pl.when(low == 1)
    def _():
        pair_edge[...] = act[:cols, :]
        mid_edge[...] = act[cols:, :]


def activate_a_kernel(cols, tile_ref, got_a, gain, _, *outs):
    activate(cols, tile_ref[0] % 2, got_a, gain, *outs)


def activate_b_kernel(cols, tile_ref, got_b, act_a, gain, _, active, mid_edge, pair_edge):
    low = tile_ref[0] % 2
    activate(cols, low, got_b, gain, active.at[1 - low], mid_edge, pair_edge)
    active[low] = act_a[...]


def usable_flag(clips, frame_at, tap):
    end = jnp.int32(0)
    start = jnp.int32(0)
    for i in range(clips.shape[0]):
        end = end + clips[i]
        start = start + jnp.where(end <= frame_at, clips[i], 0)
    return frame_at - (2 - tap) >= start


def shift_add(part, cols, ch):
    at = lax.broadcasted_iota(jnp.int32, (cols, ch), 0)
    left = jnp.where(at == 0, 0.0, pltpu.roll(part[:, :ch], 1, 0))
    right = jnp.where(at == cols - 1, 0.0, pltpu.roll(part[:, 2 * ch :], cols - 1, 0))
    return part[:, ch : 2 * ch] + left + right


def weigh(flag, block):
    return (block.astype(f32) * flag).astype(bf16)


def flags_of(clips, frame_at):
    return [
        [usable_flag(clips, frame_at + f, tap).astype(f32) for tap in range(3)] for f in range(2)
    ]


def with_edges(tile_ref, pair_a, mid_a, pair_b, mid_b, body):
    odd = tile_ref[0] % 2 == 1

    @pl.when(odd)
    def _():
        body((pair_a, pair_b), (mid_a, mid_b))

    @pl.when(jnp.logical_not(odd))
    def _():
        body((mid_b, mid_a), (pair_b, pair_a))


def next_own_kernel(cols, span_ref, clips, mid, w, out):
    ch = mid.shape[-1]
    flag = flags_of(clips, (span_ref[0] + 1) * 2)
    first_row, second_row = slice(0, cols), slice(cols, 2 * cols)
    pair = [
        jnp.concatenate([mid[f, first_row, :], mid[f, second_row, :]], axis=1) for f in range(2)
    ]
    last = jnp.concatenate([weigh(flag[0][0], pair[0]), weigh(flag[1][0], pair[1])], axis=0)
    middle = weigh(flag[0][1], pair[1])
    for part, taps in ((first_row, slice(ch, 3 * ch)), (second_row, slice(0, 2 * ch))):
        far = dot32(last, w[0, taps])
        out[0, part, :] = shift_add(far[:cols] + dot32(middle, w[1, taps]), cols, ch)
        out[1, part, :] = shift_add(far[cols:], cols, ch)


def next_edge_kernel(
    cols, tile_ref, span_ref, clips, mid_a, pair_a, mid_b, pair_b, w, partial, out
):
    ch = w.shape[-1] // 3
    flag = flags_of(clips, (span_ref[0] + 1) * 2)

    def body(above, below):
        for edge, part, taps in (
            (above, slice(0, cols), slice(0, ch)),
            (below, slice(cols, 2 * cols), slice(2 * ch, 3 * ch)),
        ):
            first, second = edge[0][...], edge[1][...]
            last = jnp.concatenate([weigh(flag[0][0], first), weigh(flag[1][0], second)], axis=0)
            far = dot32(last, w[0, taps])
            near = far[:cols] + dot32(weigh(flag[0][1], second), w[1, taps])
            for f, val in ((0, near), (1, far[cols:])):
                out[f, part, :] = (shift_add(val, cols, ch) + partial[f, part, :]).astype(bf16)

    with_edges(tile_ref, pair_a, mid_a, pair_b, mid_b, body)


def own_kernel(
    cols,
    tile_ref,
    span_ref,
    clips,
    mid,
    mid_a,
    pair_a,
    mid_b,
    pair_b,
    w,
    got_a,
    got_b,
    out,
    attended,
):
    low = tile_ref[0] % 2
    attended[low] = got_a[...]
    attended[1 - low] = got_b[...]
    ch = mid.shape[-1]
    flag = usable_flag(clips, span_ref[0] * 2 + 1, 1).astype(f32)

    def body(above, below):
        wide = []
        for f in range(2):
            rows = [above[f][...], mid[f, :cols, :], mid[f, cols:, :], below[f][...]]
            wide += [jnp.concatenate(rows[r : r + 3], axis=1) for r in range(2)]
        here = dot32(jnp.concatenate(wide, axis=0), w[2])
        back = dot32(weigh(flag, jnp.concatenate(wide[:2], axis=0)), w[1])
        for r in range(2):
            part = slice(r * cols, (r + 1) * cols)
            out[0, part, :] = shift_add(here[part], cols, ch)
            after = here[(2 + r) * cols : (3 + r) * cols]
            out[1, part, :] = shift_add(after + back[part], cols, ch)

    with_edges(tile_ref, pair_a, mid_a, pair_b, mid_b, body)


def finish_kernel(span_ref, own, link_got, core_got, out):
    span = span_ref[0]

    @pl.when(span == 0)
    def _():
        out[...] = own[...].astype(bf16)

    @pl.when(span % 2 == 1)
    def _():
        out[...] = (own[...] + core_got[...].astype(f32)).astype(bf16)

    @pl.when(jnp.logical_and(span % 2 == 0, span > 0))
    def _():
        out[...] = (own[...] + link_got[...].astype(f32)).astype(bf16)


def on_device(features, clip_lengths, norm_gain, w_qkv, w_out, conv_gain, w_conv):
    frames, row_count, cols, ch = features.shape
    tiles, spans = lax.axis_size("tile"), lax.axis_size("span")
    if tiles != 4 or spans % 2 or frames != 2 or row_count != 2:
        return general(features, clip_lengths, norm_gain, w_qkv, w_out, conv_gain, w_conv)
    cells = row_count * cols
    both = ("tile", "span")
    tile = lax.axis_index("tile").astype(jnp.int32).reshape(1)
    span = lax.axis_index("span").astype(jnp.int32).reshape(1)
    other_core = [(i, i ^ 1) for i in range(spans)]
    route_a, route_b = frame_route(spans, 0), frame_route(spans, 1)
    x = features.reshape(frames, cells, ch)
    send_a, send_b = call(
        pick_kernel,
        "pick",
        (pltpu.VMEM((cells, ch), bf16), pltpu.VMEM((cells, ch), bf16)),
        [SMEM, ANY],
        [pltpu.SemaphoreType.DMA((2,))],
        62,
    )(tile, x)
    own_a = lax.ppermute(send_a, both, route_a)
    own_b = lax.ppermute(send_b, both, route_b)
    w_qkv, w_out, norm_gain = call(
        load_small_kernel,
        "load_small",
        (pltpu.VMEM(w_qkv.shape, bf16), pltpu.VMEM(w_out.shape, bf16), pltpu.VMEM((ch,), f32)),
        [ANY, ANY, VMEM],
        [pltpu.SemaphoreType.DMA((2,))],
        60,
    )(w_qkv, w_out, norm_gain)
    own_a, w_qkv = lax.optimization_barrier((own_a, w_qkv))
    other_a = lax.ppermute(own_a, "span", other_core)
    other_b = lax.ppermute(own_b, "span", other_core)
    kv_flops = 2 * 2 * cells * ch * 2 * ch
    row_flops = 2 * cells * ch * (2 * ch + 8 * cells)
    kv_a = call(keys_kernel, "keys", struct((3 * cells, 2 * ch)), [VMEM] * 5, flops=kv_flops)(
        own_a, other_a, own_b, norm_gain, w_qkv
    )
    kv_b, att_a = call(
        attend_kernel,
        "attend",
        (struct((cells, 2 * ch)), struct((cells, ch))),
        [VMEM] * 6,
        flops=kv_flops + row_flops,
    )(other_b, own_a, kv_a, norm_gain, w_qkv, w_out)
    got_a = lax.ppermute(att_a, both, route_a)
    att_b = call(
        attend_rest_kernel,
        "attend_rest",
        struct((cells, ch)),
        [VMEM] * 6,
        flops=3 * row_flops,
    )(own_b, kv_a, kv_b, norm_gain, w_qkv, w_out)
    got_b = lax.ppermute(att_b, both, route_b)
    pairs, middle = [(0, 1), (1, 0), (2, 3), (3, 2)], [(1, 2), (2, 1)]
    one, edge = struct((cells, ch)), struct((cols, ch))
    sums = struct((frames, cells, ch), f32)
    unit = 2 * cells * 9 * ch * ch
    where = (tile, span, clip_lengths)
    w_packed = call(
        load_kernel,
        "load_conv",
        struct((3, 3 * ch, 3 * ch)),
        [ANY, ANY],
        [pltpu.SemaphoreType.DMA((27,))],
        42,
        size=1 << 12,
    )(att_b, w_conv)
    act_a, mid_edge, pair_edge = call(
        functools.partial(activate_a_kernel, cols), "activate_a", (one, edge, edge), [SMEM, VMEM, VMEM, ANY]
    )(tile, got_a, conv_gain, w_packed)
    mid_a = lax.ppermute(mid_edge, "tile", middle)
    pair_a = lax.ppermute(pair_edge, "tile", pairs)
    active, mid_edge, pair_edge = call(
        functools.partial(activate_b_kernel, cols),
        "activate_b",
        (struct((frames, cells, ch)), edge, edge),
        [SMEM] + [VMEM] * 3 + [ANY],
    )(tile, got_b, act_a, conv_gain, w_packed)
    mid_b = lax.ppermute(mid_edge, "tile", middle)
    pair_b = lax.ppermute(pair_edge, "tile", pairs)
    edges = (mid_a, pair_a, mid_b, pair_b)
    started = call(
        functools.partial(next_own_kernel, cols),
        "next_own",
        sums,
        [SMEM] * 2 + [VMEM] * 2,
        flops=2 * unit,
    )(span, clip_lengths, active, w_packed)
    for_next = call(
        functools.partial(next_edge_kernel, cols),
        "next_edge",
        struct((frames, cells, ch)),
        [SMEM] * 3 + [VMEM] * 6,
        flops=unit,
    )(*where, *edges, w_packed, started)
    link = [(s + d, s + 1 - d) for s in range(1, spans - 1, 2) for d in range(2)]
    link_got = lax.ppermute(for_next, "span", link)
    core_got = lax.ppermute(for_next, "span", other_core)
    own, attended = call(
        functools.partial(own_kernel, cols),
        "own",
        (sums, struct((frames, cells, ch))),
        [SMEM] * 3 + [VMEM] * 8,
        flops=3 * unit,
    )(*where, active, *edges, w_packed, got_a, got_b)
    hidden = call(
        finish_kernel, "finish", struct((frames, cells, ch)), [SMEM] + [VMEM] * 3
    )(span, own, link_got, core_got)
    shape = (frames, row_count, cols, ch)
    return attended.reshape(shape), hidden.reshape(shape)


def extended(x, sides, width):
    for axis, dim in sides:
        size, length = (lax.axis_size(axis), x.shape[dim])
        up = [(i, (i + 1) % size) for i in range(size - 1)]
        down = [(j, i) for i, j in up]
        last = lax.slice_in_dim(x, length - width, length, axis=dim)
        first = lax.slice_in_dim(x, 0, width, axis=dim)
        before = lax.ppermute(last, axis, up)
        after = lax.ppermute(first, axis, down)
        x = jnp.concatenate([before, x, after], axis=dim)
    return x


def general(features, clip_lengths, norm_gain, w_qkv, w_out, conv_gain, w_conv):
    frames, row_count, col_count, channels = features.shape
    cell_count = row_count * col_count
    normed_grid = rms_scale(features, norm_gain).astype(jnp.bfloat16)
    view_frames = normed_grid.shape[0]
    view_cells = normed_grid.shape[1] * normed_grid.shape[2]
    normed = normed_grid.reshape(view_frames, view_cells, channels)
    queries = jnp.dot(
        normed.reshape(-1, channels), w_qkv[:, :channels], preferred_element_type=jnp.float32
    )
    queries = queries.astype(jnp.bfloat16).reshape(view_frames, view_cells, channels)
    kv_weight = w_qkv[:, channels:]
    score_scale = channels ** (-0.5)
    outgoing = jnp.dot(normed.reshape(-1, channels), kv_weight, preferred_element_type=jnp.float32)
    outgoing = outgoing.astype(jnp.bfloat16).reshape(view_frames, view_cells, 2 * channels)
    portion = lax.all_gather(outgoing, "tile", axis=1, tiled=True)
    key_part = portion[:, :, :channels]
    value_part = portion[:, :, channels:]
    row_top = jnp.full((view_frames, view_cells, 1), -1e30, jnp.float32)
    scores = (
        jnp.einsum("fqc,fkc->fqk", queries, key_part, preferred_element_type=jnp.float32)
        * score_scale
    )
    new_top = jnp.maximum(row_top, jnp.max(scores, axis=2, keepdims=True))
    raised_f = jnp.exp(scores - new_top)
    row_total = jnp.sum(raised_f, axis=2, keepdims=True)
    weighted = jnp.einsum(
        "fqk,fkc->fqc",
        raised_f.astype(jnp.bfloat16),
        value_part,
        preferred_element_type=jnp.float32,
    )
    mixture_grid = (weighted / row_total).astype(jnp.bfloat16)
    mixture = mixture_grid.reshape(-1, channels)
    projected = jnp.dot(mixture, w_out, preferred_element_type=jnp.float32)
    attended = (features.reshape(-1, channels).astype(jnp.float32) + projected).astype(jnp.bfloat16)
    attended = attended.reshape(frames, row_count, col_count, channels)
    lifted = rms_scale(attended, conv_gain)
    activated = (lifted * jax.nn.sigmoid(lifted)).astype(jnp.bfloat16)
    earlier = from_behind(activated, "span", 1)
    stacked = jnp.concatenate([earlier, activated], axis=0)
    edged = extended(stacked, (("tile", 1),), 1)
    padded = jnp.pad(edged, ((0, 0), (0, 0), (1, 1), (0, 0)))
    clip_ends = jnp.cumsum(clip_lengths)
    position = lax.axis_index("span") * frames + jnp.arange(frames, dtype=jnp.int32)
    clip_start = jnp.sum(
        jnp.where(clip_ends[None, :] <= position[:, None], clip_lengths[None, :], 0), axis=1
    )
    summed = jnp.zeros((frames * cell_count, channels), jnp.float32)
    for t_tap in range(3):
        usable = position - (2 - t_tap) >= clip_start
        for r_tap in range(3):
            for c_tap in range(3):
                shifted = padded[
                    t_tap : t_tap + frames, r_tap : r_tap + row_count, c_tap : c_tap + col_count
                ]
                shifted = jnp.where(
                    usable[:, None, None, None], shifted, jnp.zeros((), shifted.dtype)
                )
                summed = summed + jnp.dot(
                    shifted.reshape(-1, channels),
                    w_conv[t_tap, r_tap, c_tap],
                    preferred_element_type=jnp.float32,
                )
    hidden = summed.astype(jnp.bfloat16).reshape(frames, row_count, col_count, channels)
    return (attended, hidden)


def solution(mesh):
    in_specs = (P(("grp", "span"), "tile", None, None), P("grp"), P(), P(), P(), P(), P())
    out_specs = (P(("grp", "span"), "tile", None, None), P(("grp", "span"), "tile", None, None))
    return jax.shard_map(
        on_device, mesh=mesh, in_specs=in_specs, out_specs=out_specs, check_vma=False
    )
```

```python
import functools

import jax
import jax.numpy as jnp
from jax import lax
from jax.experimental import pallas as pl
from jax.experimental.pallas import tpu as pltpu
from jax.sharding import PartitionSpec as P

eps = 1e-06
f32, bf16 = jnp.float32, jnp.bfloat16
LOG2E = 1.4426950408889634
VMEM = pl.BlockSpec(memory_space=pltpu.VMEM)
SMEM = pl.BlockSpec(memory_space=pltpu.SMEM)
ANY = pl.BlockSpec(memory_space=pl.ANY)


def from_behind(block, axis, distance):
    devices = range(lax.axis_size(axis))
    route = [(i - distance, i) for i in devices if i - distance in devices]
    return lax.ppermute(block, axis, route)


def rms_scale(values, gain_vec):
    as_float = values.astype(f32)
    return (
        as_float * lax.rsqrt(jnp.mean(as_float * as_float, axis=-1, keepdims=True) + eps) * gain_vec
    )


def dot32(a, b):
    return jnp.dot(a, b, preferred_element_type=f32)


def struct(shape, dtype=bf16):
    return jax.ShapeDtypeStruct(shape, dtype)


def call(kernel, name, out_shape, in_specs, scratch=(), limit=16, flops=0, size=1 << 20):
    outs = jax.tree.map(lambda _: VMEM, out_shape)
    cost = pl.CostEstimate(flops=int(flops), transcendentals=0, bytes_accessed=int(size))
    return pl.pallas_call(
        kernel,
        out_shape=out_shape,
        in_specs=in_specs,
        out_specs=outs,
        scratch_shapes=list(scratch),
        compiler_params=pltpu.CompilerParams(vmem_limit_bytes=limit << 20),
        cost_estimate=cost,
        name=name,
    )


def frame_route(spans, flip):
    route = []
    for tile in range(4):
        for span in range(spans):
            high, low, column, core = tile // 2, tile % 2, span // 2, span % 2
            there = (2 * core + (low ^ flip)) * spans + 2 * column + high
            route.append((tile * spans + span, there))
    return route


def pick_kernel(tile_ref, x_hbm, first, second, sem):
    low = tile_ref[0] % 2

    def move(a, b):
        copies = [
            pltpu.make_async_copy(x_hbm.at[a], first, sem.at[0]),
            pltpu.make_async_copy(x_hbm.at[b], second, sem.at[1]),
        ]
        for copy in copies:
            copy.start()
        for copy in copies:
            copy.wait()

    @pl.when(low == 0)
    def _():
        move(0, 1)

    @pl.when(low == 1)
    def _():
        move(1, 0)


def load_small_kernel(w_qkv, w_out, gain, qkv_vm, out_vm, gain_vm, sem):
    copies = [
        pltpu.make_async_copy(w_qkv, qkv_vm, sem.at[0]),
        pltpu.make_async_copy(w_out, out_vm, sem.at[1]),
    ]
    for copy in copies:
        copy.start()
    gain_vm[...] = gain[...]
    for copy in copies:
        copy.wait()


def project_keys(block, gain_vec, w_qkv, out, place):
    cells, ch = block.shape
    normed = rms_scale(block[...], gain_vec).astype(bf16)
    out[place * cells : (place + 1) * cells, :] = dot32(normed, w_qkv[:, ch:]).astype(bf16)


def keys_kernel(own_a, other_a, own_b, gain, w_qkv, kv_out):
    gain_vec = gain[...].reshape(1, own_a.shape[1])
    for place, block in enumerate((own_a, other_a, own_b)):
        project_keys(block, gain_vec, w_qkv, kv_out, place)


def attend_rows(source, kv_parts, gain_vec, w_qkv, w_out, att_out):
    ch = source.shape[1]
    feats = source[...]
    normed = rms_scale(feats, gain_vec).astype(bf16)
    queries = dot32(normed, w_qkv[:, :ch]).astype(bf16)
    scores = [
        lax.dot_general(
            queries, kv[:, :ch], (((1,), (1,)), ((), ())), preferred_element_type=f32
        )
        * (ch ** (-0.5) * LOG2E)
        for kv in kv_parts
    ]
    top = functools.reduce(jnp.maximum, [jnp.max(s, axis=1, keepdims=True) for s in scores])
    raised = [jnp.exp2(s - top) for s in scores]
    total = sum(jnp.sum(r, axis=1, keepdims=True) for r in raised)
    mixed = sum(dot32(r.astype(bf16), kv[:, ch:]) for r, kv in zip(raised, kv_parts))
    mixture = (mixed / total).astype(bf16)
    att_out[...] = (feats.astype(f32) + dot32(mixture, w_out[...])).astype(bf16)


def attend_kernel(other_b, own_a, kv_a, gain, w_qkv, w_out, kv_b, att_a):
    gain_vec = gain[...].reshape(1, own_a.shape[1])
    project_keys(other_b, gain_vec, w_qkv, kv_b, 0)
    attend_rows(own_a, (kv_a, kv_b), gain_vec, w_qkv, w_out, att_a)


def attend_rest_kernel(own_b, kv_a, kv_b, gain, w_qkv, w_out, att_b):
    gain_vec = gain[...].reshape(1, own_b.shape[1])
    attend_rows(own_b, (kv_a, kv_b), gain_vec, w_qkv, w_out, att_b)


def load_kernel(_, w_hbm, w_vm, sem):
    ch = w_hbm.shape[-1]
    copies = [
        pltpu.make_async_copy(
            w_hbm.at[i, j, k],
            w_vm.at[i, j * ch : (j + 1) * ch, k * ch : (k + 1) * ch],
            sem.at[9 * i + 3 * j + k],
        )
        for i in range(3)
        for j in range(3)
        for k in range(3)
    ]
    for copy in copies:
        copy.start()
    for copy in copies:
        copy.wait()


def activate(cols, low, block, gain, act_out, pair_edge, mid_edge):
    lifted = rms_scale(block[...], gain[...].reshape(1, block.shape[1]))
    act = (lifted / (1.0 + jnp.exp(-lifted))).astype(bf16)
    act_out[...] = act

    @pl.when(low == 0)
    def _():
        pair_edge[...] = act[cols:, :]
        mid_edge[...] = act[:cols, :]

    @pl.when(low == 1)
    def _():
        pair_edge[...] = act[:cols, :]
        mid_edge[...] = act[cols:, :]


def activate_a_kernel(cols, tile_ref, got_a, gain, _, *outs):
    activate(cols, tile_ref[0] % 2, got_a, gain, *outs)


def activate_b_kernel(cols, tile_ref, got_b, act_a, gain, _, active, pair_edge, mid_edge):
    low = tile_ref[0] % 2
    activate(cols, low, got_b, gain, active.at[1 - low], pair_edge, mid_edge)
    active[low] = act_a[...]


def usable_flag(clips, frame_at, tap):
    end = jnp.int32(0)
    start = jnp.int32(0)
    for i in range(clips.shape[0]):
        end = end + clips[i]
        start = start + jnp.where(end <= frame_at, clips[i], 0)
    return frame_at - (2 - tap) >= start


def shift_add(part, cols, ch):
    at = lax.broadcasted_iota(jnp.int32, (cols, ch), 0)
    left = jnp.where(at == 0, 0.0, pltpu.roll(part[:, :ch], 1, 0))
    right = jnp.where(at == cols - 1, 0.0, pltpu.roll(part[:, 2 * ch :], cols - 1, 0))
    return part[:, ch : 2 * ch] + left + right


def weigh(flag, block):
    return (block.astype(f32) * flag).astype(bf16)


def flags_of(clips, frame_at):
    return [
        [usable_flag(clips, frame_at + f, tap).astype(f32) for tap in range(3)] for f in range(2)
    ]


def edge_rows(tile_ref, pair_a, mid_a, pair_b, mid_b):
    odd = (tile_ref[0] % 2).astype(f32)

    def pick(if_odd, if_even):
        return if_odd[...].astype(f32) * odd + if_even[...].astype(f32) * (1.0 - odd)

    above = [pick(pair_a, mid_b), pick(pair_b, mid_a)]
    below = [pick(mid_a, pair_b), pick(mid_b, pair_a)]
    return above, below


def next_own_kernel(cols, span_ref, clips, mid, w, out):
    ch = mid.shape[-1]
    flag = flags_of(clips, (span_ref[0] + 1) * 2)
    first_row, second_row = slice(0, cols), slice(cols, 2 * cols)
    pair = [
        jnp.concatenate([mid[f, first_row, :], mid[f, second_row, :]], axis=1) for f in range(2)
    ]
    last = jnp.concatenate([weigh(flag[0][0], pair[0]), weigh(flag[1][0], pair[1])], axis=0)
    middle = weigh(flag[0][1], pair[1])
    for part, taps in ((first_row, slice(ch, 3 * ch)), (second_row, slice(0, 2 * ch))):
        far = dot32(last, w[0, taps])
        out[0, part, :] = shift_add(far[:cols] + dot32(middle, w[1, taps]), cols, ch)
        out[1, part, :] = shift_add(far[cols:], cols, ch)


def edge_part(cols, flag, first, second, above, w, partial, put):
    ch = w.shape[-1] // 3
    part = slice(0, cols) if above else slice(cols, 2 * cols)
    taps = slice(0, ch) if above else slice(2 * ch, 3 * ch)
    last = jnp.concatenate([weigh(flag[0][0], first), weigh(flag[1][0], second)], axis=0)
    far = dot32(last, w[0, taps])
    near = far[:cols] + dot32(weigh(flag[0][1], second), w[1, taps])
    for f, val in ((0, near), (1, far[cols:])):
        put(f, part, (shift_add(val, cols, ch) + partial[f, part, :]).astype(bf16))


def pair_edge_kernel(cols, tile_ref, span_ref, clips, pair_a, pair_b, w, partial, out):
    flag = flags_of(clips, (span_ref[0] + 1) * 2)

    def put(f, part, val):
        out[f] = val

    @pl.when(tile_ref[0] % 2 == 1)
    def _():
        edge_part(cols, flag, pair_a[...], pair_b[...], True, w, partial, put)

    @pl.when(tile_ref[0] % 2 == 0)
    def _():
        edge_part(cols, flag, pair_b[...], pair_a[...], False, w, partial, put)


def mid_edge_kernel(cols, tile_ref, span_ref, clips, mid_a, mid_b, w, partial, pair_rows, out):
    flag = flags_of(clips, (span_ref[0] + 1) * 2)

    def put(f, part, val):
        out[f, part, :] = val

    @pl.when(tile_ref[0] % 2 == 1)
    def _():
        out[:, :cols, :] = pair_rows[...]
        edge_part(cols, flag, mid_a[...], mid_b[...], False, w, partial, put)

    @pl.when(tile_ref[0] % 2 == 0)
    def _():
        out[:, cols:, :] = pair_rows[...]
        edge_part(cols, flag, mid_b[...], mid_a[...], True, w, partial, put)


def own_kernel(
    cols,
    tile_ref,
    span_ref,
    clips,
    mid,
    pair_a,
    mid_a,
    pair_b,
    mid_b,
    w,
    got_a,
    got_b,
    out,
    attended,
):
    low = tile_ref[0] % 2
    attended[low] = got_a[...]
    attended[1 - low] = got_b[...]
    ch = mid.shape[-1]
    above, below = edge_rows(tile_ref, pair_a, mid_a, pair_b, mid_b)
    wide = []
    for f in range(2):
        rows = [above[f].astype(bf16), mid[f, :cols, :], mid[f, cols:, :], below[f].astype(bf16)]
        wide += [jnp.concatenate(rows[r : r + 3], axis=1) for r in range(2)]
    here = dot32(jnp.concatenate(wide, axis=0), w[2])
    flag = usable_flag(clips, span_ref[0] * 2 + 1, 1).astype(f32)
    back = dot32(weigh(flag, jnp.concatenate(wide[:2], axis=0)), w[1])
    for r in range(2):
        part = slice(r * cols, (r + 1) * cols)
        out[0, part, :] = shift_add(here[part], cols, ch)
        after = here[(2 + r) * cols : (3 + r) * cols]
        out[1, part, :] = shift_add(after + back[part], cols, ch)


def finish_kernel(cols, span_ref, own, link_got, core_got, out_hbm, held, sem):
    span = span_ref[0]
    copies = []
    for f in range(2):
        for r in range(2):
            part = slice(r * cols, (r + 1) * cols)

            @pl.when(span == 0)
            def _(f=f, part=part):
                held[f, part, :] = own[f, part, :].astype(bf16)

            @pl.when(span % 2 == 1)
            def _(f=f, part=part):
                total = own[f, part, :] + core_got[f, part, :].astype(f32)
                held[f, part, :] = total.astype(bf16)

            @pl.when(jnp.logical_and(span % 2 == 0, span > 0))
            def _(f=f, part=part):
                total = own[f, part, :] + link_got[f, part, :].astype(f32)
                held[f, part, :] = total.astype(bf16)

            copy = pltpu.make_async_copy(
                held.at[f, part], out_hbm.at[f, part], sem.at[2 * f + r]
            )
            copy.start()
            copies.append(copy)
    for copy in copies:
        copy.wait()


def on_device(features, clip_lengths, norm_gain, w_qkv, w_out, conv_gain, w_conv):
    frames, row_count, cols, ch = features.shape
    tiles, spans = lax.axis_size("tile"), lax.axis_size("span")
    if tiles != 4 or spans % 2 or frames != 2 or row_count != 2:
        return general(features, clip_lengths, norm_gain, w_qkv, w_out, conv_gain, w_conv)
    cells = row_count * cols
    both = ("tile", "span")
    tile = lax.axis_index("tile").astype(jnp.int32).reshape(1)
    span = lax.axis_index("span").astype(jnp.int32).reshape(1)
    other_core = [(i, i ^ 1) for i in range(spans)]
    route_a, route_b = frame_route(spans, 0), frame_route(spans, 1)
    x = features.reshape(frames, cells, ch)
    send_a, send_b = call(
        pick_kernel,
        "pick",
        (pltpu.VMEM((cells, ch), bf16), pltpu.VMEM((cells, ch), bf16)),
        [SMEM, ANY],
        [pltpu.SemaphoreType.DMA((2,))],
        62,
    )(tile, x)
    own_a = lax.ppermute(send_a, both, route_a)
    own_b = lax.ppermute(send_b, both, route_b)
    w_qkv, w_out, norm_gain = call(
        load_small_kernel,
        "load_small",
        (pltpu.VMEM(w_qkv.shape, bf16), pltpu.VMEM(w_out.shape, bf16), pltpu.VMEM((ch,), f32)),
        [ANY, ANY, VMEM],
        [pltpu.SemaphoreType.DMA((2,))],
        60,
    )(w_qkv, w_out, norm_gain)
    own_a, w_qkv = lax.optimization_barrier((own_a, w_qkv))
    other_a = lax.ppermute(own_a, "span", other_core)
    other_b = lax.ppermute(own_b, "span", other_core)
    kv_flops = 2 * 2 * cells * ch * 2 * ch
    row_flops = 2 * cells * ch * (2 * ch + 8 * cells)
    kv_a = call(keys_kernel, "keys", struct((3 * cells, 2 * ch)), [VMEM] * 5, flops=kv_flops)(
        own_a, other_a, own_b, norm_gain, w_qkv
    )
    kv_b, att_a = call(
        attend_kernel,
        "attend",
        (struct((cells, 2 * ch)), struct((cells, ch))),
        [VMEM] * 6,
        flops=kv_flops + row_flops,
    )(other_b, own_a, kv_a, norm_gain, w_qkv, w_out)
    got_a = lax.ppermute(att_a, both, route_a)
    att_b = call(
        attend_rest_kernel,
        "attend_rest",
        struct((cells, ch)),
        [VMEM] * 6,
        flops=3 * row_flops,
    )(own_b, kv_a, kv_b, norm_gain, w_qkv, w_out)
    got_b = lax.ppermute(att_b, both, route_b)
    pairs, middle = [(0, 1), (1, 0), (2, 3), (3, 2)], [(1, 2), (2, 1)]
    one, edge = struct((cells, ch)), struct((cols, ch))
    sums = struct((frames, cells, ch), f32)
    unit = 2 * cells * 9 * ch * ch
    where = (tile, span, clip_lengths)
    w_packed = call(
        load_kernel,
        "load_conv",
        struct((3, 3 * ch, 3 * ch)),
        [ANY, ANY],
        [pltpu.SemaphoreType.DMA((27,))],
        42,
        size=1 << 12,
    )(att_b, w_conv)
    act_a, pair_edge, mid_edge = call(
        functools.partial(activate_a_kernel, cols), "activate_a", (one, edge, edge), [SMEM, VMEM, VMEM, ANY]
    )(tile, got_a, conv_gain, w_packed)
    pair_a = lax.ppermute(pair_edge, "tile", pairs)
    mid_a = lax.ppermute(mid_edge, "tile", middle)
    active, pair_edge, mid_edge = call(
        functools.partial(activate_b_kernel, cols),
        "activate_b",
        (struct((frames, cells, ch)), edge, edge),
        [SMEM] + [VMEM] * 3 + [ANY],
    )(tile, got_b, act_a, conv_gain, w_packed)
    pair_b = lax.ppermute(pair_edge, "tile", pairs)
    mid_b = lax.ppermute(mid_edge, "tile", middle)
    edges = (pair_a, mid_a, pair_b, mid_b)
    started = call(
        functools.partial(next_own_kernel, cols),
        "next_own",
        sums,
        [SMEM] * 2 + [VMEM] * 2,
        flops=2 * unit,
    )(span, clip_lengths, active, w_packed)
    pair_rows = call(
        functools.partial(pair_edge_kernel, cols),
        "pair_edge",
        struct((frames, cols, ch)),
        [SMEM] * 3 + [VMEM] * 4,
        flops=unit // 2,
    )(*where, pair_a, pair_b, w_packed, started)
    for_next = call(
        functools.partial(mid_edge_kernel, cols),
        "mid_edge",
        struct((frames, cells, ch)),
        [SMEM] * 3 + [VMEM] * 5,
        flops=unit // 2,
    )(*where, mid_a, mid_b, w_packed, started, pair_rows)
    link = [(s + d, s + 1 - d) for s in range(1, spans - 1, 2) for d in range(2)]
    link_got = lax.ppermute(for_next, "span", link)
    core_got = lax.ppermute(for_next, "span", other_core)
    own, attended = call(
        functools.partial(own_kernel, cols),
        "own",
        (sums, struct((frames, cells, ch))),
        [SMEM] * 3 + [VMEM] * 8,
        flops=3 * unit,
    )(*where, active, *edges, w_packed, got_a, got_b)
    hidden = pl.pallas_call(
        functools.partial(finish_kernel, cols),
        out_shape=struct((frames, cells, ch)),
        in_specs=[SMEM] + [VMEM] * 3,
        out_specs=ANY,
        scratch_shapes=[
            pltpu.VMEM((frames, cells, ch), bf16),
            pltpu.SemaphoreType.DMA((4,)),
        ],
        compiler_params=pltpu.CompilerParams(vmem_limit_bytes=16 << 20),
        name="finish",
    )(span, own, link_got, core_got)
    shape = (frames, row_count, cols, ch)
    return attended.reshape(shape), hidden.reshape(shape)


def extended(x, sides, width):
    for axis, dim in sides:
        size, length = (lax.axis_size(axis), x.shape[dim])
        up = [(i, (i + 1) % size) for i in range(size - 1)]
        down = [(j, i) for i, j in up]
        last = lax.slice_in_dim(x, length - width, length, axis=dim)
        first = lax.slice_in_dim(x, 0, width, axis=dim)
        before = lax.ppermute(last, axis, up)
        after = lax.ppermute(first, axis, down)
        x = jnp.concatenate([before, x, after], axis=dim)
    return x


def general(features, clip_lengths, norm_gain, w_qkv, w_out, conv_gain, w_conv):
    frames, row_count, col_count, channels = features.shape
    cell_count = row_count * col_count
    normed_grid = rms_scale(features, norm_gain).astype(jnp.bfloat16)
    view_frames = normed_grid.shape[0]
    view_cells = normed_grid.shape[1] * normed_grid.shape[2]
    normed = normed_grid.reshape(view_frames, view_cells, channels)
    queries = jnp.dot(
        normed.reshape(-1, channels), w_qkv[:, :channels], preferred_element_type=jnp.float32
    )
    queries = queries.astype(jnp.bfloat16).reshape(view_frames, view_cells, channels)
    kv_weight = w_qkv[:, channels:]
    score_scale = channels ** (-0.5)
    outgoing = jnp.dot(normed.reshape(-1, channels), kv_weight, preferred_element_type=jnp.float32)
    outgoing = outgoing.astype(jnp.bfloat16).reshape(view_frames, view_cells, 2 * channels)
    portion = lax.all_gather(outgoing, "tile", axis=1, tiled=True)
    key_part = portion[:, :, :channels]
    value_part = portion[:, :, channels:]
    row_top = jnp.full((view_frames, view_cells, 1), -1e30, jnp.float32)
    scores = (
        jnp.einsum("fqc,fkc->fqk", queries, key_part, preferred_element_type=jnp.float32)
        * score_scale
    )
    new_top = jnp.maximum(row_top, jnp.max(scores, axis=2, keepdims=True))
    raised_f = jnp.exp(scores - new_top)
    row_total = jnp.sum(raised_f, axis=2, keepdims=True)
    weighted = jnp.einsum(
        "fqk,fkc->fqc",
        raised_f.astype(jnp.bfloat16),
        value_part,
        preferred_element_type=jnp.float32,
    )
    mixture_grid = (weighted / row_total).astype(jnp.bfloat16)
    mixture = mixture_grid.reshape(-1, channels)
    projected = jnp.dot(mixture, w_out, preferred_element_type=jnp.float32)
    attended = (features.reshape(-1, channels).astype(jnp.float32) + projected).astype(jnp.bfloat16)
    attended = attended.reshape(frames, row_count, col_count, channels)
    lifted = rms_scale(attended, conv_gain)
    activated = (lifted * jax.nn.sigmoid(lifted)).astype(jnp.bfloat16)
    earlier = from_behind(activated, "span", 1)
    stacked = jnp.concatenate([earlier, activated], axis=0)
    edged = extended(stacked, (("tile", 1),), 1)
    padded = jnp.pad(edged, ((0, 0), (0, 0), (1, 1), (0, 0)))
    clip_ends = jnp.cumsum(clip_lengths)
    position = lax.axis_index("span") * frames + jnp.arange(frames, dtype=jnp.int32)
    clip_start = jnp.sum(
        jnp.where(clip_ends[None, :] <= position[:, None], clip_lengths[None, :], 0), axis=1
    )
    summed = jnp.zeros((frames * cell_count, channels), jnp.float32)
    for t_tap in range(3):
        usable = position - (2 - t_tap) >= clip_start
        for r_tap in range(3):
            for c_tap in range(3):
                shifted = padded[
                    t_tap : t_tap + frames, r_tap : r_tap + row_count, c_tap : c_tap + col_count
                ]
                shifted = jnp.where(
                    usable[:, None, None, None], shifted, jnp.zeros((), shifted.dtype)
                )
                summed = summed + jnp.dot(
                    shifted.reshape(-1, channels),
                    w_conv[t_tap, r_tap, c_tap],
                    preferred_element_type=jnp.float32,
                )
    hidden = summed.astype(jnp.bfloat16).reshape(frames, row_count, col_count, channels)
    return (attended, hidden)


def solution(mesh):
    in_specs = (P(("grp", "span"), "tile", None, None), P("grp"), P(), P(), P(), P(), P())
    out_specs = (P(("grp", "span"), "tile", None, None), P(("grp", "span"), "tile", None, None))
    return jax.shard_map(
        on_device, mesh=mesh, in_specs=in_specs, out_specs=out_specs, check_vma=False
    )
```

```python
import functools

import jax
import jax.numpy as jnp
from jax import lax
from jax.experimental import pallas as pl
from jax.experimental.pallas import tpu as pltpu
from jax.sharding import PartitionSpec as P

eps = 1e-06
f32, bf16 = jnp.float32, jnp.bfloat16
LOG2E = 1.4426950408889634
VMEM = pl.BlockSpec(memory_space=pltpu.VMEM)
SMEM = pl.BlockSpec(memory_space=pltpu.SMEM)
ANY = pl.BlockSpec(memory_space=pl.ANY)


def from_behind(block, axis, distance):
    devices = range(lax.axis_size(axis))
    route = [(i - distance, i) for i in devices if i - distance in devices]
    return lax.ppermute(block, axis, route)


def rms_scale(values, gain_vec):
    as_float = values.astype(f32)
    return (
        as_float * lax.rsqrt(jnp.mean(as_float * as_float, axis=-1, keepdims=True) + eps) * gain_vec
    )


def dot32(a, b):
    return jnp.dot(a, b, preferred_element_type=f32)


def struct(shape, dtype=bf16):
    return jax.ShapeDtypeStruct(shape, dtype)


def call(kernel, name, out_shape, in_specs, scratch=(), limit=16, flops=0, size=1 << 20):
    outs = jax.tree.map(lambda _: VMEM, out_shape)
    cost = pl.CostEstimate(flops=int(flops), transcendentals=0, bytes_accessed=int(size))
    return pl.pallas_call(
        kernel,
        out_shape=out_shape,
        in_specs=in_specs,
        out_specs=outs,
        scratch_shapes=list(scratch),
        compiler_params=pltpu.CompilerParams(vmem_limit_bytes=limit << 20),
        cost_estimate=cost,
        name=name,
    )


def frame_route(spans, flip):
    route = []
    for tile in range(4):
        for span in range(spans):
            high, low, column, core = tile // 2, tile % 2, span // 2, span % 2
            there = (2 * core + (low ^ flip)) * spans + 2 * column + high
            route.append((tile * spans + span, there))
    return route


def pick_kernel(tile_ref, x_hbm, first, second, sem):
    low = tile_ref[0] % 2

    def move(a, b):
        copies = [
            pltpu.make_async_copy(x_hbm.at[a], first, sem.at[0]),
            pltpu.make_async_copy(x_hbm.at[b], second, sem.at[1]),
        ]
        for copy in copies:
            copy.start()
        for copy in copies:
            copy.wait()

    @pl.when(low == 0)
    def _():
        move(0, 1)

    @pl.when(low == 1)
    def _():
        move(1, 0)


def load_small_kernel(w_qkv, w_out, gain, qkv_vm, out_vm, gain_vm, sem):
    copies = [
        pltpu.make_async_copy(w_qkv, qkv_vm, sem.at[0]),
        pltpu.make_async_copy(w_out, out_vm, sem.at[1]),
    ]
    for copy in copies:
        copy.start()
    gain_vm[...] = gain[...]
    for copy in copies:
        copy.wait()


def project_keys(block, gain_vec, w_qkv, out, place):
    cells, ch = block.shape
    normed = rms_scale(block[...], gain_vec).astype(bf16)
    out[place * cells : (place + 1) * cells, :] = dot32(normed, w_qkv[:, ch:]).astype(bf16)


def keys_kernel(own_a, other_a, own_b, gain, w_qkv, kv_out):
    gain_vec = gain[...].reshape(1, own_a.shape[1])
    for place, block in enumerate((own_a, other_a, own_b)):
        project_keys(block, gain_vec, w_qkv, kv_out, place)


def attend_rows(source, kv_parts, gain_vec, w_qkv, w_out, att_out):
    ch = source.shape[1]
    feats = source[...]
    normed = rms_scale(feats, gain_vec).astype(bf16)
    queries = dot32(normed, w_qkv[:, :ch]).astype(bf16)
    scores = [
        lax.dot_general(
            queries, kv[:, :ch], (((1,), (1,)), ((), ())), preferred_element_type=f32
        )
        * (ch ** (-0.5) * LOG2E)
        for kv in kv_parts
    ]
    top = functools.reduce(jnp.maximum, [jnp.max(s, axis=1, keepdims=True) for s in scores])
    raised = [jnp.exp2(s - top) for s in scores]
    total = sum(jnp.sum(r, axis=1, keepdims=True) for r in raised)
    mixed = sum(dot32(r.astype(bf16), kv[:, ch:]) for r, kv in zip(raised, kv_parts))
    mixture = (mixed / total).astype(bf16)
    att_out[...] = (feats.astype(f32) + dot32(mixture, w_out[...])).astype(bf16)


def attend_kernel(other_b, own_a, kv_a, gain, w_qkv, w_out, kv_b, att_a):
    gain_vec = gain[...].reshape(1, own_a.shape[1])
    project_keys(other_b, gain_vec, w_qkv, kv_b, 0)
    attend_rows(own_a, (kv_a, kv_b), gain_vec, w_qkv, w_out, att_a)


def attend_rest_kernel(own_b, kv_a, kv_b, gain, w_qkv, w_out, att_b):
    gain_vec = gain[...].reshape(1, own_b.shape[1])
    attend_rows(own_b, (kv_a, kv_b), gain_vec, w_qkv, w_out, att_b)


def load_kernel(_, w_hbm, w_vm, sem):
    ch = w_hbm.shape[-1]
    copies = [
        pltpu.make_async_copy(
            w_hbm.at[i, j, k],
            w_vm.at[i, j * ch : (j + 1) * ch, k * ch : (k + 1) * ch],
            sem.at[9 * i + 3 * j + k],
        )
        for i in range(3)
        for j in range(3)
        for k in range(3)
    ]
    for copy in copies:
        copy.start()
    for copy in copies:
        copy.wait()


def activate(cols, low, block, gain, act_out, pair_edge, mid_edge):
    lifted = rms_scale(block[...], gain[...].reshape(1, block.shape[1]))
    act = (lifted / (1.0 + jnp.exp(-lifted))).astype(bf16)
    act_out[...] = act

    @pl.when(low == 0)
    def _():
        pair_edge[...] = act[cols:, :]
        mid_edge[...] = act[:cols, :]

    @pl.when(low == 1)
    def _():
        pair_edge[...] = act[:cols, :]
        mid_edge[...] = act[cols:, :]


def activate_a_kernel(cols, tile_ref, got_a, gain, _, *outs):
    activate(cols, tile_ref[0] % 2, got_a, gain, *outs)


def activate_b_kernel(cols, tile_ref, got_b, act_a, gain, _, active, pair_edge, mid_edge):
    low = tile_ref[0] % 2
    activate(cols, low, got_b, gain, active.at[1 - low], pair_edge, mid_edge)
    active[low] = act_a[...]


def usable_flag(clips, frame_at, tap):
    end = jnp.int32(0)
    start = jnp.int32(0)
    for i in range(clips.shape[0]):
        end = end + clips[i]
        start = start + jnp.where(end <= frame_at, clips[i], 0)
    return frame_at - (2 - tap) >= start


def shift_add(part, cols, ch):
    at = lax.broadcasted_iota(jnp.int32, (cols, ch), 0)
    left = jnp.where(at == 0, 0.0, pltpu.roll(part[:, :ch], 1, 0))
    right = jnp.where(at == cols - 1, 0.0, pltpu.roll(part[:, 2 * ch :], cols - 1, 0))
    return part[:, ch : 2 * ch] + left + right


def weigh(flag, block):
    return (block.astype(f32) * flag).astype(bf16)


def flags_of(clips, frame_at):
    return [
        [usable_flag(clips, frame_at + f, tap).astype(f32) for tap in range(3)] for f in range(2)
    ]


def edge_rows(tile_ref, pair_a, mid_a, pair_b, mid_b):
    odd = (tile_ref[0] % 2).astype(f32)

    def pick(if_odd, if_even):
        return if_odd[...].astype(f32) * odd + if_even[...].astype(f32) * (1.0 - odd)

    above = [pick(pair_a, mid_b), pick(pair_b, mid_a)]
    below = [pick(mid_a, pair_b), pick(mid_b, pair_a)]
    return above, below


def next_own_kernel(cols, span_ref, clips, mid, w, out):
    ch = mid.shape[-1]
    flag = flags_of(clips, (span_ref[0] + 1) * 2)
    use_far, use_near = flag[0][0] + flag[1][0] > 0.0, flag[0][1] > 0.0
    parts = ((slice(0, cols), slice(ch, 3 * ch)), (slice(cols, 2 * cols), slice(0, 2 * ch)))

    def pair(f):
        return jnp.concatenate([mid[f, :cols, :], mid[f, cols:, :]], axis=1)

    @pl.when(use_far)
    def _():
        last = jnp.concatenate([weigh(flag[f][0], pair(f)) for f in range(2)], axis=0)
        for part, taps in parts:
            far = dot32(last, w[0, taps])
            out[0, part, :] = shift_add(far[:cols], cols, ch)
            out[1, part, :] = shift_add(far[cols:], cols, ch)

    @pl.when(jnp.logical_not(use_far))
    def _():
        out[...] = jnp.zeros_like(out)

    @pl.when(use_near)
    def _():
        middle = pair(1)
        for part, taps in parts:
            out[0, part, :] += shift_add(dot32(middle, w[1, taps]), cols, ch)


def next_edge_kernel(
    cols, tile_ref, span_ref, clips, pair_a, mid_a, pair_b, mid_b, w, partial, out, total
):
    ch = w.shape[-1] // 3
    flag = flags_of(clips, (span_ref[0] + 1) * 2)
    use_far, use_near = flag[0][0] + flag[1][0] > 0.0, flag[0][1] > 0.0
    parts = ((slice(0, cols), slice(0, ch)), (slice(cols, 2 * cols), slice(2 * ch, 3 * ch)))
    total[...] = partial[...]

    @pl.when(use_far)
    def _():
        edges = edge_rows(tile_ref, pair_a, mid_a, pair_b, mid_b)
        for edge, (part, taps) in zip(edges, parts):
            last = jnp.concatenate([edge[f] * flag[f][0] for f in range(2)], axis=0)
            far = dot32(last.astype(bf16), w[0, taps])
            total[0, part, :] += shift_add(far[:cols], cols, ch)
            total[1, part, :] += shift_add(far[cols:], cols, ch)

    @pl.when(use_near)
    def _():
        edges = edge_rows(tile_ref, pair_a, mid_a, pair_b, mid_b)
        for edge, (part, taps) in zip(edges, parts):
            near = dot32(edge[1].astype(bf16), w[1, taps])
            total[0, part, :] += shift_add(near, cols, ch)

    out[...] = total[...].astype(bf16)


def own_kernel(
    cols,
    tile_ref,
    span_ref,
    clips,
    mid,
    pair_a,
    mid_a,
    pair_b,
    mid_b,
    w,
    got_a,
    got_b,
    out,
    attended,
):
    low = tile_ref[0] % 2
    attended[low] = got_a[...]
    attended[1 - low] = got_b[...]
    ch = mid.shape[-1]
    above, below = edge_rows(tile_ref, pair_a, mid_a, pair_b, mid_b)
    wide = []
    for f in range(2):
        rows = [above[f].astype(bf16), mid[f, :cols, :], mid[f, cols:, :], below[f].astype(bf16)]
        wide += [jnp.concatenate(rows[r : r + 3], axis=1) for r in range(2)]
    here = dot32(jnp.concatenate(wide, axis=0), w[2])
    flag = usable_flag(clips, span_ref[0] * 2 + 1, 1).astype(f32)
    back = dot32(weigh(flag, jnp.concatenate(wide[:2], axis=0)), w[1])
    for r in range(2):
        part = slice(r * cols, (r + 1) * cols)
        out[0, part, :] = shift_add(here[part], cols, ch)
        after = here[(2 + r) * cols : (3 + r) * cols]
        out[1, part, :] = shift_add(after + back[part], cols, ch)


def finish_kernel(span_ref, own, link_got, core_got, out):
    span = span_ref[0]

    @pl.when(span == 0)
    def _():
        out[...] = own[...].astype(bf16)

    @pl.when(span % 2 == 1)
    def _():
        out[...] = (own[...] + core_got[...].astype(f32)).astype(bf16)

    @pl.when(jnp.logical_and(span % 2 == 0, span > 0))
    def _():
        out[...] = (own[...] + link_got[...].astype(f32)).astype(bf16)


def on_device(features, clip_lengths, norm_gain, w_qkv, w_out, conv_gain, w_conv):
    frames, row_count, cols, ch = features.shape
    tiles, spans = lax.axis_size("tile"), lax.axis_size("span")
    if tiles != 4 or spans % 2 or frames != 2 or row_count != 2:
        return general(features, clip_lengths, norm_gain, w_qkv, w_out, conv_gain, w_conv)
    cells = row_count * cols
    both = ("tile", "span")
    tile = lax.axis_index("tile").astype(jnp.int32).reshape(1)
    span = lax.axis_index("span").astype(jnp.int32).reshape(1)
    other_core = [(i, i ^ 1) for i in range(spans)]
    route_a, route_b = frame_route(spans, 0), frame_route(spans, 1)
    x = features.reshape(frames, cells, ch)
    send_a, send_b = call(
        pick_kernel,
        "pick",
        (pltpu.VMEM((cells, ch), bf16), pltpu.VMEM((cells, ch), bf16)),
        [SMEM, ANY],
        [pltpu.SemaphoreType.DMA((2,))],
        62,
    )(tile, x)
    own_a = lax.ppermute(send_a, both, route_a)
    own_b = lax.ppermute(send_b, both, route_b)
    w_qkv, w_out, norm_gain = call(
        load_small_kernel,
        "load_small",
        (pltpu.VMEM(w_qkv.shape, bf16), pltpu.VMEM(w_out.shape, bf16), pltpu.VMEM((ch,), f32)),
        [ANY, ANY, VMEM],
        [pltpu.SemaphoreType.DMA((2,))],
        60,
    )(w_qkv, w_out, norm_gain)
    own_a, w_qkv = lax.optimization_barrier((own_a, w_qkv))
    other_a = lax.ppermute(own_a, "span", other_core)
    other_b = lax.ppermute(own_b, "span", other_core)
    kv_flops = 2 * 2 * cells * ch * 2 * ch
    row_flops = 2 * cells * ch * (2 * ch + 8 * cells)
    kv_a = call(keys_kernel, "keys", struct((3 * cells, 2 * ch)), [VMEM] * 5, flops=kv_flops)(
        own_a, other_a, own_b, norm_gain, w_qkv
    )
    kv_b, att_a = call(
        attend_kernel,
        "attend",
        (struct((cells, 2 * ch)), struct((cells, ch))),
        [VMEM] * 6,
        flops=kv_flops + row_flops,
    )(other_b, own_a, kv_a, norm_gain, w_qkv, w_out)
    got_a = lax.ppermute(att_a, both, route_a)
    att_b = call(
        attend_rest_kernel,
        "attend_rest",
        struct((cells, ch)),
        [VMEM] * 6,
        flops=3 * row_flops,
    )(own_b, kv_a, kv_b, norm_gain, w_qkv, w_out)
    got_b = lax.ppermute(att_b, both, route_b)
    pairs, middle = [(0, 1), (1, 0), (2, 3), (3, 2)], [(1, 2), (2, 1)]
    one, edge = struct((cells, ch)), struct((cols, ch))
    sums = struct((frames, cells, ch), f32)
    unit = 2 * cells * 9 * ch * ch
    where = (tile, span, clip_lengths)
    w_packed = call(
        load_kernel,
        "load_conv",
        struct((3, 3 * ch, 3 * ch)),
        [ANY, ANY],
        [pltpu.SemaphoreType.DMA((27,))],
        42,
        size=1 << 12,
    )(att_b, w_conv)
    act_a, pair_edge, mid_edge = call(
        functools.partial(activate_a_kernel, cols), "activate_a", (one, edge, edge), [SMEM, VMEM, VMEM, ANY]
    )(tile, got_a, conv_gain, w_packed)
    pair_a = lax.ppermute(pair_edge, "tile", pairs)
    mid_a = lax.ppermute(mid_edge, "tile", middle)
    active, pair_edge, mid_edge = call(
        functools.partial(activate_b_kernel, cols),
        "activate_b",
        (struct((frames, cells, ch)), edge, edge),
        [SMEM] + [VMEM] * 3 + [ANY],
    )(tile, got_b, act_a, conv_gain, w_packed)
    pair_b = lax.ppermute(pair_edge, "tile", pairs)
    mid_b = lax.ppermute(mid_edge, "tile", middle)
    edges = (pair_a, mid_a, pair_b, mid_b)
    started = call(
        functools.partial(next_own_kernel, cols),
        "next_own",
        sums,
        [SMEM] * 2 + [VMEM] * 2,
        flops=2 * unit,
    )(span, clip_lengths, active, w_packed)
    for_next = call(
        functools.partial(next_edge_kernel, cols),
        "next_edge",
        struct((frames, cells, ch)),
        [SMEM] * 3 + [VMEM] * 6,
        [pltpu.VMEM((frames, cells, ch), f32)],
        flops=unit,
    )(*where, *edges, w_packed, started)
    link = [(s + d, s + 1 - d) for s in range(1, spans - 1, 2) for d in range(2)]
    link_got = lax.ppermute(for_next, "span", link)
    core_got = lax.ppermute(for_next, "span", other_core)
    own, attended = call(
        functools.partial(own_kernel, cols),
        "own",
        (sums, struct((frames, cells, ch))),
        [SMEM] * 3 + [VMEM] * 8,
        flops=3 * unit,
    )(*where, active, *edges, w_packed, got_a, got_b)
    hidden = call(
        finish_kernel, "finish", struct((frames, cells, ch)), [SMEM] + [VMEM] * 3
    )(span, own, link_got, core_got)
    shape = (frames, row_count, cols, ch)
    return attended.reshape(shape), hidden.reshape(shape)


def extended(x, sides, width):
    for axis, dim in sides:
        size, length = (lax.axis_size(axis), x.shape[dim])
        up = [(i, (i + 1) % size) for i in range(size - 1)]
        down = [(j, i) for i, j in up]
        last = lax.slice_in_dim(x, length - width, length, axis=dim)
        first = lax.slice_in_dim(x, 0, width, axis=dim)
        before = lax.ppermute(last, axis, up)
        after = lax.ppermute(first, axis, down)
        x = jnp.concatenate([before, x, after], axis=dim)
    return x


def general(features, clip_lengths, norm_gain, w_qkv, w_out, conv_gain, w_conv):
    frames, row_count, col_count, channels = features.shape
    cell_count = row_count * col_count
    normed_grid = rms_scale(features, norm_gain).astype(jnp.bfloat16)
    view_frames = normed_grid.shape[0]
    view_cells = normed_grid.shape[1] * normed_grid.shape[2]
    normed = normed_grid.reshape(view_frames, view_cells, channels)
    queries = jnp.dot(
        normed.reshape(-1, channels), w_qkv[:, :channels], preferred_element_type=jnp.float32
    )
    queries = queries.astype(jnp.bfloat16).reshape(view_frames, view_cells, channels)
    kv_weight = w_qkv[:, channels:]
    score_scale = channels ** (-0.5)
    outgoing = jnp.dot(normed.reshape(-1, channels), kv_weight, preferred_element_type=jnp.float32)
    outgoing = outgoing.astype(jnp.bfloat16).reshape(view_frames, view_cells, 2 * channels)
    portion = lax.all_gather(outgoing, "tile", axis=1, tiled=True)
    key_part = portion[:, :, :channels]
    value_part = portion[:, :, channels:]
    row_top = jnp.full((view_frames, view_cells, 1), -1e30, jnp.float32)
    scores = (
        jnp.einsum("fqc,fkc->fqk", queries, key_part, preferred_element_type=jnp.float32)
        * score_scale
    )
    new_top = jnp.maximum(row_top, jnp.max(scores, axis=2, keepdims=True))
    raised_f = jnp.exp(scores - new_top)
    row_total = jnp.sum(raised_f, axis=2, keepdims=True)
    weighted = jnp.einsum(
        "fqk,fkc->fqc",
        raised_f.astype(jnp.bfloat16),
        value_part,
        preferred_element_type=jnp.float32,
    )
    mixture_grid = (weighted / row_total).astype(jnp.bfloat16)
    mixture = mixture_grid.reshape(-1, channels)
    projected = jnp.dot(mixture, w_out, preferred_element_type=jnp.float32)
    attended = (features.reshape(-1, channels).astype(jnp.float32) + projected).astype(jnp.bfloat16)
    attended = attended.reshape(frames, row_count, col_count, channels)
    lifted = rms_scale(attended, conv_gain)
    activated = (lifted * jax.nn.sigmoid(lifted)).astype(jnp.bfloat16)
    earlier = from_behind(activated, "span", 1)
    stacked = jnp.concatenate([earlier, activated], axis=0)
    edged = extended(stacked, (("tile", 1),), 1)
    padded = jnp.pad(edged, ((0, 0), (0, 0), (1, 1), (0, 0)))
    clip_ends = jnp.cumsum(clip_lengths)
    position = lax.axis_index("span") * frames + jnp.arange(frames, dtype=jnp.int32)
    clip_start = jnp.sum(
        jnp.where(clip_ends[None, :] <= position[:, None], clip_lengths[None, :], 0), axis=1
    )
    summed = jnp.zeros((frames * cell_count, channels), jnp.float32)
    for t_tap in range(3):
        usable = position - (2 - t_tap) >= clip_start
        for r_tap in range(3):
            for c_tap in range(3):
                shifted = padded[
                    t_tap : t_tap + frames, r_tap : r_tap + row_count, c_tap : c_tap + col_count
                ]
                shifted = jnp.where(
                    usable[:, None, None, None], shifted, jnp.zeros((), shifted.dtype)
                )
                summed = summed + jnp.dot(
                    shifted.reshape(-1, channels),
                    w_conv[t_tap, r_tap, c_tap],
                    preferred_element_type=jnp.float32,
                )
    hidden = summed.astype(jnp.bfloat16).reshape(frames, row_count, col_count, channels)
    return (attended, hidden)


def solution(mesh):
    in_specs = (P(("grp", "span"), "tile", None, None), P("grp"), P(), P(), P(), P(), P())
    out_specs = (P(("grp", "span"), "tile", None, None), P(("grp", "span"), "tile", None, None))
    return jax.shard_map(
        on_device, mesh=mesh, in_specs=in_specs, out_specs=out_specs, check_vma=False
    )
```

```python
import functools

import jax
import jax.numpy as jnp
from jax import lax
from jax.experimental import pallas as pl
from jax.experimental.pallas import tpu as pltpu
from jax.sharding import PartitionSpec as P

eps = 1e-06
f32, bf16 = jnp.float32, jnp.bfloat16
LOG2E = 1.4426950408889634
VMEM = pl.BlockSpec(memory_space=pltpu.VMEM)
SMEM = pl.BlockSpec(memory_space=pltpu.SMEM)
ANY = pl.BlockSpec(memory_space=pl.ANY)


def from_behind(block, axis, distance):
    devices = range(lax.axis_size(axis))
    route = [(i - distance, i) for i in devices if i - distance in devices]
    return lax.ppermute(block, axis, route)


def rms_scale(values, gain_vec):
    as_float = values.astype(f32)
    return (
        as_float * lax.rsqrt(jnp.mean(as_float * as_float, axis=-1, keepdims=True) + eps) * gain_vec
    )


def dot32(a, b):
    return jnp.dot(a, b, preferred_element_type=f32)


def struct(shape, dtype=bf16):
    return jax.ShapeDtypeStruct(shape, dtype)


def call(kernel, name, out_shape, in_specs, scratch=(), limit=16, flops=0, size=1 << 20):
    outs = jax.tree.map(lambda _: VMEM, out_shape)
    cost = pl.CostEstimate(flops=int(flops), transcendentals=0, bytes_accessed=int(size))
    return pl.pallas_call(
        kernel,
        out_shape=out_shape,
        in_specs=in_specs,
        out_specs=outs,
        scratch_shapes=list(scratch),
        compiler_params=pltpu.CompilerParams(vmem_limit_bytes=limit << 20),
        cost_estimate=cost,
        name=name,
    )


def frame_route(spans, flip):
    route = []
    for tile in range(4):
        for span in range(spans):
            high, low, column, core = tile // 2, tile % 2, span // 2, span % 2
            there = (2 * core + (low ^ flip)) * spans + 2 * column + high
            route.append((tile * spans + span, there))
    return route


def pick_kernel(tile_ref, x_hbm, first, second, sem):
    low = tile_ref[0] % 2

    def move(a, b):
        copies = [
            pltpu.make_async_copy(x_hbm.at[a], first, sem.at[0]),
            pltpu.make_async_copy(x_hbm.at[b], second, sem.at[1]),
        ]
        for copy in copies:
            copy.start()
        for copy in copies:
            copy.wait()

    @pl.when(low == 0)
    def _():
        move(0, 1)

    @pl.when(low == 1)
    def _():
        move(1, 0)


def load_small_kernel(w_qkv, w_out, gain, qkv_vm, out_vm, gain_vm, sem):
    copies = [
        pltpu.make_async_copy(w_qkv, qkv_vm, sem.at[0]),
        pltpu.make_async_copy(w_out, out_vm, sem.at[1]),
    ]
    for copy in copies:
        copy.start()
    gain_vm[...] = gain[...]
    for copy in copies:
        copy.wait()


def project_keys(block, gain_vec, w_qkv, out, place):
    cells, ch = block.shape
    normed = rms_scale(block[...], gain_vec).astype(bf16)
    out[place * cells : (place + 1) * cells, :] = dot32(normed, w_qkv[:, ch:]).astype(bf16)


def keys_kernel(own_a, other_a, own_b, gain, w_qkv, kv_out):
    gain_vec = gain[...].reshape(1, own_a.shape[1])
    for place, block in enumerate((own_a, other_a, own_b)):
        project_keys(block, gain_vec, w_qkv, kv_out, place)


def attend_rows(source, kv_parts, gain_vec, w_qkv, w_out, att_out):
    ch = source.shape[1]
    feats = source[...]
    normed = rms_scale(feats, gain_vec).astype(bf16)
    queries = dot32(normed, w_qkv[:, :ch]).astype(bf16)
    scores = [
        lax.dot_general(
            queries, kv[:, :ch], (((1,), (1,)), ((), ())), preferred_element_type=f32
        )
        * (ch ** (-0.5) * LOG2E)
        for kv in kv_parts
    ]
    top = functools.reduce(jnp.maximum, [jnp.max(s, axis=1, keepdims=True) for s in scores])
    raised = [jnp.exp2(s - top) for s in scores]
    total = sum(jnp.sum(r, axis=1, keepdims=True) for r in raised)
    mixed = sum(dot32(r.astype(bf16), kv[:, ch:]) for r, kv in zip(raised, kv_parts))
    mixture = (mixed / total).astype(bf16)
    att_out[...] = (feats.astype(f32) + dot32(mixture, w_out[...])).astype(bf16)


def attend_kernel(other_b, own_a, kv_a, gain, w_qkv, w_out, kv_b, att_a):
    gain_vec = gain[...].reshape(1, own_a.shape[1])
    project_keys(other_b, gain_vec, w_qkv, kv_b, 0)
    attend_rows(own_a, (kv_a, kv_b), gain_vec, w_qkv, w_out, att_a)


def attend_rest_kernel(own_b, kv_a, kv_b, gain, w_qkv, w_out, att_b):
    gain_vec = gain[...].reshape(1, own_b.shape[1])
    attend_rows(own_b, (kv_a, kv_b), gain_vec, w_qkv, w_out, att_b)


def load_kernel(_, w_hbm, w_vm, sem):
    ch = w_hbm.shape[-1]
    copies = [
        pltpu.make_async_copy(
            w_hbm.at[i, j, k],
            w_vm.at[i, j * ch : (j + 1) * ch, k * ch : (k + 1) * ch],
            sem.at[9 * i + 3 * j + k],
        )
        for i in range(3)
        for j in range(3)
        for k in range(3)
    ]
    for copy in copies:
        copy.start()
    for copy in copies:
        copy.wait()


def activate(cols, low, block, gain, act_out, pair_edge, mid_edge):
    lifted = rms_scale(block[...], gain[...].reshape(1, block.shape[1]))
    act = (lifted / (1.0 + jnp.exp(-lifted))).astype(bf16)
    act_out[...] = act

    @pl.when(low == 0)
    def _():
        pair_edge[...] = act[cols:, :]
        mid_edge[...] = act[:cols, :]

    @pl.when(low == 1)
    def _():
        pair_edge[...] = act[:cols, :]
        mid_edge[...] = act[cols:, :]


def activate_a_kernel(cols, tile_ref, got_a, gain, _, *outs):
    activate(cols, tile_ref[0] % 2, got_a, gain, *outs)


def activate_b_kernel(cols, tile_ref, got_b, act_a, gain, _, active, pair_edge, mid_edge):
    low = tile_ref[0] % 2
    activate(cols, low, got_b, gain, active.at[1 - low], pair_edge, mid_edge)
    active[low] = act_a[...]


def usable_flag(clips, frame_at, tap):
    end = jnp.int32(0)
    start = jnp.int32(0)
    for i in range(clips.shape[0]):
        end = end + clips[i]
        start = start + jnp.where(end <= frame_at, clips[i], 0)
    return frame_at - (2 - tap) >= start


def shift_add(part, cols, ch):
    at = lax.broadcasted_iota(jnp.int32, (cols, ch), 0)
    left = jnp.where(at == 0, 0.0, pltpu.roll(part[:, :ch], 1, 0))
    right = jnp.where(at == cols - 1, 0.0, pltpu.roll(part[:, 2 * ch :], cols - 1, 0))
    return part[:, ch : 2 * ch] + left + right


def weigh(flag, block):
    return (block.astype(f32) * flag).astype(bf16)


def flags_of(clips, frame_at):
    return [
        [usable_flag(clips, frame_at + f, tap).astype(f32) for tap in range(3)] for f in range(2)
    ]


def edge_rows(tile_ref, pair_a, mid_a, pair_b, mid_b):
    odd = (tile_ref[0] % 2).astype(f32)

    def pick(if_odd, if_even):
        return if_odd[...].astype(f32) * odd + if_even[...].astype(f32) * (1.0 - odd)

    above = [pick(pair_a, mid_b), pick(pair_b, mid_a)]
    below = [pick(mid_a, pair_b), pick(mid_b, pair_a)]
    return above, below


def next_own_kernel(cols, span_ref, clips, mid, w, out):
    ch = mid.shape[-1]
    flag = flags_of(clips, (span_ref[0] + 1) * 2)
    use_far, use_near = flag[0][0] + flag[1][0] > 0.0, flag[0][1] > 0.0
    parts = ((slice(0, cols), slice(ch, 3 * ch)), (slice(cols, 2 * cols), slice(0, 2 * ch)))

    def pair(f):
        return jnp.concatenate([mid[f, :cols, :], mid[f, cols:, :]], axis=1)

    @pl.when(use_far)
    def _():
        last = jnp.concatenate([weigh(flag[f][0], pair(f)) for f in range(2)], axis=0)
        for part, taps in parts:
            far = dot32(last, w[0, taps])
            out[0, part, :] = shift_add(far[:cols], cols, ch)
            out[1, part, :] = shift_add(far[cols:], cols, ch)

    @pl.when(jnp.logical_not(use_far))
    def _():
        out[...] = jnp.zeros_like(out)

    @pl.when(use_near)
    def _():
        middle = pair(1)
        for part, taps in parts:
            out[0, part, :] += shift_add(dot32(middle, w[1, taps]), cols, ch)


def edge_part(cols, flag, first, second, above, w, partial, total):
    ch = w.shape[-1] // 3
    part = slice(0, cols) if above else slice(cols, 2 * cols)
    taps = slice(0, ch) if above else slice(2 * ch, 3 * ch)
    total[...] = partial[:, part, :]

    @pl.when(flag[0][0] + flag[1][0] > 0.0)
    def _():
        last = jnp.concatenate(
            [weigh(flag[0][0], first[...]), weigh(flag[1][0], second[...])], axis=0
        )
        far = dot32(last, w[0, taps])
        total[0] += shift_add(far[:cols], cols, ch)
        total[1] += shift_add(far[cols:], cols, ch)

    @pl.when(flag[0][1] > 0.0)
    def _():
        total[0] += shift_add(dot32(second[...], w[1, taps]), cols, ch)


def pair_edge_kernel(cols, tile_ref, span_ref, clips, pair_a, pair_b, w, partial, out, total):
    flag = flags_of(clips, (span_ref[0] + 1) * 2)

    @pl.when(tile_ref[0] % 2 == 1)
    def _():
        edge_part(cols, flag, pair_a, pair_b, True, w, partial, total)

    @pl.when(tile_ref[0] % 2 == 0)
    def _():
        edge_part(cols, flag, pair_b, pair_a, False, w, partial, total)

    out[...] = total[...].astype(bf16)


def mid_edge_kernel(
    cols, tile_ref, span_ref, clips, mid_a, mid_b, w, partial, pair_rows, out, total
):
    flag = flags_of(clips, (span_ref[0] + 1) * 2)

    @pl.when(tile_ref[0] % 2 == 1)
    def _():
        edge_part(cols, flag, mid_a, mid_b, False, w, partial, total)
        out[:, :cols, :] = pair_rows[...]
        out[:, cols:, :] = total[...].astype(bf16)

    @pl.when(tile_ref[0] % 2 == 0)
    def _():
        edge_part(cols, flag, mid_b, mid_a, True, w, partial, total)
        out[:, cols:, :] = pair_rows[...]
        out[:, :cols, :] = total[...].astype(bf16)


def own_kernel(
    cols,
    tile_ref,
    span_ref,
    clips,
    mid,
    pair_a,
    mid_a,
    pair_b,
    mid_b,
    w,
    got_a,
    got_b,
    out,
    attended,
):
    low = tile_ref[0] % 2
    attended[low] = got_a[...]
    attended[1 - low] = got_b[...]
    ch = mid.shape[-1]
    above, below = edge_rows(tile_ref, pair_a, mid_a, pair_b, mid_b)
    wide = []
    for f in range(2):
        rows = [above[f].astype(bf16), mid[f, :cols, :], mid[f, cols:, :], below[f].astype(bf16)]
        wide += [jnp.concatenate(rows[r : r + 3], axis=1) for r in range(2)]
    here = dot32(jnp.concatenate(wide, axis=0), w[2])
    flag = usable_flag(clips, span_ref[0] * 2 + 1, 1).astype(f32)
    back = dot32(weigh(flag, jnp.concatenate(wide[:2], axis=0)), w[1])
    for r in range(2):
        part = slice(r * cols, (r + 1) * cols)
        out[0, part, :] = shift_add(here[part], cols, ch)
        after = here[(2 + r) * cols : (3 + r) * cols]
        out[1, part, :] = shift_add(after + back[part], cols, ch)


def finish_kernel(span_ref, own, link_got, core_got, out):
    span = span_ref[0]

    @pl.when(span == 0)
    def _():
        out[...] = own[...].astype(bf16)

    @pl.when(span % 2 == 1)
    def _():
        out[...] = (own[...] + core_got[...].astype(f32)).astype(bf16)

    @pl.when(jnp.logical_and(span % 2 == 0, span > 0))
    def _():
        out[...] = (own[...] + link_got[...].astype(f32)).astype(bf16)


def on_device(features, clip_lengths, norm_gain, w_qkv, w_out, conv_gain, w_conv):
    frames, row_count, cols, ch = features.shape
    tiles, spans = lax.axis_size("tile"), lax.axis_size("span")
    if tiles != 4 or spans % 2 or frames != 2 or row_count != 2:
        return general(features, clip_lengths, norm_gain, w_qkv, w_out, conv_gain, w_conv)
    cells = row_count * cols
    both = ("tile", "span")
    tile = lax.axis_index("tile").astype(jnp.int32).reshape(1)
    span = lax.axis_index("span").astype(jnp.int32).reshape(1)
    other_core = [(i, i ^ 1) for i in range(spans)]
    route_a, route_b = frame_route(spans, 0), frame_route(spans, 1)
    x = features.reshape(frames, cells, ch)
    send_a, send_b = call(
        pick_kernel,
        "pick",
        (pltpu.VMEM((cells, ch), bf16), pltpu.VMEM((cells, ch), bf16)),
        [SMEM, ANY],
        [pltpu.SemaphoreType.DMA((2,))],
        62,
    )(tile, x)
    own_a = lax.ppermute(send_a, both, route_a)
    own_b = lax.ppermute(send_b, both, route_b)
    w_qkv, w_out, norm_gain = call(
        load_small_kernel,
        "load_small",
        (pltpu.VMEM(w_qkv.shape, bf16), pltpu.VMEM(w_out.shape, bf16), pltpu.VMEM((ch,), f32)),
        [ANY, ANY, VMEM],
        [pltpu.SemaphoreType.DMA((2,))],
        60,
    )(w_qkv, w_out, norm_gain)
    own_a, w_qkv = lax.optimization_barrier((own_a, w_qkv))
    other_a = lax.ppermute(own_a, "span", other_core)
    other_b = lax.ppermute(own_b, "span", other_core)
    kv_flops = 2 * 2 * cells * ch * 2 * ch
    row_flops = 2 * cells * ch * (2 * ch + 8 * cells)
    kv_a = call(keys_kernel, "keys", struct((3 * cells, 2 * ch)), [VMEM] * 5, flops=kv_flops)(
        own_a, other_a, own_b, norm_gain, w_qkv
    )
    kv_b, att_a = call(
        attend_kernel,
        "attend",
        (struct((cells, 2 * ch)), struct((cells, ch))),
        [VMEM] * 6,
        flops=kv_flops + row_flops,
    )(other_b, own_a, kv_a, norm_gain, w_qkv, w_out)
    got_a = lax.ppermute(att_a, both, route_a)
    att_b = call(
        attend_rest_kernel,
        "attend_rest",
        struct((cells, ch)),
        [VMEM] * 6,
        flops=3 * row_flops,
    )(own_b, kv_a, kv_b, norm_gain, w_qkv, w_out)
    got_b = lax.ppermute(att_b, both, route_b)
    pairs, middle = [(0, 1), (1, 0), (2, 3), (3, 2)], [(1, 2), (2, 1)]
    one, edge = struct((cells, ch)), struct((cols, ch))
    sums = struct((frames, cells, ch), f32)
    unit = 2 * cells * 9 * ch * ch
    where = (tile, span, clip_lengths)
    w_packed = call(
        load_kernel,
        "load_conv",
        struct((3, 3 * ch, 3 * ch)),
        [ANY, ANY],
        [pltpu.SemaphoreType.DMA((27,))],
        42,
        size=1 << 12,
    )(att_b, w_conv)
    act_a, pair_edge, mid_edge = call(
        functools.partial(activate_a_kernel, cols), "activate_a", (one, edge, edge), [SMEM, VMEM, VMEM, ANY]
    )(tile, got_a, conv_gain, w_packed)
    pair_a = lax.ppermute(pair_edge, "tile", pairs)
    mid_a = lax.ppermute(mid_edge, "tile", middle)
    active, pair_edge, mid_edge = call(
        functools.partial(activate_b_kernel, cols),
        "activate_b",
        (struct((frames, cells, ch)), edge, edge),
        [SMEM] + [VMEM] * 3 + [ANY],
    )(tile, got_b, act_a, conv_gain, w_packed)
    pair_b = lax.ppermute(pair_edge, "tile", pairs)
    mid_b = lax.ppermute(mid_edge, "tile", middle)
    edges = (pair_a, mid_a, pair_b, mid_b)
    started = call(
        functools.partial(next_own_kernel, cols),
        "next_own",
        sums,
        [SMEM] * 2 + [VMEM] * 2,
        flops=2 * unit,
    )(span, clip_lengths, active, w_packed)
    rows_sum = pltpu.VMEM((frames, cols, ch), f32)
    pair_rows = call(
        functools.partial(pair_edge_kernel, cols),
        "pair_edge",
        struct((frames, cols, ch)),
        [SMEM] * 3 + [VMEM] * 4,
        [rows_sum],
        flops=unit // 2,
    )(*where, pair_a, pair_b, w_packed, started)
    for_next = call(
        functools.partial(mid_edge_kernel, cols),
        "mid_edge",
        struct((frames, cells, ch)),
        [SMEM] * 3 + [VMEM] * 5,
        [rows_sum],
        flops=unit // 2,
    )(*where, mid_a, mid_b, w_packed, started, pair_rows)
    link = [(s + d, s + 1 - d) for s in range(1, spans - 1, 2) for d in range(2)]
    link_got = lax.ppermute(for_next, "span", link)
    core_got = lax.ppermute(for_next, "span", other_core)
    own, attended = call(
        functools.partial(own_kernel, cols),
        "own",
        (sums, struct((frames, cells, ch))),
        [SMEM] * 3 + [VMEM] * 8,
        flops=3 * unit,
    )(*where, active, *edges, w_packed, got_a, got_b)
    hidden = call(
        finish_kernel, "finish", struct((frames, cells, ch)), [SMEM] + [VMEM] * 3
    )(span, own, link_got, core_got)
    shape = (frames, row_count, cols, ch)
    return attended.reshape(shape), hidden.reshape(shape)


def extended(x, sides, width):
    for axis, dim in sides:
        size, length = (lax.axis_size(axis), x.shape[dim])
        up = [(i, (i + 1) % size) for i in range(size - 1)]
        down = [(j, i) for i, j in up]
        last = lax.slice_in_dim(x, length - width, length, axis=dim)
        first = lax.slice_in_dim(x, 0, width, axis=dim)
        before = lax.ppermute(last, axis, up)
        after = lax.ppermute(first, axis, down)
        x = jnp.concatenate([before, x, after], axis=dim)
    return x


def general(features, clip_lengths, norm_gain, w_qkv, w_out, conv_gain, w_conv):
    frames, row_count, col_count, channels = features.shape
    cell_count = row_count * col_count
    normed_grid = rms_scale(features, norm_gain).astype(jnp.bfloat16)
    view_frames = normed_grid.shape[0]
    view_cells = normed_grid.shape[1] * normed_grid.shape[2]
    normed = normed_grid.reshape(view_frames, view_cells, channels)
    queries = jnp.dot(
        normed.reshape(-1, channels), w_qkv[:, :channels], preferred_element_type=jnp.float32
    )
    queries = queries.astype(jnp.bfloat16).reshape(view_frames, view_cells, channels)
    kv_weight = w_qkv[:, channels:]
    score_scale = channels ** (-0.5)
    outgoing = jnp.dot(normed.reshape(-1, channels), kv_weight, preferred_element_type=jnp.float32)
    outgoing = outgoing.astype(jnp.bfloat16).reshape(view_frames, view_cells, 2 * channels)
    portion = lax.all_gather(outgoing, "tile", axis=1, tiled=True)
    key_part = portion[:, :, :channels]
    value_part = portion[:, :, channels:]
    row_top = jnp.full((view_frames, view_cells, 1), -1e30, jnp.float32)
    scores = (
        jnp.einsum("fqc,fkc->fqk", queries, key_part, preferred_element_type=jnp.float32)
        * score_scale
    )
    new_top = jnp.maximum(row_top, jnp.max(scores, axis=2, keepdims=True))
    raised_f = jnp.exp(scores - new_top)
    row_total = jnp.sum(raised_f, axis=2, keepdims=True)
    weighted = jnp.einsum(
        "fqk,fkc->fqc",
        raised_f.astype(jnp.bfloat16),
        value_part,
        preferred_element_type=jnp.float32,
    )
    mixture_grid = (weighted / row_total).astype(jnp.bfloat16)
    mixture = mixture_grid.reshape(-1, channels)
    projected = jnp.dot(mixture, w_out, preferred_element_type=jnp.float32)
    attended = (features.reshape(-1, channels).astype(jnp.float32) + projected).astype(jnp.bfloat16)
    attended = attended.reshape(frames, row_count, col_count, channels)
    lifted = rms_scale(attended, conv_gain)
    activated = (lifted * jax.nn.sigmoid(lifted)).astype(jnp.bfloat16)
    earlier = from_behind(activated, "span", 1)
    stacked = jnp.concatenate([earlier, activated], axis=0)
    edged = extended(stacked, (("tile", 1),), 1)
    padded = jnp.pad(edged, ((0, 0), (0, 0), (1, 1), (0, 0)))
    clip_ends = jnp.cumsum(clip_lengths)
    position = lax.axis_index("span") * frames + jnp.arange(frames, dtype=jnp.int32)
    clip_start = jnp.sum(
        jnp.where(clip_ends[None, :] <= position[:, None], clip_lengths[None, :], 0), axis=1
    )
    summed = jnp.zeros((frames * cell_count, channels), jnp.float32)
    for t_tap in range(3):
        usable = position - (2 - t_tap) >= clip_start
        for r_tap in range(3):
            for c_tap in range(3):
                shifted = padded[
                    t_tap : t_tap + frames, r_tap : r_tap + row_count, c_tap : c_tap + col_count
                ]
                shifted = jnp.where(
                    usable[:, None, None, None], shifted, jnp.zeros((), shifted.dtype)
                )
                summed = summed + jnp.dot(
                    shifted.reshape(-1, channels),
                    w_conv[t_tap, r_tap, c_tap],
                    preferred_element_type=jnp.float32,
                )
    hidden = summed.astype(jnp.bfloat16).reshape(frames, row_count, col_count, channels)
    return (attended, hidden)


def solution(mesh):
    in_specs = (P(("grp", "span"), "tile", None, None), P("grp"), P(), P(), P(), P(), P())
    out_specs = (P(("grp", "span"), "tile", None, None), P(("grp", "span"), "tile", None, None))
    return jax.shard_map(
        on_device, mesh=mesh, in_specs=in_specs, out_specs=out_specs, check_vma=False
    )
```

```python
import functools

import jax
import jax.numpy as jnp
from jax import lax
from jax.experimental import pallas as pl
from jax.experimental.pallas import tpu as pltpu
from jax.sharding import PartitionSpec as P

eps = 1e-06
f32, bf16 = jnp.float32, jnp.bfloat16
LOG2E = 1.4426950408889634
VMEM = pl.BlockSpec(memory_space=pltpu.VMEM)
SMEM = pl.BlockSpec(memory_space=pltpu.SMEM)
ANY = pl.BlockSpec(memory_space=pl.ANY)


def from_behind(block, axis, distance):
    devices = range(lax.axis_size(axis))
    route = [(i - distance, i) for i in devices if i - distance in devices]
    return lax.ppermute(block, axis, route)


def rms_scale(values, gain_vec):
    as_float = values.astype(f32)
    return (
        as_float * lax.rsqrt(jnp.mean(as_float * as_float, axis=-1, keepdims=True) + eps) * gain_vec
    )


def dot32(a, b):
    return jnp.dot(a, b, preferred_element_type=f32)


def struct(shape, dtype=bf16):
    return jax.ShapeDtypeStruct(shape, dtype)


def call(kernel, name, out_shape, in_specs, scratch=(), limit=16, flops=0, size=1 << 20):
    outs = jax.tree.map(lambda _: VMEM, out_shape)
    cost = pl.CostEstimate(flops=int(flops), transcendentals=0, bytes_accessed=int(size))
    return pl.pallas_call(
        kernel,
        out_shape=out_shape,
        in_specs=in_specs,
        out_specs=outs,
        scratch_shapes=list(scratch),
        compiler_params=pltpu.CompilerParams(vmem_limit_bytes=limit << 20),
        cost_estimate=cost,
        name=name,
    )


def frame_route(spans, flip):
    route = []
    for tile in range(4):
        for span in range(spans):
            high, low, column, core = tile // 2, tile % 2, span // 2, span % 2
            there = (2 * core + (low ^ flip)) * spans + 2 * column + high
            route.append((tile * spans + span, there))
    return route


def pick_kernel(tile_ref, x_hbm, first, second, sem):
    low = tile_ref[0] % 2

    def move(a, b):
        copies = [
            pltpu.make_async_copy(x_hbm.at[a], first, sem.at[0]),
            pltpu.make_async_copy(x_hbm.at[b], second, sem.at[1]),
        ]
        for copy in copies:
            copy.start()
        for copy in copies:
            copy.wait()

    @pl.when(low == 0)
    def _():
        move(0, 1)

    @pl.when(low == 1)
    def _():
        move(1, 0)


def load_small_kernel(w_qkv, w_out, gain, qkv_vm, out_vm, gain_vm, sem):
    copies = [
        pltpu.make_async_copy(w_qkv, qkv_vm, sem.at[0]),
        pltpu.make_async_copy(w_out, out_vm, sem.at[1]),
    ]
    for copy in copies:
        copy.start()
    gain_vm[...] = gain[...]
    for copy in copies:
        copy.wait()


def project_keys(block, gain_vec, w_qkv, out, place):
    cells, ch = block.shape
    normed = rms_scale(block[...], gain_vec).astype(bf16)
    out[place * cells : (place + 1) * cells, :] = dot32(normed, w_qkv[:, ch:]).astype(bf16)


def keys_kernel(own_a, other_a, own_b, gain, w_qkv, kv_out, q_out):
    cells, ch = own_a.shape
    gain_vec = gain[...].reshape(1, ch)
    project_keys(other_a, gain_vec, w_qkv, kv_out, 1)
    for place, block in ((0, own_a), (2, own_b)):
        normed = rms_scale(block[...], gain_vec).astype(bf16)
        qkv = dot32(normed, w_qkv[...]).astype(bf16)
        q_out[place // 2] = qkv[:, :ch]
        kv_out[place * cells : (place + 1) * cells, :] = qkv[:, ch:]


def attend_rows(source, queries, kv_parts, w_out, att_out):
    ch = source.shape[1]
    scores = [
        lax.dot_general(
            queries, kv[:, :ch], (((1,), (1,)), ((), ())), preferred_element_type=f32
        )
        * (ch ** (-0.5) * LOG2E)
        for kv in kv_parts
    ]
    top = functools.reduce(jnp.maximum, [jnp.max(s, axis=1, keepdims=True) for s in scores])
    raised = [jnp.exp2(s - top) for s in scores]
    total = sum(jnp.sum(r, axis=1, keepdims=True) for r in raised)
    mixed = sum(dot32(r.astype(bf16), kv[:, ch:]) for r, kv in zip(raised, kv_parts))
    mixture = (mixed / total).astype(bf16)
    att_out[...] = (source[...].astype(f32) + dot32(mixture, w_out[...])).astype(bf16)


def attend_kernel(other_b, own_a, queries, kv_a, gain, w_qkv, w_out, kv_b, att_a):
    project_keys(other_b, gain[...].reshape(1, own_a.shape[1]), w_qkv, kv_b, 0)
    attend_rows(own_a, queries[0], (kv_a, kv_b), w_out, att_a)


def attend_rest_kernel(own_b, queries, kv_a, kv_b, w_out, att_b):
    attend_rows(own_b, queries[1], (kv_a, kv_b), w_out, att_b)


def load_kernel(_, w_hbm, w_vm, sem):
    ch = w_hbm.shape[-1]
    copies = [
        pltpu.make_async_copy(
            w_hbm.at[i, j, k],
            w_vm.at[i, j * ch : (j + 1) * ch, k * ch : (k + 1) * ch],
            sem.at[9 * i + 3 * j + k],
        )
        for i in range(3)
        for j in range(3)
        for k in range(3)
    ]
    for copy in copies:
        copy.start()
    for copy in copies:
        copy.wait()


def activate(cols, low, block, gain, act_out, pair_edge, mid_edge):
    lifted = rms_scale(block[...], gain[...].reshape(1, block.shape[1]))
    act = (lifted / (1.0 + jnp.exp(-lifted))).astype(bf16)
    act_out[...] = act

    @pl.when(low == 0)
    def _():
        pair_edge[...] = act[cols:, :]
        mid_edge[...] = act[:cols, :]

    @pl.when(low == 1)
    def _():
        pair_edge[...] = act[:cols, :]
        mid_edge[...] = act[cols:, :]


def activate_a_kernel(cols, tile_ref, got_a, gain, _, *outs):
    activate(cols, tile_ref[0] % 2, got_a, gain, *outs)


def activate_b_kernel(cols, tile_ref, got_b, act_a, gain, _, active, pair_edge, mid_edge):
    low = tile_ref[0] % 2
    activate(cols, low, got_b, gain, active.at[1 - low], pair_edge, mid_edge)
    active[low] = act_a[...]


def usable_flag(clips, frame_at, tap):
    end = jnp.int32(0)
    start = jnp.int32(0)
    for i in range(clips.shape[0]):
        end = end + clips[i]
        start = start + jnp.where(end <= frame_at, clips[i], 0)
    return frame_at - (2 - tap) >= start


def shift_add(part, cols, ch):
    at = lax.broadcasted_iota(jnp.int32, (cols, ch), 0)
    left = jnp.where(at == 0, 0.0, pltpu.roll(part[:, :ch], 1, 0))
    right = jnp.where(at == cols - 1, 0.0, pltpu.roll(part[:, 2 * ch :], cols - 1, 0))
    return part[:, ch : 2 * ch] + left + right


def weigh(flag, block):
    return (block.astype(f32) * flag).astype(bf16)


def flags_of(clips, frame_at):
    return [
        [usable_flag(clips, frame_at + f, tap).astype(f32) for tap in range(3)] for f in range(2)
    ]


def edge_rows(tile_ref, pair_a, mid_a, pair_b, mid_b):
    odd = (tile_ref[0] % 2).astype(f32)

    def pick(if_odd, if_even):
        return if_odd[...].astype(f32) * odd + if_even[...].astype(f32) * (1.0 - odd)

    above = [pick(pair_a, mid_b), pick(pair_b, mid_a)]
    below = [pick(mid_a, pair_b), pick(mid_b, pair_a)]
    return above, below


def next_own_kernel(cols, span_ref, clips, mid, w, out):
    ch = mid.shape[-1]
    flag = flags_of(clips, (span_ref[0] + 1) * 2)
    use_far, use_near = flag[0][0] + flag[1][0] > 0.0, flag[0][1] > 0.0
    parts = ((slice(0, cols), slice(ch, 3 * ch)), (slice(cols, 2 * cols), slice(0, 2 * ch)))

    def pair(f):
        return jnp.concatenate([mid[f, :cols, :], mid[f, cols:, :]], axis=1)

    @pl.when(use_far)
    def _():
        last = jnp.concatenate([weigh(flag[f][0], pair(f)) for f in range(2)], axis=0)
        for part, taps in parts:
            far = dot32(last, w[0, taps])
            out[0, part, :] = shift_add(far[:cols], cols, ch)
            out[1, part, :] = shift_add(far[cols:], cols, ch)

    @pl.when(jnp.logical_not(use_far))
    def _():
        out[...] = jnp.zeros_like(out)

    @pl.when(use_near)
    def _():
        middle = pair(1)
        for part, taps in parts:
            out[0, part, :] += shift_add(dot32(middle, w[1, taps]), cols, ch)


def edge_part(cols, flag, first, second, above, w, partial, total):
    ch = w.shape[-1] // 3
    part = slice(0, cols) if above else slice(cols, 2 * cols)
    taps = slice(0, ch) if above else slice(2 * ch, 3 * ch)
    total[...] = partial[:, part, :]

    @pl.when(flag[0][0] + flag[1][0] > 0.0)
    def _():
        last = jnp.concatenate(
            [weigh(flag[0][0], first[...]), weigh(flag[1][0], second[...])], axis=0
        )
        far = dot32(last, w[0, taps])
        total[0] += shift_add(far[:cols], cols, ch)
        total[1] += shift_add(far[cols:], cols, ch)

    @pl.when(flag[0][1] > 0.0)
    def _():
        total[0] += shift_add(dot32(second[...], w[1, taps]), cols, ch)


def pair_edge_kernel(cols, tile_ref, span_ref, clips, pair_a, pair_b, w, partial, out, total):
    flag = flags_of(clips, (span_ref[0] + 1) * 2)

    @pl.when(tile_ref[0] % 2 == 1)
    def _():
        edge_part(cols, flag, pair_a, pair_b, True, w, partial, total)

    @pl.when(tile_ref[0] % 2 == 0)
    def _():
        edge_part(cols, flag, pair_b, pair_a, False, w, partial, total)

    out[...] = total[...].astype(bf16)


def mid_edge_kernel(
    cols, tile_ref, span_ref, clips, mid_a, mid_b, w, partial, pair_rows, out, total
):
    flag = flags_of(clips, (span_ref[0] + 1) * 2)

    @pl.when(tile_ref[0] % 2 == 1)
    def _():
        edge_part(cols, flag, mid_a, mid_b, False, w, partial, total)
        out[:, :cols, :] = pair_rows[...]
        out[:, cols:, :] = total[...].astype(bf16)

    @pl.when(tile_ref[0] % 2 == 0)
    def _():
        edge_part(cols, flag, mid_b, mid_a, True, w, partial, total)
        out[:, cols:, :] = pair_rows[...]
        out[:, :cols, :] = total[...].astype(bf16)


def own_kernel(
    cols,
    tile_ref,
    span_ref,
    clips,
    mid,
    pair_a,
    mid_a,
    pair_b,
    mid_b,
    w,
    got_a,
    got_b,
    out,
    attended,
):
    low = tile_ref[0] % 2
    attended[low] = got_a[...]
    attended[1 - low] = got_b[...]
    ch = mid.shape[-1]
    above, below = edge_rows(tile_ref, pair_a, mid_a, pair_b, mid_b)
    wide = []
    for f in range(2):
        rows = [above[f].astype(bf16), mid[f, :cols, :], mid[f, cols:, :], below[f].astype(bf16)]
        wide += [jnp.concatenate(rows[r : r + 3], axis=1) for r in range(2)]
    here = dot32(jnp.concatenate(wide, axis=0), w[2])
    flag = usable_flag(clips, span_ref[0] * 2 + 1, 1).astype(f32)
    back = dot32(weigh(flag, jnp.concatenate(wide[:2], axis=0)), w[1])
    for r in range(2):
        part = slice(r * cols, (r + 1) * cols)
        out[0, part, :] = shift_add(here[part], cols, ch)
        after = here[(2 + r) * cols : (3 + r) * cols]
        out[1, part, :] = shift_add(after + back[part], cols, ch)


def finish_kernel(span_ref, own, link_got, core_got, out):
    span = span_ref[0]

    @pl.when(span == 0)
    def _():
        out[...] = own[...].astype(bf16)

    @pl.when(span % 2 == 1)
    def _():
        out[...] = (own[...] + core_got[...].astype(f32)).astype(bf16)

    @pl.when(jnp.logical_and(span % 2 == 0, span > 0))
    def _():
        out[...] = (own[...] + link_got[...].astype(f32)).astype(bf16)


def on_device(features, clip_lengths, norm_gain, w_qkv, w_out, conv_gain, w_conv):
    frames, row_count, cols, ch = features.shape
    tiles, spans = lax.axis_size("tile"), lax.axis_size("span")
    if tiles != 4 or spans % 2 or frames != 2 or row_count != 2:
        return general(features, clip_lengths, norm_gain, w_qkv, w_out, conv_gain, w_conv)
    cells = row_count * cols
    both = ("tile", "span")
    tile = lax.axis_index("tile").astype(jnp.int32).reshape(1)
    span = lax.axis_index("span").astype(jnp.int32).reshape(1)
    other_core = [(i, i ^ 1) for i in range(spans)]
    route_a, route_b = frame_route(spans, 0), frame_route(spans, 1)
    x = features.reshape(frames, cells, ch)
    send_a, send_b = call(
        pick_kernel,
        "pick",
        (pltpu.VMEM((cells, ch), bf16), pltpu.VMEM((cells, ch), bf16)),
        [SMEM, ANY],
        [pltpu.SemaphoreType.DMA((2,))],
        62,
    )(tile, x)
    own_a = lax.ppermute(send_a, both, route_a)
    own_b = lax.ppermute(send_b, both, route_b)
    w_qkv, w_out, norm_gain = call(
        load_small_kernel,
        "load_small",
        (pltpu.VMEM(w_qkv.shape, bf16), pltpu.VMEM(w_out.shape, bf16), pltpu.VMEM((ch,), f32)),
        [ANY, ANY, VMEM],
        [pltpu.SemaphoreType.DMA((2,))],
        60,
    )(w_qkv, w_out, norm_gain)
    own_a, w_qkv = lax.optimization_barrier((own_a, w_qkv))
    other_a = lax.ppermute(own_a, "span", other_core)
    other_b = lax.ppermute(own_b, "span", other_core)
    kv_flops = 2 * 2 * cells * ch * 2 * ch
    row_flops = 2 * cells * ch * (2 * ch + 8 * cells)
    kv_a, queries = call(
        keys_kernel,
        "keys",
        (struct((3 * cells, 2 * ch)), struct((2, cells, ch))),
        [VMEM] * 5,
        flops=kv_flops,
    )(own_a, other_a, own_b, norm_gain, w_qkv)
    kv_b, att_a = call(
        attend_kernel,
        "attend",
        (struct((cells, 2 * ch)), struct((cells, ch))),
        [VMEM] * 7,
        flops=kv_flops + row_flops,
    )(other_b, own_a, queries, kv_a, norm_gain, w_qkv, w_out)
    got_a = lax.ppermute(att_a, both, route_a)
    att_b = call(
        attend_rest_kernel, "attend_rest", struct((cells, ch)), [VMEM] * 5, flops=3 * row_flops
    )(own_b, queries, kv_a, kv_b, w_out)
    got_b = lax.ppermute(att_b, both, route_b)
    pairs, middle = [(0, 1), (1, 0), (2, 3), (3, 2)], [(1, 2), (2, 1)]
    one, edge = struct((cells, ch)), struct((cols, ch))
    sums = struct((frames, cells, ch), f32)
    unit = 2 * cells * 9 * ch * ch
    where = (tile, span, clip_lengths)
    w_packed = call(
        load_kernel,
        "load_conv",
        struct((3, 3 * ch, 3 * ch)),
        [ANY, ANY],
        [pltpu.SemaphoreType.DMA((27,))],
        42,
        size=1 << 12,
    )(att_b, w_conv)
    act_a, pair_edge, mid_edge = call(
        functools.partial(activate_a_kernel, cols), "activate_a", (one, edge, edge), [SMEM, VMEM, VMEM, ANY]
    )(tile, got_a, conv_gain, w_packed)
    pair_a = lax.ppermute(pair_edge, "tile", pairs)
    mid_a = lax.ppermute(mid_edge, "tile", middle)
    active, pair_edge, mid_edge = call(
        functools.partial(activate_b_kernel, cols),
        "activate_b",
        (struct((frames, cells, ch)), edge, edge),
        [SMEM] + [VMEM] * 3 + [ANY],
    )(tile, got_b, act_a, conv_gain, w_packed)
    pair_b = lax.ppermute(pair_edge, "tile", pairs)
    mid_b = lax.ppermute(mid_edge, "tile", middle)
    edges = (pair_a, mid_a, pair_b, mid_b)
    started = call(
        functools.partial(next_own_kernel, cols),
        "next_own",
        sums,
        [SMEM] * 2 + [VMEM] * 2,
        flops=2 * unit,
    )(span, clip_lengths, active, w_packed)
    rows_sum = pltpu.VMEM((frames, cols, ch), f32)
    pair_rows = call(
        functools.partial(pair_edge_kernel, cols),
        "pair_edge",
        struct((frames, cols, ch)),
        [SMEM] * 3 + [VMEM] * 4,
        [rows_sum],
        flops=unit // 2,
    )(*where, pair_a, pair_b, w_packed, started)
    for_next = call(
        functools.partial(mid_edge_kernel, cols),
        "mid_edge",
        struct((frames, cells, ch)),
        [SMEM] * 3 + [VMEM] * 5,
        [rows_sum],
        flops=unit // 2,
    )(*where, mid_a, mid_b, w_packed, started, pair_rows)
    link = [(s + d, s + 1 - d) for s in range(1, spans - 1, 2) for d in range(2)]
    link_got = lax.ppermute(for_next, "span", link)
    core_got = lax.ppermute(for_next, "span", other_core)
    own, attended = call(
        functools.partial(own_kernel, cols),
        "own",
        (sums, struct((frames, cells, ch))),
        [SMEM] * 3 + [VMEM] * 8,
        flops=3 * unit,
    )(*where, active, *edges, w_packed, got_a, got_b)
    hidden = call(
        finish_kernel, "finish", struct((frames, cells, ch)), [SMEM] + [VMEM] * 3
    )(span, own, link_got, core_got)
    shape = (frames, row_count, cols, ch)
    return attended.reshape(shape), hidden.reshape(shape)


def extended(x, sides, width):
    for axis, dim in sides:
        size, length = (lax.axis_size(axis), x.shape[dim])
        up = [(i, (i + 1) % size) for i in range(size - 1)]
        down = [(j, i) for i, j in up]
        last = lax.slice_in_dim(x, length - width, length, axis=dim)
        first = lax.slice_in_dim(x, 0, width, axis=dim)
        before = lax.ppermute(last, axis, up)
        after = lax.ppermute(first, axis, down)
        x = jnp.concatenate([before, x, after], axis=dim)
    return x


def general(features, clip_lengths, norm_gain, w_qkv, w_out, conv_gain, w_conv):
    frames, row_count, col_count, channels = features.shape
    cell_count = row_count * col_count
    normed_grid = rms_scale(features, norm_gain).astype(jnp.bfloat16)
    view_frames = normed_grid.shape[0]
    view_cells = normed_grid.shape[1] * normed_grid.shape[2]
    normed = normed_grid.reshape(view_frames, view_cells, channels)
    queries = jnp.dot(
        normed.reshape(-1, channels), w_qkv[:, :channels], preferred_element_type=jnp.float32
    )
    queries = queries.astype(jnp.bfloat16).reshape(view_frames, view_cells, channels)
    kv_weight = w_qkv[:, channels:]
    score_scale = channels ** (-0.5)
    outgoing = jnp.dot(normed.reshape(-1, channels), kv_weight, preferred_element_type=jnp.float32)
    outgoing = outgoing.astype(jnp.bfloat16).reshape(view_frames, view_cells, 2 * channels)
    portion = lax.all_gather(outgoing, "tile", axis=1, tiled=True)
    key_part = portion[:, :, :channels]
    value_part = portion[:, :, channels:]
    row_top = jnp.full((view_frames, view_cells, 1), -1e30, jnp.float32)
    scores = (
        jnp.einsum("fqc,fkc->fqk", queries, key_part, preferred_element_type=jnp.float32)
        * score_scale
    )
    new_top = jnp.maximum(row_top, jnp.max(scores, axis=2, keepdims=True))
    raised_f = jnp.exp(scores - new_top)
    row_total = jnp.sum(raised_f, axis=2, keepdims=True)
    weighted = jnp.einsum(
        "fqk,fkc->fqc",
        raised_f.astype(jnp.bfloat16),
        value_part,
        preferred_element_type=jnp.float32,
    )
    mixture_grid = (weighted / row_total).astype(jnp.bfloat16)
    mixture = mixture_grid.reshape(-1, channels)
    projected = jnp.dot(mixture, w_out, preferred_element_type=jnp.float32)
    attended = (features.reshape(-1, channels).astype(jnp.float32) + projected).astype(jnp.bfloat16)
    attended = attended.reshape(frames, row_count, col_count, channels)
    lifted = rms_scale(attended, conv_gain)
    activated = (lifted * jax.nn.sigmoid(lifted)).astype(jnp.bfloat16)
    earlier = from_behind(activated, "span", 1)
    stacked = jnp.concatenate([earlier, activated], axis=0)
    edged = extended(stacked, (("tile", 1),), 1)
    padded = jnp.pad(edged, ((0, 0), (0, 0), (1, 1), (0, 0)))
    clip_ends = jnp.cumsum(clip_lengths)
    position = lax.axis_index("span") * frames + jnp.arange(frames, dtype=jnp.int32)
    clip_start = jnp.sum(
        jnp.where(clip_ends[None, :] <= position[:, None], clip_lengths[None, :], 0), axis=1
    )
    summed = jnp.zeros((frames * cell_count, channels), jnp.float32)
    for t_tap in range(3):
        usable = position - (2 - t_tap) >= clip_start
        for r_tap in range(3):
            for c_tap in range(3):
                shifted = padded[
                    t_tap : t_tap + frames, r_tap : r_tap + row_count, c_tap : c_tap + col_count
                ]
                shifted = jnp.where(
                    usable[:, None, None, None], shifted, jnp.zeros((), shifted.dtype)
                )
                summed = summed + jnp.dot(
                    shifted.reshape(-1, channels),
                    w_conv[t_tap, r_tap, c_tap],
                    preferred_element_type=jnp.float32,
                )
    hidden = summed.astype(jnp.bfloat16).reshape(frames, row_count, col_count, channels)
    return (attended, hidden)


def solution(mesh):
    in_specs = (P(("grp", "span"), "tile", None, None), P("grp"), P(), P(), P(), P(), P())
    out_specs = (P(("grp", "span"), "tile", None, None), P(("grp", "span"), "tile", None, None))
    return jax.shard_map(
        on_device, mesh=mesh, in_specs=in_specs, out_specs=out_specs, check_vma=False
    )
```

```python
import functools

import jax
import jax.numpy as jnp
from jax import lax
from jax.experimental import pallas as pl
from jax.experimental.pallas import tpu as pltpu
from jax.sharding import PartitionSpec as P

eps = 1e-06
f32, bf16 = jnp.float32, jnp.bfloat16
LOG2E = 1.4426950408889634
VMEM = pl.BlockSpec(memory_space=pltpu.VMEM)
SMEM = pl.BlockSpec(memory_space=pltpu.SMEM)
ANY = pl.BlockSpec(memory_space=pl.ANY)


def from_behind(block, axis, distance):
    devices = range(lax.axis_size(axis))
    route = [(i - distance, i) for i in devices if i - distance in devices]
    return lax.ppermute(block, axis, route)


def rms_scale(values, gain_vec):
    as_float = values.astype(f32)
    return (
        as_float * lax.rsqrt(jnp.mean(as_float * as_float, axis=-1, keepdims=True) + eps) * gain_vec
    )


def dot32(a, b):
    return jnp.dot(a, b, preferred_element_type=f32)


def struct(shape, dtype=bf16):
    return jax.ShapeDtypeStruct(shape, dtype)


def call(kernel, name, out_shape, in_specs, scratch=(), limit=16, flops=0, size=1 << 20):
    outs = jax.tree.map(lambda _: VMEM, out_shape)
    cost = pl.CostEstimate(flops=int(flops), transcendentals=0, bytes_accessed=int(size))
    return pl.pallas_call(
        kernel,
        out_shape=out_shape,
        in_specs=in_specs,
        out_specs=outs,
        scratch_shapes=list(scratch),
        compiler_params=pltpu.CompilerParams(vmem_limit_bytes=limit << 20),
        cost_estimate=cost,
        name=name,
    )


def frame_route(spans, flip):
    route = []
    for tile in range(4):
        for span in range(spans):
            high, low, column, core = tile // 2, tile % 2, span // 2, span % 2
            there = (2 * core + (low ^ flip)) * spans + 2 * column + high
            route.append((tile * spans + span, there))
    return route


def pick_kernel(tile_ref, x_hbm, first, second, sem):
    low = tile_ref[0] % 2

    def move(a, b):
        copies = [
            pltpu.make_async_copy(x_hbm.at[a], first, sem.at[0]),
            pltpu.make_async_copy(x_hbm.at[b], second, sem.at[1]),
        ]
        for copy in copies:
            copy.start()
        for copy in copies:
            copy.wait()

    @pl.when(low == 0)
    def _():
        move(0, 1)

    @pl.when(low == 1)
    def _():
        move(1, 0)


def load_small_kernel(w_qkv, w_out, gain, qkv_vm, out_vm, gain_vm, sem):
    copies = [
        pltpu.make_async_copy(w_qkv, qkv_vm, sem.at[0]),
        pltpu.make_async_copy(w_out, out_vm, sem.at[1]),
    ]
    for copy in copies:
        copy.start()
    gain_vm[...] = gain[...]
    for copy in copies:
        copy.wait()


def project_keys(block, gain_vec, w_qkv, out, place):
    cells, ch = block.shape
    normed = rms_scale(block[...], gain_vec).astype(bf16)
    out[place * cells : (place + 1) * cells, :] = dot32(normed, w_qkv[:, ch:]).astype(bf16)


def keys_kernel(own_a, other_a, own_b, gain, w_qkv, kv_out, q_out):
    cells, ch = own_a.shape
    gain_vec = gain[...].reshape(1, ch)
    project_keys(other_a, gain_vec, w_qkv, kv_out, 1)
    for place, block in ((0, own_a), (2, own_b)):
        normed = rms_scale(block[...], gain_vec).astype(bf16)
        qkv = dot32(normed, w_qkv[...]).astype(bf16)
        q_out[place // 2] = qkv[:, :ch]
        kv_out[place * cells : (place + 1) * cells, :] = qkv[:, ch:]


def attend_rows(source, queries, kv_parts, w_out, att_out):
    ch = source.shape[1]
    scores = [
        lax.dot_general(
            queries, kv[:, :ch], (((1,), (1,)), ((), ())), preferred_element_type=f32
        )
        * (ch ** (-0.5) * LOG2E)
        for kv in kv_parts
    ]
    top = functools.reduce(jnp.maximum, [jnp.max(s, axis=1, keepdims=True) for s in scores])
    raised = [jnp.exp2(s - top) for s in scores]
    total = sum(jnp.sum(r, axis=1, keepdims=True) for r in raised)
    mixed = sum(dot32(r.astype(bf16), kv[:, ch:]) for r, kv in zip(raised, kv_parts))
    mixture = (mixed / total).astype(bf16)
    att_out[...] = (source[...].astype(f32) + dot32(mixture, w_out[...])).astype(bf16)


def attend_kernel(other_b, own_a, queries, kv_a, gain, w_qkv, w_out, kv_b, att_a):
    project_keys(other_b, gain[...].reshape(1, own_a.shape[1]), w_qkv, kv_b, 0)
    attend_rows(own_a, queries[0], (kv_a, kv_b), w_out, att_a)


def attend_rest_kernel(own_b, queries, kv_a, kv_b, w_out, att_b):
    attend_rows(own_b, queries[1], (kv_a, kv_b), w_out, att_b)


def load_kernel(_, w_hbm, w_vm, sem):
    ch = w_hbm.shape[-1]
    copies = [
        pltpu.make_async_copy(
            w_hbm.at[i, j, k],
            w_vm.at[i, j * ch : (j + 1) * ch, k * ch : (k + 1) * ch],
            sem.at[9 * i + 3 * j + k],
        )
        for i in range(3)
        for j in range(3)
        for k in range(3)
    ]
    for copy in copies:
        copy.start()
    for copy in copies:
        copy.wait()


def activate(cols, low, block, gain, act_out, pair_edge, mid_edge):
    lifted = rms_scale(block[...], gain[...].reshape(1, block.shape[1]))
    act = (lifted / (1.0 + jnp.exp(-lifted))).astype(bf16)
    act_out[...] = act

    @pl.when(low == 0)
    def _():
        pair_edge[...] = act[cols:, :]
        mid_edge[...] = act[:cols, :]

    @pl.when(low == 1)
    def _():
        pair_edge[...] = act[:cols, :]
        mid_edge[...] = act[cols:, :]


def activate_a_kernel(cols, tile_ref, got_a, gain, _, *outs):
    activate(cols, tile_ref[0] % 2, got_a, gain, *outs)


def activate_b_kernel(cols, tile_ref, got_b, act_a, gain, _, active, pair_edge, mid_edge):
    low = tile_ref[0] % 2
    activate(cols, low, got_b, gain, active.at[1 - low], pair_edge, mid_edge)
    active[low] = act_a[...]


def usable_flag(clips, frame_at, tap):
    end = jnp.int32(0)
    start = jnp.int32(0)
    for i in range(clips.shape[0]):
        end = end + clips[i]
        start = start + jnp.where(end <= frame_at, clips[i], 0)
    return frame_at - (2 - tap) >= start


def shift_add(part, cols, ch):
    at = lax.broadcasted_iota(jnp.int32, (cols, ch), 0)
    left = jnp.where(at == 0, 0.0, pltpu.roll(part[:, :ch], 1, 0))
    right = jnp.where(at == cols - 1, 0.0, pltpu.roll(part[:, 2 * ch :], cols - 1, 0))
    return part[:, ch : 2 * ch] + left + right


def weigh(flag, block):
    return (block.astype(f32) * flag).astype(bf16)


def flags_of(clips, frame_at):
    return [
        [usable_flag(clips, frame_at + f, tap).astype(f32) for tap in range(3)] for f in range(2)
    ]


def edge_rows(tile_ref, pair_a, mid_a, pair_b, mid_b):
    odd = (tile_ref[0] % 2).astype(f32)

    def pick(if_odd, if_even):
        return if_odd[...].astype(f32) * odd + if_even[...].astype(f32) * (1.0 - odd)

    above = [pick(pair_a, mid_b), pick(pair_b, mid_a)]
    below = [pick(mid_a, pair_b), pick(mid_b, pair_a)]
    return above, below


def next_own_kernel(cols, span_ref, clips, mid, w, out):
    ch = mid.shape[-1]
    flag = flags_of(clips, (span_ref[0] + 1) * 2)
    first_row, second_row = slice(0, cols), slice(cols, 2 * cols)
    pair = [
        jnp.concatenate([mid[f, first_row, :], mid[f, second_row, :]], axis=1) for f in range(2)
    ]
    last = jnp.concatenate([weigh(flag[0][0], pair[0]), weigh(flag[1][0], pair[1])], axis=0)
    middle = weigh(flag[0][1], pair[1])
    for part, taps in ((first_row, slice(ch, 3 * ch)), (second_row, slice(0, 2 * ch))):
        far = dot32(last, w[0, taps])
        out[0, part, :] = shift_add(far[:cols] + dot32(middle, w[1, taps]), cols, ch)
        out[1, part, :] = shift_add(far[cols:], cols, ch)


def next_edge_kernel(
    cols, tile_ref, span_ref, clips, pair_a, mid_a, pair_b, mid_b, w, partial, out
):
    ch = w.shape[-1] // 3
    flag = flags_of(clips, (span_ref[0] + 1) * 2)
    above, below = edge_rows(tile_ref, pair_a, mid_a, pair_b, mid_b)
    for edge, part, taps in (
        (above, slice(0, cols), slice(0, ch)),
        (below, slice(cols, 2 * cols), slice(2 * ch, 3 * ch)),
    ):
        last = jnp.concatenate([edge[0] * flag[0][0], edge[1] * flag[1][0]], axis=0).astype(bf16)
        middle = (edge[1] * flag[0][1]).astype(bf16)
        far = dot32(last, w[0, taps])
        near = far[:cols] + dot32(middle, w[1, taps])
        for f, val in ((0, near), (1, far[cols:])):
            out[f, part, :] = (shift_add(val, cols, ch) + partial[f, part, :]).astype(bf16)


def own_kernel(
    cols,
    tile_ref,
    span_ref,
    clips,
    mid,
    pair_a,
    mid_a,
    pair_b,
    mid_b,
    w,
    got_a,
    got_b,
    out,
    attended,
):
    low = tile_ref[0] % 2
    attended[low] = got_a[...]
    attended[1 - low] = got_b[...]
    ch = mid.shape[-1]
    above, below = edge_rows(tile_ref, pair_a, mid_a, pair_b, mid_b)
    wide = []
    for f in range(2):
        rows = [above[f].astype(bf16), mid[f, :cols, :], mid[f, cols:, :], below[f].astype(bf16)]
        wide += [jnp.concatenate(rows[r : r + 3], axis=1) for r in range(2)]
    here = dot32(jnp.concatenate(wide, axis=0), w[2])
    flag = usable_flag(clips, span_ref[0] * 2 + 1, 1).astype(f32)
    back = dot32(weigh(flag, jnp.concatenate(wide[:2], axis=0)), w[1])
    for r in range(2):
        part = slice(r * cols, (r + 1) * cols)
        out[0, part, :] = shift_add(here[part], cols, ch)
        after = here[(2 + r) * cols : (3 + r) * cols]
        out[1, part, :] = shift_add(after + back[part], cols, ch)


def finish_kernel(span_ref, own, link_got, core_got, out):
    span = span_ref[0]

    @pl.when(span == 0)
    def _():
        out[...] = own[...].astype(bf16)

    @pl.when(span % 2 == 1)
    def _():
        out[...] = (own[...] + core_got[...].astype(f32)).astype(bf16)

    @pl.when(jnp.logical_and(span % 2 == 0, span > 0))
    def _():
        out[...] = (own[...] + link_got[...].astype(f32)).astype(bf16)


def on_device(features, clip_lengths, norm_gain, w_qkv, w_out, conv_gain, w_conv):
    frames, row_count, cols, ch = features.shape
    tiles, spans = lax.axis_size("tile"), lax.axis_size("span")
    if tiles != 4 or spans % 2 or frames != 2 or row_count != 2:
        return general(features, clip_lengths, norm_gain, w_qkv, w_out, conv_gain, w_conv)
    cells = row_count * cols
    both = ("tile", "span")
    tile = lax.axis_index("tile").astype(jnp.int32).reshape(1)
    span = lax.axis_index("span").astype(jnp.int32).reshape(1)
    other_core = [(i, i ^ 1) for i in range(spans)]
    route_a, route_b = frame_route(spans, 0), frame_route(spans, 1)
    x = features.reshape(frames, cells, ch)
    send_a, send_b = call(
        pick_kernel,
        "pick",
        (pltpu.VMEM((cells, ch), bf16), pltpu.VMEM((cells, ch), bf16)),
        [SMEM, ANY],
        [pltpu.SemaphoreType.DMA((2,))],
        62,
    )(tile, x)
    own_a = lax.ppermute(send_a, both, route_a)
    own_b = lax.ppermute(send_b, both, route_b)
    w_qkv, w_out, norm_gain = call(
        load_small_kernel,
        "load_small",
        (pltpu.VMEM(w_qkv.shape, bf16), pltpu.VMEM(w_out.shape, bf16), pltpu.VMEM((ch,), f32)),
        [ANY, ANY, VMEM],
        [pltpu.SemaphoreType.DMA((2,))],
        60,
    )(w_qkv, w_out, norm_gain)
    own_a, w_qkv = lax.optimization_barrier((own_a, w_qkv))
    other_a = lax.ppermute(own_a, "span", other_core)
    other_b = lax.ppermute(own_b, "span", other_core)
    kv_flops = 2 * 2 * cells * ch * 2 * ch
    row_flops = 2 * cells * ch * (2 * ch + 8 * cells)
    kv_a, queries = call(
        keys_kernel,
        "keys",
        (struct((3 * cells, 2 * ch)), struct((2, cells, ch))),
        [VMEM] * 5,
        flops=kv_flops,
    )(own_a, other_a, own_b, norm_gain, w_qkv)
    kv_b, att_a = call(
        attend_kernel,
        "attend",
        (struct((cells, 2 * ch)), struct((cells, ch))),
        [VMEM] * 7,
        flops=kv_flops + row_flops,
    )(other_b, own_a, queries, kv_a, norm_gain, w_qkv, w_out)
    got_a = lax.ppermute(att_a, both, route_a)
    att_b = call(
        attend_rest_kernel, "attend_rest", struct((cells, ch)), [VMEM] * 5, flops=3 * row_flops
    )(own_b, queries, kv_a, kv_b, w_out)
    got_b = lax.ppermute(att_b, both, route_b)
    pairs, middle = [(0, 1), (1, 0), (2, 3), (3, 2)], [(1, 2), (2, 1)]
    one, edge = struct((cells, ch)), struct((cols, ch))
    sums = struct((frames, cells, ch), f32)
    unit = 2 * cells * 9 * ch * ch
    where = (tile, span, clip_lengths)
    w_packed = call(
        load_kernel,
        "load_conv",
        struct((3, 3 * ch, 3 * ch)),
        [ANY, ANY],
        [pltpu.SemaphoreType.DMA((27,))],
        42,
        size=1 << 12,
    )(att_b, w_conv)
    act_a, pair_edge, mid_edge = call(
        functools.partial(activate_a_kernel, cols), "activate_a", (one, edge, edge), [SMEM, VMEM, VMEM, ANY]
    )(tile, got_a, conv_gain, w_packed)
    pair_a = lax.ppermute(pair_edge, "tile", pairs)
    mid_a = lax.ppermute(mid_edge, "tile", middle)
    active, pair_edge, mid_edge = call(
        functools.partial(activate_b_kernel, cols),
        "activate_b",
        (struct((frames, cells, ch)), edge, edge),
        [SMEM] + [VMEM] * 3 + [ANY],
    )(tile, got_b, act_a, conv_gain, w_packed)
    pair_b = lax.ppermute(pair_edge, "tile", pairs)
    mid_b = lax.ppermute(mid_edge, "tile", middle)
    edges = (pair_a, mid_a, pair_b, mid_b)
    started = call(
        functools.partial(next_own_kernel, cols),
        "next_own",
        sums,
        [SMEM] * 2 + [VMEM] * 2,
        flops=2 * unit,
    )(span, clip_lengths, active, w_packed)
    for_next = call(
        functools.partial(next_edge_kernel, cols),
        "next_edge",
        struct((frames, cells, ch)),
        [SMEM] * 3 + [VMEM] * 6,
        flops=unit,
    )(*where, *edges, w_packed, started)
    link = [(s + d, s + 1 - d) for s in range(1, spans - 1, 2) for d in range(2)]
    link_got = lax.ppermute(for_next, "span", link)
    core_got = lax.ppermute(for_next, "span", other_core)
    own, attended = call(
        functools.partial(own_kernel, cols),
        "own",
        (sums, struct((frames, cells, ch))),
        [SMEM] * 3 + [VMEM] * 8,
        flops=3 * unit,
    )(*where, active, *edges, w_packed, got_a, got_b)
    hidden = call(
        finish_kernel, "finish", struct((frames, cells, ch)), [SMEM] + [VMEM] * 3
    )(span, own, link_got, core_got)
    shape = (frames, row_count, cols, ch)
    return attended.reshape(shape), hidden.reshape(shape)


def extended(x, sides, width):
    for axis, dim in sides:
        size, length = (lax.axis_size(axis), x.shape[dim])
        up = [(i, (i + 1) % size) for i in range(size - 1)]
        down = [(j, i) for i, j in up]
        last = lax.slice_in_dim(x, length - width, length, axis=dim)
        first = lax.slice_in_dim(x, 0, width, axis=dim)
        before = lax.ppermute(last, axis, up)
        after = lax.ppermute(first, axis, down)
        x = jnp.concatenate([before, x, after], axis=dim)
    return x


def general(features, clip_lengths, norm_gain, w_qkv, w_out, conv_gain, w_conv):
    frames, row_count, col_count, channels = features.shape
    cell_count = row_count * col_count
    normed_grid = rms_scale(features, norm_gain).astype(jnp.bfloat16)
    view_frames = normed_grid.shape[0]
    view_cells = normed_grid.shape[1] * normed_grid.shape[2]
    normed = normed_grid.reshape(view_frames, view_cells, channels)
    queries = jnp.dot(
        normed.reshape(-1, channels), w_qkv[:, :channels], preferred_element_type=jnp.float32
    )
    queries = queries.astype(jnp.bfloat16).reshape(view_frames, view_cells, channels)
    kv_weight = w_qkv[:, channels:]
    score_scale = channels ** (-0.5)
    outgoing = jnp.dot(normed.reshape(-1, channels), kv_weight, preferred_element_type=jnp.float32)
    outgoing = outgoing.astype(jnp.bfloat16).reshape(view_frames, view_cells, 2 * channels)
    portion = lax.all_gather(outgoing, "tile", axis=1, tiled=True)
    key_part = portion[:, :, :channels]
    value_part = portion[:, :, channels:]
    row_top = jnp.full((view_frames, view_cells, 1), -1e30, jnp.float32)
    scores = (
        jnp.einsum("fqc,fkc->fqk", queries, key_part, preferred_element_type=jnp.float32)
        * score_scale
    )
    new_top = jnp.maximum(row_top, jnp.max(scores, axis=2, keepdims=True))
    raised_f = jnp.exp(scores - new_top)
    row_total = jnp.sum(raised_f, axis=2, keepdims=True)
    weighted = jnp.einsum(
        "fqk,fkc->fqc",
        raised_f.astype(jnp.bfloat16),
        value_part,
        preferred_element_type=jnp.float32,
    )
    mixture_grid = (weighted / row_total).astype(jnp.bfloat16)
    mixture = mixture_grid.reshape(-1, channels)
    projected = jnp.dot(mixture, w_out, preferred_element_type=jnp.float32)
    attended = (features.reshape(-1, channels).astype(jnp.float32) + projected).astype(jnp.bfloat16)
    attended = attended.reshape(frames, row_count, col_count, channels)
    lifted = rms_scale(attended, conv_gain)
    activated = (lifted * jax.nn.sigmoid(lifted)).astype(jnp.bfloat16)
    earlier = from_behind(activated, "span", 1)
    stacked = jnp.concatenate([earlier, activated], axis=0)
    edged = extended(stacked, (("tile", 1),), 1)
    padded = jnp.pad(edged, ((0, 0), (0, 0), (1, 1), (0, 0)))
    clip_ends = jnp.cumsum(clip_lengths)
    position = lax.axis_index("span") * frames + jnp.arange(frames, dtype=jnp.int32)
    clip_start = jnp.sum(
        jnp.where(clip_ends[None, :] <= position[:, None], clip_lengths[None, :], 0), axis=1
    )
    summed = jnp.zeros((frames * cell_count, channels), jnp.float32)
    for t_tap in range(3):
        usable = position - (2 - t_tap) >= clip_start
        for r_tap in range(3):
            for c_tap in range(3):
                shifted = padded[
                    t_tap : t_tap + frames, r_tap : r_tap + row_count, c_tap : c_tap + col_count
                ]
                shifted = jnp.where(
                    usable[:, None, None, None], shifted, jnp.zeros((), shifted.dtype)
                )
                summed = summed + jnp.dot(
                    shifted.reshape(-1, channels),
                    w_conv[t_tap, r_tap, c_tap],
                    preferred_element_type=jnp.float32,
                )
    hidden = summed.astype(jnp.bfloat16).reshape(frames, row_count, col_count, channels)
    return (attended, hidden)


def solution(mesh):
    in_specs = (P(("grp", "span"), "tile", None, None), P("grp"), P(), P(), P(), P(), P())
    out_specs = (P(("grp", "span"), "tile", None, None), P(("grp", "span"), "tile", None, None))
    return jax.shard_map(
        on_device, mesh=mesh, in_specs=in_specs, out_specs=out_specs, check_vma=False
    )
```
